128 devices in a mesh: rows: 8 (over z, x_lo), cols: 16 (over y, x_hi, core).
Axes of the slice: x: 4 (x_hi: 2, x_lo: 2; x = x_hi * 2 + x_lo), y: 4, z: 4, core: 2. Of those that a mesh axis runs over, the one named last changes fastest.
Arguments:
- global_in: bfloat16 [16, 64, 1024], P('rows', None, 'cols'), may hold values from -6 to 6
- global_first: bfloat16 [3, 3, 1024, 1024], P(None, None, None, 'cols'), may hold values from -0.0625 to 0.0625
- global_second: bfloat16 [3, 3, 1024, 1024], P(None, None, None, 'cols'), may hold values from -0.0625 to 0.0625
- project_weight: bfloat16 [1024, 128], replicated, may hold values from -0.1875 to 0.1875
- enhancer_input: bfloat16 [256, 1024, 128], P('rows', 'cols'), may hold values from -6 to 6
- instance_map: int32 [256, 1024], P('rows', 'cols'), may hold values from 0 to 255, as said below
- encoder_features: float32 [16, 256, 1024], P(None, 'rows', 'cols'), may hold values from -5 to 5
- instance_weight: float32 [16, 128], replicated, may hold values from -4 to 4
- enhancer_first: bfloat16 [3, 3, 128, 128], replicated, may hold values from -0.1875 to 0.1875
- enhancer_second: bfloat16 [3, 3, 128, 128], replicated, may hold values from -0.1875 to 0.1875
- output_cotangent: bfloat16 [256, 1024, 128], P('rows', 'cols'), may hold values from -6 to 6
Outputs:
- enhanced: bfloat16 [256, 1024, 128], P('rows', 'cols')
- gradient_first: float32 [3, 3, 128, 128], replicated
- gradient_second: float32 [3, 3, 128, 128], replicated
- global_gradient: float32 [16, 64, 128], P('rows', 'cols')
The draws below stay inside these ranges and needn't reach their ends.
Inputs may be any that keep to these rules, and one draw needn't show every extreme that they name: `instance_map`: constant on each aligned 16 x 16 block of fine pixels.
All inputs are finite; a program needn't handle non-finite values.
Results may differ from the reference program's by a relative error of at most 0.0075.
Values may be sent and summed in bfloat16 or wider, within the bound.
A program may use at most 64 MiB of HBM per device.

```python
import math
import jax
import jax.numpy as jnp
from jax import lax

GLOBAL_WIDTH = 1024
LOCAL_WIDTH = 128
ENCODER_WIDTH = 16
INSTANCES = 256
UPSCALE = 16
MAP_ROWS = 256
MAP_COLS = 1024
COARSE_ROWS = 16
COARSE_COLS = 64


def draw_instance_map(key, part):
    block_rows = MAP_ROWS // UPSCALE
    block_cols = MAP_COLS // UPSCALE
    first_draw = jax.random.randint(jax.random.fold_in(key, 11), (block_rows, block_cols), 0, INSTANCES)
    second_draw = jax.random.randint(jax.random.fold_in(key, 12), (block_rows, block_cols), 0, INSTANCES)
    labels = jnp.minimum(first_draw, second_draw)
    half_rows = block_rows // 2
    copied = jax.random.randint(jax.random.fold_in(key, 13), (half_rows, block_cols), 0, 2)
    upper = labels[:half_rows]
    lower = jnp.where(copied == 1, upper, labels[half_rows:2 * half_rows])
    labels = jnp.concatenate([upper, lower, labels[2 * half_rows:]], axis=0)
    labels = labels.at[0, 0].set(INSTANCES - 1)
    return jnp.repeat(jnp.repeat(labels, UPSCALE, 0), UPSCALE, 1).astype(jnp.int32)


def draw_encoder_features(key, part):
    base_key = jax.random.fold_in(key, 21)
    noise_key = jax.random.fold_in(key, 22)
    base = jnp.clip(jax.random.normal(base_key, (ENCODER_WIDTH, MAP_ROWS // UPSCALE, MAP_COLS // UPSCALE), jnp.float32), -4.0, 4.0)
    noise = jnp.clip(0.3 * jax.random.normal(noise_key, (ENCODER_WIDTH, MAP_ROWS, MAP_COLS), jnp.float32), -1.0, 1.0)
    return (jnp.repeat(jnp.repeat(base, UPSCALE, 1), UPSCALE, 2) + noise).astype(jnp.float32)


def block_scale(stream_key, dims, cuts, least, top_value):
    def one(position, shards_of):
        steps = jax.random.uniform(jax.random.fold_in(jax.random.fold_in(stream_key, 6), position), (shards_of,), jnp.float32, least / len(cuts), top_value / len(cuts))
        return jnp.repeat(jnp.exp(steps), dims[position] // shards_of).reshape((-1,) + (1,) * (len(dims) - position - 1))

    loudness = one(*cuts[0])
    for cut in cuts[1:]:
        loudness = loudness * one(*cut)
    return loudness


def normal_values(key, extent, width, reach, cuts=(), kind=jnp.bfloat16):
    values = width * jax.random.normal(key, extent, jnp.float32)
    if cuts:
        values = values * block_scale(key, extent, cuts, -0.22, 0.18)
    return jnp.clip(values, -reach, reach).astype(kind)


def setup_inputs(seed: int = 0) -> dict:
    arg_keys = jax.random.split(jax.random.key(seed), 12)
    global_in = normal_values(arg_keys[0], (COARSE_ROWS, COARSE_COLS, GLOBAL_WIDTH), 1.0, 6.0, ((0, 8), (2, 16)))
    global_first = normal_values(arg_keys[1], (3, 3, GLOBAL_WIDTH, GLOBAL_WIDTH), (9 * GLOBAL_WIDTH) ** -0.5, 0.0625, ((3, 16),))
    global_second = normal_values(arg_keys[2], (3, 3, GLOBAL_WIDTH, GLOBAL_WIDTH), (9 * GLOBAL_WIDTH) ** -0.5, 0.0625, ((3, 16),))
    project_weight = normal_values(arg_keys[3], (GLOBAL_WIDTH, LOCAL_WIDTH), GLOBAL_WIDTH ** -0.5, 0.1875)
    enhancer_input = normal_values(arg_keys[4], (MAP_ROWS, MAP_COLS, LOCAL_WIDTH), 1.0, 6.0, ((0, 8), (1, 16)))
    instance_map = draw_instance_map(jax.random.fold_in(arg_keys[11], 71), 0)
    encoder_features = draw_encoder_features(jax.random.fold_in(arg_keys[11], 71), 0)
    instance_weight = normal_values(arg_keys[7], (ENCODER_WIDTH, LOCAL_WIDTH), 1.0, 4.0, (), jnp.float32)
    enhancer_first = normal_values(arg_keys[8], (3, 3, LOCAL_WIDTH, LOCAL_WIDTH), (9 * LOCAL_WIDTH) ** -0.5, 0.1875)
    enhancer_second = normal_values(arg_keys[9], (3, 3, LOCAL_WIDTH, LOCAL_WIDTH), (9 * LOCAL_WIDTH) ** -0.5, 0.1875)
    output_cotangent = normal_values(arg_keys[10], (MAP_ROWS, MAP_COLS, LOCAL_WIDTH), 1.0, 6.0, ((0, 8), (1, 16)))
    return {"global_in": global_in, "global_first": global_first, "global_second": global_second, "project_weight": project_weight, "enhancer_input": enhancer_input, "instance_map": instance_map, "encoder_features": encoder_features, "instance_weight": instance_weight, "enhancer_first": enhancer_first, "enhancer_second": enhancer_second, "output_cotangent": output_cotangent}


norm_eps = 1e-05

def pad_map(field):
    return jnp.pad(field, ((1, 1), (1, 1), (0, 0)))

def conv_taps(padded, weight, row_count, col_count):
    summed = jnp.zeros((row_count * col_count, weight.shape[3]), jnp.float32)
    for tap_row in range(3):
        for tap_col in range(3):
            window = padded[tap_row:tap_row + row_count, tap_col:tap_col + col_count]
            summed = summed + jnp.dot(window.reshape(row_count * col_count, window.shape[2]), weight[tap_row, tap_col], preferred_element_type=jnp.float32)
    return summed

def back_taps(padded, weight, row_count, col_count):
    summed = jnp.zeros((row_count * col_count, weight.shape[2]), jnp.float32)
    for tap_row in range(3):
        for tap_col in range(3):
            window = padded[2 - tap_row:2 - tap_row + row_count, 2 - tap_col:2 - tap_col + col_count]
            summed = summed + jnp.dot(window.reshape(row_count * col_count, window.shape[2]), weight[tap_row, tap_col].T, preferred_element_type=jnp.float32)
    return summed

def weight_taps(padded, gradient, row_count, col_count):
    flattened = gradient.reshape(row_count * col_count, gradient.shape[2])
    stacked = []
    for tap_row in range(3):
        line = []
        for tap_col in range(3):
            window = padded[tap_row:tap_row + row_count, tap_col:tap_col + col_count]
            line.append(lax.dot_general(window.reshape(row_count * col_count, window.shape[2]), flattened, (((0,), (0,)), ((), ())), preferred_element_type=jnp.float32))
        stacked.append(jnp.stack(line))
    return jnp.stack(stacked)

def reference(global_in, global_first, global_second, project_weight, enhancer_input, instance_map, encoder_features, instance_weight, enhancer_first, enhancer_second, output_cotangent):
    coarse_rows, coarse_cols, global_width = global_in.shape
    map_rows, map_cols, local_width = enhancer_input.shape
    first_raw = conv_taps(pad_map(global_in), global_first, coarse_rows, coarse_cols)
    band_total = coarse_rows * coarse_cols
    band_mean = lax.optimization_barrier(jnp.sum(first_raw, 0)) / band_total
    band_var = lax.optimization_barrier(jnp.sum(first_raw * first_raw, 0)) / band_total - band_mean * band_mean
    normed = (first_raw - band_mean) * lax.rsqrt(band_var + norm_eps)
    hidden = jnp.maximum(normed, 0.0).astype(jnp.bfloat16).reshape(coarse_rows, coarse_cols, global_width)
    second_raw = conv_taps(pad_map(hidden), global_second, coarse_rows, coarse_cols)
    global_out = (global_in.astype(jnp.float32).reshape(-1, global_width) + second_raw).astype(jnp.bfloat16)
    coarse = jnp.dot(global_out, project_weight, preferred_element_type=jnp.float32).astype(jnp.bfloat16)
    coarse = coarse.reshape(coarse_rows, coarse_cols, local_width)
    pixel_labels = instance_map.reshape(-1)
    flat_features = encoder_features.reshape(encoder_features.shape[0], -1).T
    feature_sums = jax.ops.segment_sum(flat_features, pixel_labels, num_segments=INSTANCES)
    member_counts = jax.ops.segment_sum(jnp.ones(pixel_labels.shape, jnp.float32), pixel_labels, num_segments=INSTANCES)
    averages = feature_sums / jnp.maximum(member_counts, 1.0)[:, None]
    lookup = jnp.dot(averages, instance_weight, precision=lax.Precision.HIGHEST)
    pooled = jnp.take(lookup, pixel_labels, axis=0).reshape(map_rows, map_cols, local_width)
    upsampled = jnp.repeat(jnp.repeat(coarse, UPSCALE, 0), UPSCALE, 1)
    mixed = (enhancer_input.astype(jnp.float32) + upsampled.astype(jnp.float32) + pooled).astype(jnp.bfloat16)
    mixed_padded = pad_map(mixed)
    first_act = conv_taps(mixed_padded, enhancer_first, map_rows, map_cols)
    pixel_total = map_rows * map_cols
    act_mean = lax.optimization_barrier(jnp.sum(first_act, 0)) / pixel_total
    act_var = lax.optimization_barrier(jnp.sum(first_act * first_act, 0)) / pixel_total - act_mean * act_mean
    inverse_dev = lax.rsqrt(act_var + norm_eps)
    normed_act = (first_act - act_mean) * inverse_dev
    activated = jax.nn.silu(normed_act).astype(jnp.bfloat16).reshape(map_rows, map_cols, local_width)
    active_padded = pad_map(activated)
    second_act = conv_taps(active_padded, enhancer_second, map_rows, map_cols)
    enhanced = (mixed.astype(jnp.float32).reshape(-1, local_width) + second_act).astype(jnp.bfloat16).reshape(map_rows, map_cols, local_width)
    second_sum = weight_taps(active_padded, output_cotangent, map_rows, map_cols)
    act_grad = back_taps(pad_map(output_cotangent), enhancer_second, map_rows, map_cols)
    gate_value = jax.nn.sigmoid(normed_act)
    normed_grad = act_grad * gate_value * (1.0 + normed_act * (1.0 - gate_value))
    grad_mean = lax.optimization_barrier(jnp.sum(normed_grad, 0)) / pixel_total
    cross_mean = lax.optimization_barrier(jnp.sum(normed_grad * normed_act, 0)) / pixel_total
    first_grad = (inverse_dev * (normed_grad - grad_mean - normed_act * cross_mean)).astype(jnp.bfloat16).reshape(map_rows, map_cols, local_width)
    first_sum = weight_taps(mixed_padded, first_grad, map_rows, map_cols)
    mixed_grad = output_cotangent.astype(jnp.float32).reshape(-1, local_width) + back_taps(pad_map(first_grad), enhancer_first, map_rows, map_cols)
    rescale = 1.0 / math.sqrt(pixel_total)
    global_gradient = mixed_grad.reshape(coarse_rows, UPSCALE, coarse_cols, UPSCALE, local_width).sum(axis=(1, 3)) / UPSCALE
    return (enhanced, first_sum * rescale, second_sum * rescale, global_gradient)
```

```python
import functools
import math

import jax
import jax.numpy as jnp
from jax import lax
from jax.experimental import pallas as pl
from jax.experimental.pallas import tpu as pltpu
from jax.sharding import PartitionSpec as P

MESH = pl.DeviceIdType.MESH
HIGH = lax.Precision.HIGHEST
F32 = jnp.float32
BF16 = jnp.bfloat16
EPS = 1e-05
LABELS = 256
UP = 16
W = 80
DIRS = [(dr, dc) for dr in (-1, 0, 1) for dc in (-1, 0, 1) if (dr, dc) != (0, 0)]


def mm(a, b):
    return jnp.dot(a, b, preferred_element_type=F32)


def mm_t0(a, b, **kw):
    return lax.dot_general(a, b, (((0,), (0,)), ((), ())), preferred_element_type=F32, **kw)


def mm_t1(a, b, **kw):
    return lax.dot_general(a, b, (((1,), (1,)), ((), ())), preferred_element_type=F32, **kw)


def kernel(
    nr,
    nc,
    gin,
    gw1_hbm,
    gw2_hbm,
    pw,
    ein,
    imap,
    feats,
    iw,
    w1,
    w2,
    cot,
    enh_out,
    g1_out,
    g2_out,
    gg_out,
    gw1,
    gw2,
    gbuf,
    hbuf,
    hsend,
    xcat,
    zs,
    psend,
    precv,
    ssend,
    sbuf,
    gop,
    gos,
    gob,
    gobn,
    einp,
    cotp,
    pbuf,
    pall,
    nbp,
    ringp,
    fsend,
    fbuf,
    m3,
    a3,
    c3,
    cott,
    fgt,
    w2t,
    fa,
    ag,
    tsend,
    tcol,
    tsum,
    trow,
    gacc,
    gcol,
    gred,
    grow,
    gfin,
    gall,
    local_sem,
    col_s,
    col_r,
    nb_s,
    nb_r,
    part_s,
    part_r,
    row_s,
    row_r,
    go_s,
    go_r,
):
    r = lax.axis_index("rows")
    c = lax.axis_index("cols")

    def remote(src, dst, ss, rs, dev):
        return pltpu.make_async_remote_copy(
            src_ref=src, dst_ref=dst, send_sem=ss, recv_sem=rs, device_id=dev, device_id_type=MESH
        )

    def to_cols(n, src_of, dst, wait=False):
        def body(k, carry):
            t = lax.rem(c + k, nc)
            slot = t if wait else c
            copy = remote(src_of(t), dst(slot), col_s.at[n, t], col_r.at[n, slot], (r, t))
            copy.wait() if wait else copy.start()
            return carry

        lax.fori_loop(1, nc, body, 0)

    def to_rows(n, src, dst, wait=False):
        def body(k, carry):
            t = lax.rem(r + k, nr)
            slot = t if wait else r
            copy = remote(src, dst(slot), row_s.at[n, t], row_r.at[n, slot], (t, c))
            copy.wait() if wait else copy.start()
            return carry

        lax.fori_loop(1, nr, body, 0)

    def wrap_r(d):
        return lax.rem(r + d + nr, nr)

    def wrap_c(d):
        return lax.rem(c + d + nc, nc)

    own = [
        pltpu.make_async_copy(gw1_hbm, gw1, local_sem.at[0]),
        pltpu.make_async_copy(gw2_hbm, gw2, local_sem.at[1]),
        pltpu.make_async_copy(ein, einp.at[pl.ds(2, 32), pl.ds(8, 64)], local_sem.at[2]),
        pltpu.make_async_copy(cot, cotp.at[pl.ds(2, 32), pl.ds(8, 64)], local_sem.at[3]),
    ]
    for copy in own:
        copy.start()

    barrier = pltpu.get_barrier_semaphore()

    def greet(dr, dc):
        pl.semaphore_signal(barrier, inc=1, device_id=(wrap_r(dr), lax.rem(c + dc, nc)), device_id_type=MESH)

    def greet_cols(k, carry):
        @pl.when(k > 0)
        def _():
            greet(0, k)

        greet(1, k)
        greet(-1, k)
        return carry

    lax.fori_loop(0, nc, greet_cols, 0)
    for k in range(2, nr - 1):
        greet(k, 0)

    lane8 = lax.broadcasted_iota(jnp.int32, (8, 64), 1)
    row8 = lax.broadcasted_iota(jnp.int32, (8, 64), 0)
    packed = jnp.zeros((8, 16), F32)
    label = jnp.zeros((8, 1), F32)
    for br in range(2):
        strip = jnp.sum(feats[:, br * UP : (br + 1) * UP, :], axis=1)
        pick = ((lane8 // UP == row8 % 4) & (row8 // 4 == br)).astype(F32)
        packed = packed + mm_t1(pick, strip, precision=HIGH)
        corner = ((lane8 == UP * (row8 % 4)) & (row8 // 4 == br)).astype(F32)
        line = imap[br * UP : br * UP + 1, :].astype(F32)
        label = label + jnp.sum(corner * line, axis=1, keepdims=True)
    pbuf[...] = jnp.zeros_like(pbuf)
    pbuf[:, 0:16] = packed
    pbuf[:, 16:17] = jnp.full((8, 1), float(UP * UP), F32)
    pbuf[:, 17:18] = label

    pl.semaphore_wait(barrier, 3 * nc - 1 + nr - 3)

    to_cols(0, lambda t: gin, lambda s: gbuf.at[s])
    to_cols(1, lambda t: pbuf, lambda s: pall.at[s])

    def halo(i, d, src, dst):
        dr, dc = d
        rows_from = {-1: (0, 2), 0: (0, 32), 1: (30, 2)}[dr]
        rows_to = {-1: 34, 0: 2, 1: 0}[dr]
        cols_from = {-1: (0, 8), 0: (0, 64), 1: (56, 8)}[dc]
        cols_to = {-1: 72, 0: 8, 1: 0}[dc]
        n = (dr + 1) * 3 + dc + 1
        return remote(
            src.at[pl.ds(*rows_from), pl.ds(*cols_from)],
            dst.at[pl.ds(rows_to, rows_from[1]), pl.ds(cols_to, cols_from[1])],
            nb_s.at[i, n],
            nb_r.at[i, n],
            (wrap_r(dr), wrap_c(dc)),
        )

    def near(d):
        dr, dc = d
        n = (dr + 1) * 3 + dc + 1
        return remote(
            pbuf, nbp.at[1 - dr, 1 - dc], nb_s.at[2, n], nb_r.at[2, n], (wrap_r(dr), wrap_c(dc))
        )

    for d in DIRS:
        near(d).start()
    for d in DIRS:
        halo(1, d, cot, cotp).start()
    for d in DIRS:
        halo(0, d, ein, einp).start()

    gbuf[pl.ds(c, 1)] = gin[...][None]
    pall[pl.ds(c, 1)] = pbuf[...][None]
    nbp[1, 1] = pbuf[...]
    for a in range(3):
        for b in range(3):
            w2t[a, b * 128 : (b + 1) * 128, :] = (
                w2[2 - a, (2 - b) * 128 : (3 - b) * 128, :].astype(F32).T.astype(BF16)
            )

    col80 = lax.broadcasted_iota(jnp.int32, (W, 128), 0)
    colmap = ((col80 >= 8) | (c > 0)) & ((col80 < 72) | (c < nc - 1))
    colown = (col80 >= 8) & (col80 < 72)

    def spread(dst, i, value):
        dst[i, :, 0:128] = pltpu.roll(value, 1, 0).astype(BF16)
        dst[i, :, 128:256] = value.astype(BF16)
        dst[i, :, 256:384] = pltpu.roll(value, W - 1, 0).astype(BF16)

    def in_map(i, first, last):
        return colmap & ((i >= first) | (r > 0)) & ((i <= last) | (r < nr - 1))

    to_cols(1, lambda t: pbuf, lambda s: pall.at[s], wait=True)
    band_p = pall[...].reshape(8 * nc, 128)
    hot = (
        lax.broadcasted_iota(jnp.int32, (8 * nc, LABELS), 1) == band_p[:, 17:18].astype(jnp.int32)
    ).astype(F32)
    fsend[...] = mm_t0(band_p, hot, precision=HIGH)[0:24, :]
    to_rows(0, fsend, lambda s: fbuf.at[s])
    fbuf[pl.ds(r, 1)] = fsend[...][None]

    def band_conv(buf, w, n):
        for k in range(nc):
            xcat[:, k * 64 : (k + 1) * 64] = buf[k]
        x = xcat[...]
        j = lax.broadcasted_iota(jnp.int32, (128, 64), 0) % 64
        out = []
        for a in range(3):
            total = mm(x, w[a, 1])
            zs[8:136, :] = mm(x, w[a, 0])
            total = total + jnp.where(j > 0, zs[7:135, :], 0.0)
            zs[8:136, :] = mm(x, w[a, 2])
            total = total + jnp.where(j < 63, zs[9:137, :], 0.0)
            out.append(total)
        psend[n, 0] = out[2][0:64]
        psend[n, 1] = out[0][64:128]
        up = remote(psend.at[n, 0], precv.at[n, 1], part_s.at[n, 0], part_r.at[n, 1], (wrap_r(-1), c))
        down = remote(psend.at[n, 1], precv.at[n, 0], part_s.at[n, 1], part_r.at[n, 0], (wrap_r(1), c))
        up.start()
        down.start()
        top = out[1][0:64] + out[2][64:128]
        low = out[0][0:64] + out[1][64:128]
        up.wait()
        down.wait()
        top = top + jnp.where(r > 0, precv[n, 0], 0.0)
        low = low + jnp.where(r < nr - 1, precv[n, 1], 0.0)
        return jnp.concatenate([top, low], axis=0)

    zs[...] = jnp.zeros_like(zs)
    to_cols(0, lambda t: gin, lambda s: gbuf.at[s], wait=True)
    own[0].wait()
    first_raw = band_conv(gbuf, gw1, 0)
    ssend[...] = jnp.zeros_like(ssend)
    ssend[0:1, :] = jnp.sum(first_raw, 0, keepdims=True)
    ssend[1:2, :] = jnp.sum(first_raw * first_raw, 0, keepdims=True)
    to_rows(1, ssend, lambda s: sbuf.at[s])
    sbuf[pl.ds(r, 1)] = ssend[...][None]
    to_rows(1, ssend, lambda s: sbuf.at[s], wait=True)
    sums = jnp.sum(sbuf[...], axis=0)
    band_total = float(nr * 128)
    band_mean = sums[0:1, :] / band_total
    band_var = sums[1:2, :] / band_total - band_mean * band_mean
    normed = (first_raw - band_mean) * lax.rsqrt(band_var + EPS)
    hsend[...] = jnp.maximum(normed, 0.0).astype(BF16)
    to_cols(2, lambda t: hsend, lambda s: hbuf.at[s])
    hbuf[pl.ds(c, 1)] = hsend[...][None]

    own[3].wait()
    for d in DIRS:
        halo(1, d, cot, cotp).wait()

    def cot_row(i, carry):
        value = jnp.where(in_map(i, 2, 33), cotp[i].astype(F32), 0.0)
        spread(c3, i, value)
        return carry

    lax.fori_loop(0, 36, cot_row, 0)

    def cot_turn(i, carry):
        value = jnp.where(colown, cotp[i + 2].astype(F32), 0.0)
        cott[i] = value.T.astype(BF16)
        return carry

    lax.fori_loop(0, 32, cot_turn, 0)

    to_rows(0, fsend, lambda s: fbuf.at[s], wait=True)
    for d in DIRS:
        near(d).wait()
    fsum = jnp.sum(fbuf[...], axis=0)
    averages = fsum[0:16, :] / jnp.maximum(fsum[16:17, :], 1.0)
    ringp[...] = jnp.zeros_like(ringp)
    for br in range(4):
        dr, their_br = {0: (0, 1), 1: (1, 0), 2: (1, 1), 3: (2, 0)}[br]
        for q in range(6):
            dc, their_bc = (0, 3) if q == 0 else (2, 0) if q == 5 else (1, q - 1)
            p = their_br * 4 + their_bc
            ringp[br * 8 + q : br * 8 + q + 1, :] = nbp[dr, dc, p : p + 1, :]
    ring_hot = (
        lax.broadcasted_iota(jnp.int32, (32, LABELS), 1) == ringp[:, 17:18].astype(jnp.int32)
    ).astype(F32)
    ring_avg = mm_t1(ring_hot, averages, precision=HIGH)
    pooled = jnp.dot(ring_avg, iw[...], precision=HIGH, preferred_element_type=F32)

    to_cols(2, lambda t: hsend, lambda s: hbuf.at[s], wait=True)
    own[1].wait()
    second_raw = band_conv(hbuf, gw2, 1)
    global_out = (gin[...].astype(F32) + second_raw).astype(BF16).astype(F32)
    gop[...] = jnp.zeros_like(gop)
    gop[0, 8:72, :] = global_out[0:64]
    gop[1, 8:72, :] = global_out[64:128]
    for t in range(nc):
        for row in range(2):
            gos[t, row] = gop[row, 4 * t + 7 : 4 * t + 15, :]

    def go_copies(t, wait):
        slot = t if wait else c
        copies = [
            remote(gos.at[t, 0], gobn.at[1, slot], go_s.at[0, t], go_r.at[0, slot], (wrap_r(-1), t)),
            remote(gos.at[t, 1], gobn.at[0, slot], go_s.at[1, t], go_r.at[1, slot], (wrap_r(1), t)),
        ]
        for copy in copies:
            copy.wait() if wait else copy.start()

    to_cols(3, lambda t: gos.at[t], lambda s: gob.at[s])

    def go_start(k, carry):
        go_copies(lax.rem(c + k, nc), False)
        return carry

    def go_wait(k, carry):
        go_copies(lax.rem(c + k, nc), True)
        return carry

    lax.fori_loop(0, nc, go_start, 0)
    gob[pl.ds(c, 1)] = gos[pl.ds(c, 1)]
    own[2].wait()
    for d in DIRS:
        halo(0, d, ein, einp).wait()
    lax.fori_loop(0, nc, go_wait, 0)
    to_cols(3, lambda t: gos.at[t], lambda s: gob.at[s], wait=True)
    ring = jnp.zeros((32, 128), F32)
    for k in range(nc):
        rows = jnp.concatenate([gobn[0, k], gob[k, 0], gob[k, 1], gobn[1, k]], axis=0)
        ring = ring + mm(rows.astype(BF16), pw[k * 64 : (k + 1) * 64, :])
    terms = ring.astype(BF16).astype(F32) + pooled

    def mix_rows(br, start, stop):
        pieces = []
        for q in range(6):
            line = terms[br * 8 + q : br * 8 + q + 1, :]
            pieces.append(jnp.broadcast_to(line, (8 if q in (0, 5) else UP, 128)))
        add = jnp.concatenate(pieces, axis=0)

        def mix_row(i, carry):
            value = einp[i].astype(F32) + add
            value = jnp.where(in_map(i, 2, 33), value, 0.0).astype(BF16).astype(F32)
            spread(m3, i, value)
            return carry

        lax.fori_loop(start, stop, mix_row, 0)

    mix_rows(0, 0, 2)
    mix_rows(1, 2, 18)
    mix_rows(2, 18, 34)
    mix_rows(3, 34, 36)

    def conv_part(src, w, first, count):
        x = jnp.concatenate(
            [src[first + a : first + a + count].reshape(count * W, 384) for a in range(3)], axis=1
        )
        return mm(x, w[...].reshape(1152, 128)).reshape(count, W, 128)

    for half in range(2):
        fa[17 * half : 17 * half + 17] = conv_part(m3, w1, 17 * half, 17)

    def tile_sums(n, x, y):
        tsend[n] = jnp.zeros((8, 128), F32)
        tsend[n, 0:1, :] = jnp.sum(x, axis=(0, 1))[None]
        tsend[n, 1:2, :] = jnp.sum(y, axis=(0, 1))[None]
        to_cols(4 + n, lambda t: tsend.at[n], lambda s: tcol.at[n, s])
        tcol[n, pl.ds(c, 1)] = tsend[n][None]

    def tile_sums_2(n):
        to_cols(4 + n, lambda t: tsend.at[n], lambda s: tcol.at[n, s], wait=True)
        tsum[n] = jnp.sum(tcol[n], axis=0)
        to_rows(2 + n, tsum.at[n], lambda s: trow.at[n, s])
        trow[n, pl.ds(r, 1)] = tsum[n][None]

    def tile_sums_3(n):
        to_rows(2 + n, tsum.at[n], lambda s: trow.at[n, s], wait=True)
        return jnp.sum(trow[n], axis=0)

    act = fa[1:33, 8:72, :]
    tile_sums(0, act, act * act)
    ag[0:17] = conv_part(c3, w2t, 0, 17)
    tile_sums_2(0)
    ag[17:34] = conv_part(c3, w2t, 17, 17)
    sums = tile_sums_3(0)
    pixels = float(nr * nc * 2048)
    act_mean = sums[0:1, :] / pixels
    inverse_dev = lax.rsqrt(sums[1:2, :] / pixels - act_mean * act_mean + EPS)

    def act_row(i, carry):
        na = (fa[i] - act_mean) * inverse_dev
        s = jax.nn.sigmoid(na)
        fa[i] = na
        ng = ag[i] * s * (1.0 + na * (1.0 - s))
        ag[i] = ng
        spread(a3, i, jnp.where(in_map(i, 1, 32), na * s, 0.0).astype(BF16).astype(F32))
        return carry

    lax.fori_loop(0, 34, act_row, 0)
    ng = ag[1:33, 8:72, :]
    tile_sums(1, ng, ng * fa[1:33, 8:72, :])

    def weight_part(n, turned, src, first):
        lhs = jnp.concatenate([turned[i] for i in range(32)], axis=1)
        for a in range(3):
            got = mm(lhs, src[first + a : first + a + 32].reshape(32 * W, 384))
            for b in range(3):
                gacc[n, a * 384 + b * 128 : a * 384 + (b + 1) * 128, :] = got[:, b * 128 : (b + 1) * 128].T

    chunk = 1152 // nc

    def piece(t):
        return pl.ds(pl.multiple_of(t * chunk, 8), chunk)

    def grad_1(n):
        to_cols(6 + n, lambda t: gacc.at[n, piece(t)], lambda s: gcol.at[n, s])
        gcol[n, pl.ds(c, 1)] = gacc[n, piece(c)][None]

    def grad_2(n):
        to_cols(6 + n, lambda t: gacc.at[n, piece(t)], lambda s: gcol.at[n, s], wait=True)
        gred[n] = jnp.sum(gcol[n], axis=0)
        to_rows(4 + n, gred.at[n], lambda s: grow.at[n, s])
        grow[n, pl.ds(r, 1)] = gred[n][None]

    def grad_3(n):
        to_rows(4 + n, gred.at[n], lambda s: grow.at[n, s], wait=True)
        gfin[n] = jnp.sum(grow[n], axis=0) * (1.0 / math.sqrt(pixels))
        to_cols(8 + n, lambda t: gfin.at[n], lambda s: gall.at[n, piece(s)])
        gall[n, piece(c)] = gfin[n]

    def grad_4(n, out):
        to_cols(8 + n, lambda t: gfin.at[n], lambda s: gall.at[n, piece(s)], wait=True)
        out[...] = gall[n]

    weight_part(1, cott, a3, 0)
    grad_1(1)
    tile_sums_2(1)
    for half in range(2):
        got = conv_part(a3, w2, 16 * half, 16)
        enh_out[16 * half : 16 * half + 16] = (
            m3[2 + 16 * half : 18 + 16 * half, 8:72, 128:256].astype(F32) + got[:, 8:72, :]
        ).astype(BF16)
    sums = tile_sums_3(1)
    grad_mean = sums[0:1, :] / pixels
    cross_mean = sums[1:2, :] / pixels
    grad_2(1)

    def grad_row(i, carry):
        fg = inverse_dev * (ag[i] - grad_mean - fa[i] * cross_mean)
        fg = jnp.where(in_map(i, 1, 32), fg, 0.0).astype(BF16).astype(F32)
        ag[i] = fg

        @pl.when((i > 0) & (i < 33))
        def _():
            fgt[i - 1] = jnp.where(colown, fg, 0.0).T.astype(BF16)

        return carry

    lax.fori_loop(0, 34, grad_row, 0)
    weight_part(0, fgt, m3, 1)
    grad_1(0)
    grad_3(1)

    rows24 = lax.broadcasted_iota(jnp.int32, (24, W), 0)
    cols24 = lax.broadcasted_iota(jnp.int32, (24, W), 1)
    left = UP * (rows24 % 8) + 9 - rows24 // 8
    window = ((cols24 >= left) & (cols24 < left + UP) & (rows24 % 8 < 4)).astype(F32)
    picked = [[], [], []]
    direct = []
    for br in range(2):
        total = jnp.sum(ag[UP * br + 1 : UP * br + 17], axis=0)
        below = total - ag[UP * br + 1] + ag[UP * br + 17]
        above = total - ag[UP * br + 16] + ag[UP * br]
        for a, strip in enumerate((below, total, above)):
            picked[a].append(jnp.dot(window, strip, precision=HIGH, preferred_element_type=F32))
        strip = jnp.sum(c3[UP * br + 2 : UP * br + 18, :, 128:256].astype(F32), axis=0)
        direct.append(jnp.dot(window, strip, precision=HIGH, preferred_element_type=F32)[8:16])
    result = jnp.concatenate(direct, axis=0)
    for a in range(3):
        for b in range(3):
            s_ab = jnp.concatenate([picked[a][br][8 * b : 8 * b + 8] for br in range(2)], axis=0)
            result = result + mm_t1(
                s_ab, w1[a, b * 128 : (b + 1) * 128, :].astype(F32), precision=HIGH
            )
    gg_out[0] = result[0:4] * (1.0 / UP)
    gg_out[1] = result[8:12] * (1.0 / UP)

    grad_2(0)
    grad_4(1, g2_out)
    grad_3(0)
    grad_4(0, g1_out)


def per_device(
    nr,
    nc,
    global_in,
    global_first,
    global_second,
    project_weight,
    enhancer_input,
    instance_map,
    encoder_features,
    instance_weight,
    enhancer_first,
    enhancer_second,
    output_cotangent,
):
    vm = pl.BlockSpec(memory_space=pltpu.VMEM)
    hbm = pl.BlockSpec(memory_space=pl.ANY)
    chunk = 1152 // nc
    dma = pltpu.SemaphoreType.DMA
    scratch = [
        pltpu.VMEM((3, 3, 1024, 64), BF16),
        pltpu.VMEM((3, 3, 1024, 64), BF16),
        pltpu.VMEM((nc, 128, 64), BF16),
        pltpu.VMEM((nc, 128, 64), BF16),
        pltpu.VMEM((128, 64), BF16),
        pltpu.VMEM((128, 1024), BF16),
        pltpu.VMEM((144, 64), F32),
        pltpu.VMEM((2, 2, 64, 64), F32),
        pltpu.VMEM((2, 2, 64, 64), F32),
        pltpu.VMEM((8, 64), F32),
        pltpu.VMEM((nr, 8, 64), F32),
        pltpu.VMEM((2, 80, 64), F32),
        pltpu.VMEM((nc, 2, 8, 64), F32),
        pltpu.VMEM((nc, 2, 8, 64), F32),
        pltpu.VMEM((2, nc, 8, 64), F32),
        pltpu.VMEM((36, W, 128), BF16),
        pltpu.VMEM((36, W, 128), BF16),
        pltpu.VMEM((8, 128), F32),
        pltpu.VMEM((nc, 8, 128), F32),
        pltpu.VMEM((3, 3, 8, 128), F32),
        pltpu.VMEM((32, 128), F32),
        pltpu.VMEM((24, LABELS), F32),
        pltpu.VMEM((nr, 24, LABELS), F32),
        pltpu.VMEM((36, W, 384), BF16),
        pltpu.VMEM((34, W, 384), BF16),
        pltpu.VMEM((36, W, 384), BF16),
        pltpu.VMEM((32, 128, W), BF16),
        pltpu.VMEM((32, 128, W), BF16),
        pltpu.VMEM((3, 384, 128), BF16),
        pltpu.VMEM((34, W, 128), F32),
        pltpu.VMEM((34, W, 128), F32),
        pltpu.VMEM((2, 8, 128), F32),
        pltpu.VMEM((2, nc, 8, 128), F32),
        pltpu.VMEM((2, 8, 128), F32),
        pltpu.VMEM((2, nr, 8, 128), F32),
        pltpu.VMEM((2, 1152, 128), F32),
        pltpu.VMEM((2, nc, chunk, 128), F32),
        pltpu.VMEM((2, chunk, 128), F32),
        pltpu.VMEM((2, nr, chunk, 128), F32),
        pltpu.VMEM((2, chunk, 128), F32),
        pltpu.VMEM((2, 1152, 128), F32),
        dma((4,)),
        dma((10, nc)),
        dma((10, nc)),
        dma((3, 9)),
        dma((3, 9)),
        dma((2, 2)),
        dma((2, 2)),
        dma((6, nr)),
        dma((6, nr)),
        dma((2, nc)),
        dma((2, nc)),
    ]
    enhanced, g1, g2, gg = pl.pallas_call(
        functools.partial(kernel, nr, nc),
        out_shape=(
            jax.ShapeDtypeStruct((32, 64, 128), BF16),
            jax.ShapeDtypeStruct((1152, 128), F32),
            jax.ShapeDtypeStruct((1152, 128), F32),
            jax.ShapeDtypeStruct((2, 4, 128), F32),
        ),
        in_specs=[vm, hbm, hbm, vm, hbm, vm, vm, vm, vm, vm, hbm],
        out_specs=(vm, vm, vm, vm),
        scratch_shapes=scratch,
        compiler_params=pltpu.CompilerParams(
            collective_id=0, has_side_effects=True, vmem_limit_bytes=56 * 1024 * 1024
        ),
    )(
        global_in.reshape(128, 64),
        global_first,
        global_second,
        project_weight,
        enhancer_input,
        instance_map,
        encoder_features,
        instance_weight,
        enhancer_first.reshape(3, 384, 128),
        enhancer_second.reshape(3, 384, 128),
        output_cotangent,
    )
    return (enhanced, g1.reshape(3, 3, 128, 128), g2.reshape(3, 3, 128, 128), gg)


def solution(mesh):
    nr, nc = mesh.shape["rows"], mesh.shape["cols"]
    return jax.shard_map(
        functools.partial(per_device, nr, nc),
        mesh=mesh,
        in_specs=(
            P("rows", None, "cols"),
            P(None, None, None, "cols"),
            P(None, None, None, "cols"),
            P(),
            P("rows", "cols", None),
            P("rows", "cols"),
            P(None, "rows", "cols"),
            P(),
            P(),
            P(),
            P("rows", "cols", None),
        ),
        out_specs=(P("rows", "cols", None), P(), P(), P("rows", "cols", None)),
        check_vma=False,
    )
```

```python
import functools
import math

import jax
import jax.numpy as jnp
from jax import lax
from jax.experimental import pallas as pl
from jax.experimental.pallas import tpu as pltpu
from jax.sharding import PartitionSpec as P

MESH = pl.DeviceIdType.MESH
HIGH = lax.Precision.HIGHEST
F32 = jnp.float32
BF16 = jnp.bfloat16
EPS = 1e-05
LABELS = 256
UP = 16
W = 80


class Flow:
    def __init__(self, start, wait):
        self.start = start
        self.wait = wait


def mm(a, b):
    return jnp.dot(a, b, preferred_element_type=F32)


def mm_t0(a, b, **kw):
    return lax.dot_general(a, b, (((0,), (0,)), ((), ())), preferred_element_type=F32, **kw)


def mm_t1(a, b, **kw):
    return lax.dot_general(a, b, (((1,), (1,)), ((), ())), preferred_element_type=F32, **kw)


def kernel(
    nr,
    nc,
    gin_hbm,
    gw1_hbm,
    gw2_hbm,
    pw_hbm,
    ein,
    imap_hbm,
    feats_hbm,
    iw_hbm,
    w1_hbm,
    w2_hbm,
    cot,
    enh_out,
    g1_out,
    g2_out,
    gg_out,
    gin,
    gw1,
    gw2,
    pw,
    imap,
    feats,
    iw,
    w1,
    w2,
    bd,
    gsend,
    gbuf,
    hbuf,
    hsend,
    xcat,
    zs,
    psend,
    precv,
    ssend,
    sbuf,
    gop,
    gos,
    gob,
    csend,
    crecv,
    einp,
    cotp,
    pbuf,
    pall,
    nsend,
    nbp,
    ringp,
    fsend,
    fbuf,
    m3,
    a3,
    c3,
    cott,
    fgt,
    w2t,
    fa,
    ag,
    tsend,
    tcol,
    tsum,
    trow,
    gacc,
    gpair,
    ghalf,
    gcol,
    gred,
    grow,
    gfin,
    gall,
    local_sem,
    ring_s,
    ring_r,
    fwd_s,
    fwd_r,
    col_s,
    col_r,
    row_s,
    row_r,
    nb_s,
    nb_r,
):
    r = lax.axis_index("rows")
    c = lax.axis_index("cols")
    chips = nc // 2
    chip = c // 2
    core = lax.rem(c, 2)

    def remote(src, dst, ss, rs, dev):
        return pltpu.make_async_remote_copy(
            src_ref=src, dst_ref=dst, send_sem=ss, recv_sem=rs, device_id=dev, device_id_type=MESH
        )

    def one(i, src, dst, dev):
        copy = remote(src, dst, nb_s.at[i], nb_r.at[i], dev)
        return Flow(copy.start, copy.wait)

    def many(count, copy_of, got, ss, rs):
        def start():
            def body(k, carry):
                copy_of(k).start()
                return carry

            lax.fori_loop(1, count, body, 0)

        def wait():
            pltpu.make_async_copy(got, got, ss).wait()
            pltpu.make_async_copy(got, got, rs).wait()

        return Flow(start, wait)

    def to_cols(n, src_of, dst):
        def copy_of(k):
            t = lax.rem(c + k, nc)
            return remote(src_of(t), dst.at[c], col_s.at[n], col_r.at[n], (r, t))

        return many(nc, copy_of, dst.at[pl.ds(0, nc - 1)], col_s.at[n], col_r.at[n])

    def to_rows(n, src, dst):
        def copy_of(k):
            return remote(src, dst.at[r], row_s.at[n], row_r.at[n], (lax.rem(r + k, nr), c))

        return many(nr, copy_of, dst.at[pl.ds(0, nr - 1)], row_s.at[n], row_r.at[n])

    def to_chips(n, src_of, dst, got):
        def copy_of(k):
            t = lax.rem(chip + k, chips)
            return remote(src_of(t), dst, ring_s.at[n], ring_r.at[n], (r, 2 * t + core))

        return many(chips, copy_of, got, ring_s.at[n], ring_r.at[n])

    def to_partner(n, src, dst):
        copy = remote(src, dst, fwd_s.at[n], fwd_r.at[n], (r, 2 * chip + 1 - core))
        return Flow(copy.start, copy.wait)

    def gather(n, src, dst):
        return (
            to_chips(n, lambda t: src, dst.at[core, chip], dst.at[core, pl.ds(0, chips - 1)]),
            to_partner(n, dst.at[core], dst.at[core]),
        )

    def own_block(src, dst):
        dst[pl.ds(core, 1), pl.ds(chip, 1)] = src[...][None, None]

    def wrap_r(d):
        return lax.rem(r + d + nr, nr)

    def wrap_c(d):
        return lax.rem(c + d + nc, nc)

    pairs = {
        "gin": (gin_hbm, gin),
        "feats": (feats_hbm, feats),
        "imap": (imap_hbm, imap),
        "gw1": (gw1_hbm, gw1),
        "w2": (w2_hbm, w2),
        "cot": (cot, cotp.at[pl.ds(2, 32), pl.ds(0, 64)]),
        "iw": (iw_hbm, iw),
        "gw2": (gw2_hbm, gw2),
        "pw": (pw_hbm, pw),
        "ein": (ein, einp.at[pl.ds(2, 32), pl.ds(0, 64)]),
        "w1": (w1_hbm, w1),
    }
    own = {
        name: pltpu.make_async_copy(src, dst, local_sem.at[i])
        for i, (name, (src, dst)) in enumerate(pairs.items())
    }
    for copy in own.values():
        copy.start()

    barrier = pltpu.get_barrier_semaphore()

    def greet(dr, dc):
        pl.semaphore_signal(barrier, inc=1, device_id=(wrap_r(dr), lax.rem(c + dc, nc)), device_id_type=MESH)

    def greet_cols(k, carry):
        greet(0, k)
        return carry

    def greet_rows(k, carry):
        greet(k, 0)
        return carry

    lax.fori_loop(1, nc, greet_cols, 0)
    lax.fori_loop(1, nr, greet_rows, 0)

    own["gin"].wait()
    gsend[:, 0:64] = gin[0:64, :]
    gsend[:, 64:128] = gin[64:128, :]

    own["feats"].wait()
    own["imap"].wait()
    lane8 = lax.broadcasted_iota(jnp.int32, (8, 64), 1)
    row8 = lax.broadcasted_iota(jnp.int32, (8, 64), 0)
    packed = jnp.zeros((8, 16), F32)
    label = jnp.zeros((8, 1), F32)
    for br in range(2):
        strip = jnp.sum(feats[:, br * UP : (br + 1) * UP, :], axis=1)
        pick = ((lane8 // UP == row8 % 4) & (row8 // 4 == br)).astype(F32)
        packed = packed + mm_t1(pick, strip, precision=HIGH)
        corner = ((lane8 == UP * (row8 % 4)) & (row8 // 4 == br)).astype(F32)
        line = imap[br * UP : br * UP + 1, :].astype(F32)
        label = label + jnp.sum(corner * line, axis=1, keepdims=True)
    pbuf[...] = jnp.zeros_like(pbuf)
    pbuf[:, 0:16] = packed
    pbuf[:, 16:17] = jnp.full((8, 1), float(UP * UP), F32)
    pbuf[:, 17:18] = label

    pl.semaphore_wait(barrier, nc - 1 + nr - 1)

    first_in, first_fwd = gather(0, gsend, gbuf)
    first_in.start()
    own_block(gsend, gbuf)
    sums_in, sums_fwd = gather(1, pbuf, pall)
    sums_in.start()
    own_block(pbuf, pall)

    def halo(i, src, dst):
        rows32 = pl.ds(2, 32)
        sides = [
            one(4 * i, src.at[:, pl.ds(0, 8)], dst.at[rows32, pl.ds(64, 8)], (r, wrap_c(-1))),
            one(4 * i + 1, src.at[:, pl.ds(56, 8)], dst.at[rows32, pl.ds(72, 8)], (r, wrap_c(1))),
        ]
        ends = [
            one(4 * i + 2, dst.at[pl.ds(2, 2)], dst.at[pl.ds(34, 2)], (wrap_r(-1), c)),
            one(4 * i + 3, dst.at[pl.ds(32, 2)], dst.at[pl.ds(0, 2)], (wrap_r(1), c)),
        ]
        return sides, ends

    cot_sides, cot_ends = halo(0, cot, cotp)
    ein_sides, ein_ends = halo(1, ein, einp)
    for flow in cot_sides:
        flow.start()

    own["w2"].wait()
    for a in range(3):
        for b in range(3):
            w2t[a, b * 128 : (b + 1) * 128, :] = (
                w2[2 - a, (2 - b) * 128 : (3 - b) * 128, :].astype(F32).T.astype(BF16)
            )
    own["pw"].wait()
    bd[...] = jnp.zeros_like(bd)
    for k in range(nc):
        bd[k, 0:64, 0:128] = pw[k * 64 : (k + 1) * 64, :]
        bd[k, 64:128, 128:256] = pw[k * 64 : (k + 1) * 64, :]

    col80 = lax.broadcasted_iota(jnp.int32, (W, 128), 0)
    colown = col80 < 64
    colmap = colown | ((col80 < 72) & (c < nc - 1)) | ((col80 >= 72) & (c > 0))

    def shifts(value):
        return jnp.concatenate(
            [
                pltpu.roll(value, 1, 0).astype(BF16),
                value.astype(BF16),
                pltpu.roll(value, W - 1, 0).astype(BF16),
            ],
            axis=1,
        )

    def in_map(i, first, last):
        return colmap & ((i >= first) | (r > 0)) & ((i <= last) | (r < nr - 1))

    map_sums = to_rows(0, fsend, fbuf)
    near = [
        one(8, nsend, nbp.at[2], (wrap_r(-1), c)),
        one(9, nsend, nbp.at[0], (wrap_r(1), c)),
    ]

    def window_1():
        sums_fwd.wait()
        band_p = pall[...].reshape(8 * nc, 128)
        hot = (
            lax.broadcasted_iota(jnp.int32, (8 * nc, LABELS), 1)
            == band_p[:, 17:18].astype(jnp.int32)
        ).astype(F32)
        fsend[...] = mm_t0(band_p, hot, precision=HIGH)[0:24, :]
        map_sums.start()
        fbuf[pl.ds(r, 1)] = fsend[...][None]
        nsend[1] = pbuf[...]
        for i, t in ((0, wrap_c(-1)), (2, wrap_c(1))):
            nsend[pl.ds(i, 1)] = pall[pl.ds(lax.rem(t, 2), 1), pl.ds(t // 2, 1)][0]
        nbp[1] = nsend[...]
        for flow in near:
            flow.start()
        own["cot"].wait()
        for flow in cot_sides:
            flow.wait()
        for flow in cot_ends:
            flow.start()

    def band_conv(buf, w, n, window):
        for k in range(nc):
            block = buf[k % 2, k // 2]
            xcat[0:64, k * 64 : (k + 1) * 64] = block[:, 0:64]
            xcat[64:128, k * 64 : (k + 1) * 64] = block[:, 64:128]
        j = lax.broadcasted_iota(jnp.int32, (128, 64), 0) % 64
        z = mm_t1(xcat[...], w[...].reshape(576, 1024))
        zs[8:136, :] = z
        out = []
        for a in range(3):
            t = a * 192
            before = jnp.where(j > 0, zs[7:135, t : t + 64], 0.0)
            after = jnp.where(j < 63, zs[9:137, t + 128 : t + 192], 0.0)
            out.append(before + z[:, t + 64 : t + 128] + after)
        for half in range(2):
            psend[n, 0, :, half * 64 : half * 64 + 64] = out[2][32 * half : 32 * half + 32]
            psend[n, 1, :, half * 64 : half * 64 + 64] = out[0][64 + 32 * half : 96 + 32 * half]
        up = one(10 + 2 * n, psend.at[n, 0], precv.at[n, 1], (wrap_r(-1), c))
        down = one(11 + 2 * n, psend.at[n, 1], precv.at[n, 0], (wrap_r(1), c))
        up.start()
        down.start()
        top = out[1][0:64] + out[2][64:128]
        low = out[0][0:64] + out[1][64:128]
        window()
        up.wait()
        down.wait()
        came = [
            jnp.concatenate([precv[n, i, :, 0:64], precv[n, i, :, 64:128]], axis=0)
            for i in range(2)
        ]
        top = top + jnp.where(r > 0, came[0], 0.0)
        low = low + jnp.where(r < nr - 1, came[1], 0.0)
        return jnp.concatenate([top, low], axis=0)

    zs[...] = jnp.zeros_like(zs)
    first_in.wait()
    first_fwd.start()
    sums_in.wait()
    sums_fwd.start()
    own["gw1"].wait()
    first_fwd.wait()
    first_raw = band_conv(gbuf, gw1, 0, window_1)
    ssend[...] = jnp.zeros_like(ssend)
    ssend[0:1, 0:64] = jnp.sum(first_raw, 0, keepdims=True)
    ssend[1:2, 0:64] = jnp.sum(first_raw * first_raw, 0, keepdims=True)
    band_stats = to_rows(1, ssend, sbuf)
    band_stats.start()
    sbuf[pl.ds(r, 1)] = ssend[...][None]
    for flow in ein_sides:
        flow.start()
    band_stats.wait()
    sums = jnp.sum(sbuf[...], axis=0)[:, 0:64]
    band_total = float(nr * 128)
    band_mean = sums[0:1, :] / band_total
    band_var = sums[1:2, :] / band_total - band_mean * band_mean
    normed = (first_raw - band_mean) * lax.rsqrt(band_var + EPS)
    hidden = jnp.maximum(normed, 0.0).astype(BF16)
    hsend[:, 0:64] = hidden[0:64]
    hsend[:, 64:128] = hidden[64:128]
    hidden_in, hidden_fwd = gather(2, hsend, hbuf)
    hidden_in.start()
    own_block(hsend, hbuf)

    for flow in cot_ends:
        flow.wait()
    own["ein"].wait()
    for flow in ein_sides:
        flow.wait()

    def cot_row(i, carry):
        value = jnp.where(in_map(i, 2, 33), cotp[i].astype(F32), 0.0)
        c3[i] = shifts(value)
        return carry

    lax.fori_loop(0, 36, cot_row, 0)

    def cot_turn(q, carry):
        value = cotp[pl.ds(2 + 8 * q, 8), 0:64, :].astype(F32)
        cott[q] = value.reshape(512, 128).T.astype(BF16)
        return carry

    lax.fori_loop(0, 4, cot_turn, 0)

    hidden_in.wait()
    hidden_fwd.start()
    for flow in ein_ends:
        flow.start()
    map_sums.wait()
    for flow in near:
        flow.wait()
    fsum = jnp.sum(fbuf[...], axis=0)
    averages = fsum[0:16, :] / jnp.maximum(fsum[16:17, :], 1.0)
    ringp[...] = jnp.zeros_like(ringp)
    for br in range(4):
        dr, their_br = {0: (0, 1), 1: (1, 0), 2: (1, 1), 3: (2, 0)}[br]
        for q in range(6):
            dc, their_bc = (0, 3) if q == 0 else (2, 0) if q == 5 else (1, q - 1)
            p = their_br * 4 + their_bc
            ringp[br * 8 + q : br * 8 + q + 1, :] = nbp[dr, dc, p : p + 1, :]
    ring_hot = (
        lax.broadcasted_iota(jnp.int32, (32, LABELS), 1) == ringp[:, 17:18].astype(jnp.int32)
    ).astype(F32)
    own["iw"].wait()
    ring_avg = mm_t1(ring_hot, averages, precision=HIGH)
    pooled = jnp.dot(ring_avg, iw[...], precision=HIGH, preferred_element_type=F32)

    own["gw2"].wait()
    hidden_fwd.wait()
    second_raw = band_conv(hbuf, gw2, 1, lambda: None)
    global_out = (gin[...].astype(F32) + second_raw).astype(BF16).astype(F32)
    gop[...] = jnp.zeros_like(gop)
    gop[8:72, 0:64] = global_out[0:64]
    gop[8:72, 64:128] = global_out[64:128]
    for t in range(nc):
        gos[t] = gop[4 * t + 7 : 4 * t + 15, :]

    spread_out = to_cols(0, lambda t: gos.at[t], gob)
    spread_out.start()
    gob[pl.ds(c, 1)] = gos[pl.ds(c, 1)]
    for flow in ein_ends:
        flow.wait()
    spread_out.wait()
    packets = jnp.concatenate([gob[k].astype(BF16) for k in range(nc)], axis=1)
    both = mm(packets, bd[...].reshape(nc * 128, 256)).astype(BF16).astype(F32)
    csend[0] = both[:, 0:128]
    csend[1] = both[:, 128:256]
    edges = [
        one(14, csend.at[0], crecv.at[1], (wrap_r(-1), c)),
        one(15, csend.at[1], crecv.at[0], (wrap_r(1), c)),
    ]
    for flow in edges:
        flow.start()

    def mix_rows(br, coarse, start, stop):
        terms = coarse + pooled[br * 8 : br * 8 + 8]
        pieces = []
        for q in (1, 2, 3, 4, 5, 0):
            line = terms[q : q + 1, :]
            pieces.append(jnp.broadcast_to(line, (8 if q in (0, 5) else UP, 128)))
        add = jnp.concatenate(pieces, axis=0)

        def mix_row(i, carry):
            value = einp[i].astype(F32) + add
            value = jnp.where(in_map(i, 2, 33), value, 0.0).astype(BF16).astype(F32)
            m3[i] = shifts(value)
            return carry

        lax.fori_loop(start, stop, mix_row, 0)

    mix_rows(1, both[:, 0:128], 2, 18)
    mix_rows(2, both[:, 128:256], 18, 34)
    own["w1"].wait()

    def conv_part(src, w, first, count):
        width = src.shape[1]
        x = jnp.concatenate(
            [src[first + a : first + a + count].reshape(count * width, 384) for a in range(3)],
            axis=1,
        )
        return mm(x, w[...].reshape(1152, 128)).reshape(count, width, 128)

    fa[2:17] = conv_part(m3, w1, 2, 15)
    fa[17:32] = conv_part(m3, w1, 17, 15)
    for flow in edges:
        flow.wait()
    mix_rows(0, crecv[0], 0, 2)
    mix_rows(3, crecv[1], 34, 36)
    fa[0:2] = conv_part(m3, w1, 0, 2)
    fa[32:34] = conv_part(m3, w1, 32, 2)

    tile_cols = [to_cols(1 + n, lambda t, n=n: tsend.at[n], tcol.at[n]) for n in range(2)]
    tile_rows = [to_rows(2 + n, tsum.at[n], trow.at[n]) for n in range(2)]

    def tile_sums(n, x, y):
        tsend[n] = jnp.zeros((8, 128), F32)
        tsend[n, 0:1, :] = jnp.sum(x, axis=(0, 1))[None]
        tsend[n, 1:2, :] = jnp.sum(y, axis=(0, 1))[None]
        tile_cols[n].start()
        tcol[n, pl.ds(c, 1)] = tsend[n][None]

    def tile_sums_2(n):
        tile_cols[n].wait()
        tsum[n] = jnp.sum(tcol[n], axis=0)
        tile_rows[n].start()
        trow[n, pl.ds(r, 1)] = tsum[n][None]

    def tile_sums_3(n):
        tile_rows[n].wait()
        return jnp.sum(trow[n], axis=0)

    act = fa[1:33, 0:64, :]
    tile_sums(0, act, act * act)
    ag[0:17] = conv_part(c3, w2t, 0, 17)
    tile_sums_2(0)
    ag[17:34] = conv_part(c3, w2t, 17, 17)
    sums = tile_sums_3(0)
    pixels = float(nr * nc * 2048)
    act_mean = sums[0:1, :] / pixels
    inverse_dev = lax.rsqrt(sums[1:2, :] / pixels - act_mean * act_mean + EPS)

    def act_row(i, carry):
        na = (fa[i] - act_mean) * inverse_dev
        s = jax.nn.sigmoid(na)
        fa[i] = na
        ng = ag[i] * s * (1.0 + na * (1.0 - s))
        ag[i] = ng
        value = jnp.where(in_map(i, 1, 32), na * s, 0.0).astype(BF16).astype(F32)
        a3[i] = shifts(value)[0:64]
        return carry

    lax.fori_loop(0, 34, act_row, 0)
    ng = ag[1:33, 0:64, :]
    tile_sums(1, ng, ng * fa[1:33, 0:64, :])

    def weight_part(n, turned, src, first):
        for a in range(3):
            got = jnp.zeros((128, 384), F32)
            for q in range(4):
                start = first + a + 8 * q
                rhs = src[start : start + 8, 0:64, :].reshape(512, 384)
                got = got + mm(turned[q], rhs)
            for b in range(3):
                gacc[n, a * 384 + b * 128 : a * 384 + (b + 1) * 128, :] = got[
                    :, b * 128 : (b + 1) * 128
                ].T

    half_rows = 1152 // 2
    chunk = half_rows // chips

    def half_of(h):
        return pl.ds(pl.multiple_of(h * half_rows, 16), half_rows)

    def piece(h, q):
        return pl.ds(pl.multiple_of(h * half_rows + q * chunk, 8), chunk)

    pair_sum = [to_partner(3 + n, gacc.at[n, half_of(1 - core)], gpair.at[n]) for n in range(2)]
    band_sum = [
        to_chips(
            3 + n,
            lambda t, n=n: ghalf.at[n, t],
            gcol.at[n, chip],
            gcol.at[n, pl.ds(0, chips - 1)],
        )
        for n in range(2)
    ]
    map_sum = [to_rows(4 + n, gred.at[n], grow.at[n]) for n in range(2)]
    share = [
        to_chips(
            5 + n,
            lambda t, n=n: gfin.at[n],
            gall.at[n, core, chip],
            gall.at[n, core, pl.ds(0, chips - 1)],
        )
        for n in range(2)
    ]
    share_fwd = [to_partner(5 + n, gall.at[n, core], gall.at[n, core]) for n in range(2)]

    def grad_0(n):
        pair_sum[n].start()

    def grad_1(n):
        pair_sum[n].wait()
        total = gacc[n, half_of(core)] + gpair[n]
        ghalf[n] = total.astype(BF16).reshape(chips, chunk, 128)
        band_sum[n].start()
        gcol[n, pl.ds(chip, 1)] = ghalf[n, pl.ds(chip, 1)]

    def grad_2(n):
        band_sum[n].wait()
        gred[n] = jnp.sum(gcol[n].astype(F32), axis=0)
        map_sum[n].start()
        grow[n, pl.ds(r, 1)] = gred[n][None]

    def grad_3(n):
        map_sum[n].wait()
        total = jnp.sum(grow[n], axis=0)
        gfin[n] = (total * (1.0 / math.sqrt(pixels))).astype(BF16)
        share[n].start()
        gall[n, pl.ds(core, 1), pl.ds(chip, 1)] = gfin[n][None, None]

    def grad_4(n):
        share[n].wait()
        share_fwd[n].start()

    def grad_5(n, out):
        share_fwd[n].wait()
        out[...] = gall[n].reshape(1152, 128).astype(F32)

    weight_part(1, cott, a3, 0)
    grad_0(1)
    tile_sums_2(1)
    for half in range(2):
        got = conv_part(a3, w2, 16 * half, 16)
        enh_out[16 * half : 16 * half + 16] = (
            m3[2 + 16 * half : 18 + 16 * half, 0:64, 128:256].astype(F32) + got
        ).astype(BF16)
        if half == 0:
            grad_1(1)
    sums = tile_sums_3(1)
    grad_mean = sums[0:1, :] / pixels
    cross_mean = sums[1:2, :] / pixels
    grad_2(1)

    def grad_row(i, carry):
        fg = inverse_dev * (ag[i] - grad_mean - fa[i] * cross_mean)
        fg = jnp.where(in_map(i, 1, 32), fg, 0.0).astype(BF16).astype(F32)
        ag[i] = fg

        return carry

    lax.fori_loop(0, 34, grad_row, 0)

    def grad_turn(q, carry):
        value = ag[pl.ds(1 + 8 * q, 8), 0:64, :]
        fgt[q] = value.reshape(512, 128).T.astype(BF16)
        return carry

    lax.fori_loop(0, 4, grad_turn, 0)
    weight_part(0, fgt, m3, 1)
    grad_0(0)
    grad_3(1)
    grad_1(0)

    rows24 = lax.broadcasted_iota(jnp.int32, (24, W), 0)
    cols24 = lax.broadcasted_iota(jnp.int32, (24, W), 1)
    left = UP * (rows24 % 8) + 1 - rows24 // 8
    inside = (cols24 >= left) & (cols24 < left + UP)
    window = ((inside | ((left < 0) & (cols24 == W - 1))) & (rows24 % 8 < 4)).astype(F32)
    picked = [[], [], []]
    direct = []
    for br in range(2):
        total = jnp.sum(ag[UP * br + 1 : UP * br + 17], axis=0)
        below = total - ag[UP * br + 1] + ag[UP * br + 17]
        above = total - ag[UP * br + 16] + ag[UP * br]
        for a, strip in enumerate((below, total, above)):
            picked[a].append(jnp.dot(window, strip, precision=HIGH, preferred_element_type=F32))
        strip = jnp.sum(c3[UP * br + 2 : UP * br + 18, :, 128:256].astype(F32), axis=0)
        direct.append(jnp.dot(window, strip, precision=HIGH, preferred_element_type=F32)[8:16])
    result = jnp.concatenate(direct, axis=0)
    for a in range(3):
        for b in range(3):
            s_ab = jnp.concatenate([picked[a][br][8 * b : 8 * b + 8] for br in range(2)], axis=0)
            result = result + mm_t1(
                s_ab, w1[a, b * 128 : (b + 1) * 128, :].astype(F32), precision=HIGH
            )
    gg_out[0] = result[0:4] * (1.0 / UP)
    gg_out[1] = result[8:12] * (1.0 / UP)

    grad_4(1)
    grad_2(0)
    grad_5(1, g2_out)
    grad_3(0)
    grad_4(0)
    grad_5(0, g1_out)


def hand_over(*refs):
    half = len(refs) // 2
    for source, target in zip(refs[:half], refs[half:]):
        target[...] = source[...]


def per_device(
    nr,
    nc,
    global_in,
    global_first,
    global_second,
    project_weight,
    enhancer_input,
    instance_map,
    encoder_features,
    instance_weight,
    enhancer_first,
    enhancer_second,
    output_cotangent,
):
    vm = pl.BlockSpec(memory_space=pltpu.VMEM)
    hbm = pl.BlockSpec(memory_space=pltpu.HBM)
    chunk = 1152 // nc
    dma = pltpu.SemaphoreType.DMA
    scratch = [
        pltpu.VMEM((128, 64), BF16),
        pltpu.VMEM((9, 64, 1024), BF16),
        pltpu.VMEM((9, 64, 1024), BF16),
        pltpu.VMEM((1024, 128), BF16),
        pltpu.VMEM((32, 64), jnp.int32),
        pltpu.VMEM((16, 32, 64), F32),
        pltpu.VMEM((16, 128), F32),
        pltpu.VMEM((3, 384, 128), BF16),
        pltpu.VMEM((3, 384, 128), BF16),
        pltpu.VMEM((nc, 128, 256), BF16),
        pltpu.VMEM((64, 128), BF16),
        pltpu.VMEM((2, nc // 2, 64, 128), BF16),
        pltpu.VMEM((2, nc // 2, 64, 128), BF16),
        pltpu.VMEM((64, 128), BF16),
        pltpu.VMEM((128, 1024), BF16),
        pltpu.VMEM((144, 576), F32),
        pltpu.VMEM((2, 2, 32, 128), F32),
        pltpu.VMEM((2, 2, 32, 128), F32),
        pltpu.VMEM((8, 128), F32),
        pltpu.VMEM((nr, 8, 128), F32),
        pltpu.VMEM((80, 128), F32),
        pltpu.VMEM((nc, 8, 128), F32),
        pltpu.VMEM((nc, 8, 128), F32),
        pltpu.VMEM((2, 8, 128), F32),
        pltpu.VMEM((2, 8, 128), F32),
        pltpu.VMEM((36, W, 128), BF16),
        pltpu.VMEM((36, W, 128), BF16),
        pltpu.VMEM((8, 128), F32),
        pltpu.VMEM((2, nc // 2, 8, 128), F32),
        pltpu.VMEM((3, 8, 128), F32),
        pltpu.VMEM((3, 3, 8, 128), F32),
        pltpu.VMEM((32, 128), F32),
        pltpu.VMEM((24, LABELS), F32),
        pltpu.VMEM((nr, 24, LABELS), F32),
        pltpu.VMEM((36, W, 384), BF16),
        pltpu.VMEM((34, 64, 384), BF16),
        pltpu.VMEM((36, W, 384), BF16),
        pltpu.VMEM((4, 128, 512), BF16),
        pltpu.VMEM((4, 128, 512), BF16),
        pltpu.VMEM((3, 384, 128), BF16),
        pltpu.VMEM((34, W, 128), F32),
        pltpu.VMEM((34, W, 128), F32),
        pltpu.VMEM((2, 8, 128), F32),
        pltpu.VMEM((2, nc, 8, 128), F32),
        pltpu.VMEM((2, 8, 128), F32),
        pltpu.VMEM((2, nr, 8, 128), F32),
        pltpu.VMEM((2, 1152, 128), F32),
        pltpu.VMEM((2, 576, 128), F32),
        pltpu.VMEM((2, nc // 2, chunk, 128), BF16),
        pltpu.VMEM((2, nc // 2, chunk, 128), BF16),
        pltpu.VMEM((2, chunk, 128), F32),
        pltpu.VMEM((2, nr, chunk, 128), F32),
        pltpu.VMEM((2, chunk, 128), BF16),
        pltpu.VMEM((2, 2, nc // 2, chunk, 128), BF16),
        dma((11,)),
        dma((7,)),
        dma((7,)),
        dma((7,)),
        dma((7,)),
        dma((3,)),
        dma((3,)),
        dma((6,)),
        dma((6,)),
        dma((16,)),
        dma((16,)),
    ]
    enhanced, g1, g2, gg = pl.pallas_call(
        functools.partial(kernel, nr, nc),
        out_shape=(
            jax.ShapeDtypeStruct((32, 64, 128), BF16),
            jax.ShapeDtypeStruct((1152, 128), F32),
            jax.ShapeDtypeStruct((1152, 128), F32),
            jax.ShapeDtypeStruct((2, 4, 128), F32),
        ),
        in_specs=[hbm] * 11,
        out_specs=(vm, vm, vm, vm),
        scratch_shapes=scratch,
        compiler_params=pltpu.CompilerParams(
            collective_id=0, has_side_effects=True, vmem_limit_bytes=44 * 1024 * 1024
        ),
    )(
        *(
            pltpu.with_memory_space_constraint(x, pltpu.HBM)
            for x in (
                global_in.reshape(128, 64),
                jnp.swapaxes(global_first, 2, 3).reshape(9, 64, 1024),
                jnp.swapaxes(global_second, 2, 3).reshape(9, 64, 1024),
                project_weight,
                enhancer_input,
                instance_map,
                encoder_features,
                instance_weight,
                enhancer_first.reshape(3, 384, 128),
                enhancer_second.reshape(3, 384, 128),
                output_cotangent,
            )
        )
    )
    vms = [vm] * 4
    enhanced, g1, g2, gg = pl.pallas_call(
        hand_over,
        out_shape=tuple(jax.ShapeDtypeStruct(x.shape, x.dtype) for x in (enhanced, g1, g2, gg)),
        in_specs=vms,
        out_specs=tuple(vms),
        compiler_params=pltpu.CompilerParams(vmem_limit_bytes=16 * 1024 * 1024),
    )(enhanced, g1, g2, gg)
    return (enhanced, g1.reshape(3, 3, 128, 128), g2.reshape(3, 3, 128, 128), gg)


def solution(mesh):
    nr, nc = mesh.shape["rows"], mesh.shape["cols"]
    return jax.shard_map(
        functools.partial(per_device, nr, nc),
        mesh=mesh,
        in_specs=(
            P("rows", None, "cols"),
            P(None, None, None, "cols"),
            P(None, None, None, "cols"),
            P(),
            P("rows", "cols", None),
            P("rows", "cols"),
            P(None, "rows", "cols"),
            P(),
            P(),
            P(),
            P("rows", "cols", None),
        ),
        out_specs=(P("rows", "cols", None), P(), P(), P("rows", "cols", None)),
        check_vma=False,
    )
```

```python
import functools
import math

import jax
import jax.numpy as jnp
from jax import lax
from jax.experimental import pallas as pl
from jax.experimental.pallas import tpu as pltpu
from jax.sharding import PartitionSpec as P

MESH = pl.DeviceIdType.MESH
HIGH = lax.Precision.HIGHEST
F32 = jnp.float32
BF16 = jnp.bfloat16
EPS = 1e-05
LABELS = 256
UP = 16
W = 80


class Flow:
    def __init__(self, start, wait):
        self.start = start
        self.wait = wait


def mm(a, b):
    return jnp.dot(a, b, preferred_element_type=F32)


def mm_t0(a, b, **kw):
    return lax.dot_general(a, b, (((0,), (0,)), ((), ())), preferred_element_type=F32, **kw)


def mm_t1(a, b, **kw):
    return lax.dot_general(a, b, (((1,), (1,)), ((), ())), preferred_element_type=F32, **kw)


def kernel(
    nr,
    nc,
    gin_hbm,
    gw1_hbm,
    gw2_hbm,
    pw_hbm,
    ein,
    imap_hbm,
    feats_hbm,
    iw_hbm,
    w1_hbm,
    w2_hbm,
    cot,
    enh_out,
    g1_out,
    g2_out,
    gg_out,
    gin,
    gw1,
    gw2,
    pw,
    imap,
    feats,
    iw,
    w1,
    w2,
    bd,
    gsend,
    gbuf,
    hbuf,
    hsend,
    xcat,
    zs,
    psend,
    precv,
    ssend,
    sbuf,
    gop,
    gos,
    gob,
    csend,
    crecv,
    einp,
    cotp,
    pbuf,
    pall,
    nsend,
    nbp,
    ringp,
    fsend,
    fbuf,
    m3,
    a3,
    c3,
    cott,
    fgt,
    w2t,
    fa,
    ag,
    tsend,
    tcol,
    tsum,
    trow,
    gacc,
    gpair,
    ghalf,
    gcol,
    gred,
    grow,
    gfin,
    gall,
    local_sem,
    ring_s,
    ring_r,
    fwd_s,
    fwd_r,
    col_s,
    col_r,
    row_s,
    row_r,
    nb_s,
    nb_r,
):
    r = lax.axis_index("rows")
    c = lax.axis_index("cols")
    chips = nc // 2
    chip = c // 2
    core = lax.rem(c, 2)

    def remote(src, dst, ss, rs, dev):
        return pltpu.make_async_remote_copy(
            src_ref=src, dst_ref=dst, send_sem=ss, recv_sem=rs, device_id=dev, device_id_type=MESH
        )

    def one(i, src, dst, dev):
        copy = remote(src, dst, nb_s.at[i], nb_r.at[i], dev)
        return Flow(copy.start, copy.wait)

    def many(count, copy_of, got, ss, rs):
        def start():
            def body(k, carry):
                copy_of(k).start()
                return carry

            lax.fori_loop(1, count, body, 0)

        def wait():
            pltpu.make_async_copy(got, got, ss).wait()
            pltpu.make_async_copy(got, got, rs).wait()

        return Flow(start, wait)

    def to_cols(n, src_of, dst):
        def copy_of(k):
            t = lax.rem(c + k, nc)
            return remote(src_of(t), dst.at[c], col_s.at[n], col_r.at[n], (r, t))

        return many(nc, copy_of, dst.at[pl.ds(0, nc - 1)], col_s.at[n], col_r.at[n])

    def to_rows(n, src, dst):
        def copy_of(k):
            return remote(src, dst.at[r], row_s.at[n], row_r.at[n], (lax.rem(r + k, nr), c))

        return many(nr, copy_of, dst.at[pl.ds(0, nr - 1)], row_s.at[n], row_r.at[n])

    def to_chips(n, src_of, dst, got):
        def copy_of(k):
            t = lax.rem(chip + k, chips)
            return remote(src_of(t), dst, ring_s.at[n], ring_r.at[n], (r, 2 * t + core))

        return many(chips, copy_of, got, ring_s.at[n], ring_r.at[n])

    def to_partner(n, src, dst):
        copy = remote(src, dst, fwd_s.at[n], fwd_r.at[n], (r, 2 * chip + 1 - core))
        return Flow(copy.start, copy.wait)

    def gather(n, src, dst):
        return (
            to_chips(n, lambda t: src, dst.at[core, chip], dst.at[core, pl.ds(0, chips - 1)]),
            to_partner(n, dst.at[core], dst.at[core]),
        )

    def own_block(src, dst):
        dst[pl.ds(core, 1), pl.ds(chip, 1)] = src[...][None, None]

    def wrap_r(d):
        return lax.rem(r + d + nr, nr)

    def wrap_c(d):
        return lax.rem(c + d + nc, nc)

    pairs = {
        "gin": (gin_hbm, gin),
        "feats": (feats_hbm, feats),
        "imap": (imap_hbm, imap),
        "gw1": (gw1_hbm, gw1),
        "w2": (w2_hbm, w2),
        "cot": (cot, cotp.at[pl.ds(2, 32), pl.ds(0, 64)]),
        "iw": (iw_hbm, iw),
        "gw2": (gw2_hbm, gw2),
        "pw": (pw_hbm, pw),
        "ein": (ein, einp.at[pl.ds(2, 32), pl.ds(0, 64)]),
        "w1": (w1_hbm, w1),
    }
    own = {
        name: pltpu.make_async_copy(src, dst, local_sem.at[i])
        for i, (name, (src, dst)) in enumerate(pairs.items())
    }
    for copy in own.values():
        copy.start()

    barrier = pltpu.get_barrier_semaphore()

    def greet(dr, dc):
        pl.semaphore_signal(barrier, inc=1, device_id=(wrap_r(dr), lax.rem(c + dc, nc)), device_id_type=MESH)

    def greet_cols(k, carry):
        greet(0, k)
        return carry

    def greet_rows(k, carry):
        greet(k, 0)
        return carry

    lax.fori_loop(1, nc, greet_cols, 0)
    lax.fori_loop(1, nr, greet_rows, 0)

    own["gin"].wait()
    gsend[:, 0:64] = gin[0:64, :]
    gsend[:, 64:128] = gin[64:128, :]

    own["feats"].wait()
    own["imap"].wait()
    lane8 = lax.broadcasted_iota(jnp.int32, (8, 64), 1)
    row8 = lax.broadcasted_iota(jnp.int32, (8, 64), 0)
    packed = jnp.zeros((8, 16), F32)
    label = jnp.zeros((8, 1), F32)
    for br in range(2):
        strip = jnp.sum(feats[:, br * UP : (br + 1) * UP, :], axis=1)
        pick = ((lane8 // UP == row8 % 4) & (row8 // 4 == br)).astype(F32)
        packed = packed + mm_t1(pick, strip, precision=HIGH)
        corner = ((lane8 == UP * (row8 % 4)) & (row8 // 4 == br)).astype(F32)
        line = imap[br * UP : br * UP + 1, :].astype(F32)
        label = label + jnp.sum(corner * line, axis=1, keepdims=True)
    pbuf[...] = jnp.zeros_like(pbuf)
    pbuf[:, 0:16] = packed
    pbuf[:, 16:17] = jnp.full((8, 1), float(UP * UP), F32)
    pbuf[:, 17:18] = label

    pl.semaphore_wait(barrier, nc - 1 + nr - 1)

    first_in, first_fwd = gather(0, gsend, gbuf)
    first_in.start()
    own_block(gsend, gbuf)
    sums_in, sums_fwd = gather(1, pbuf, pall)
    sums_in.start()
    own_block(pbuf, pall)

    def halo(i, src, dst):
        rows32 = pl.ds(2, 32)
        sides = [
            one(4 * i, src.at[:, pl.ds(0, 8)], dst.at[rows32, pl.ds(64, 8)], (r, wrap_c(-1))),
            one(4 * i + 1, src.at[:, pl.ds(56, 8)], dst.at[rows32, pl.ds(72, 8)], (r, wrap_c(1))),
        ]
        ends = [
            one(4 * i + 2, dst.at[pl.ds(2, 2)], dst.at[pl.ds(34, 2)], (wrap_r(-1), c)),
            one(4 * i + 3, dst.at[pl.ds(32, 2)], dst.at[pl.ds(0, 2)], (wrap_r(1), c)),
        ]
        return sides, ends

    cot_sides, cot_ends = halo(0, cot, cotp)
    ein_sides, ein_ends = halo(1, ein, einp)
    for flow in cot_sides:
        flow.start()

    own["w2"].wait()
    for a in range(3):
        for b in range(3):
            w2t[a, b * 128 : (b + 1) * 128, :] = (
                w2[2 - a, (2 - b) * 128 : (3 - b) * 128, :].astype(F32).T.astype(BF16)
            )
    own["pw"].wait()
    bd[...] = jnp.zeros_like(bd)
    for k in range(nc):
        bd[k, 0:64, 0:128] = pw[k * 64 : (k + 1) * 64, :]
        bd[k, 64:128, 128:256] = pw[k * 64 : (k + 1) * 64, :]

    col80 = lax.broadcasted_iota(jnp.int32, (W, 128), 0)
    colown = col80 < 64
    colmap = colown | ((col80 < 72) & (c < nc - 1)) | ((col80 >= 72) & (c > 0))

    def shifts(value):
        return jnp.concatenate(
            [
                pltpu.roll(value, 1, 0).astype(BF16),
                value.astype(BF16),
                pltpu.roll(value, W - 1, 0).astype(BF16),
            ],
            axis=1,
        )

    def in_map(i, first, last):
        return colmap & ((i >= first) | (r > 0)) & ((i <= last) | (r < nr - 1))

    map_sums = to_rows(0, fsend, fbuf)
    near = [
        one(8, nsend, nbp.at[2], (wrap_r(-1), c)),
        one(9, nsend, nbp.at[0], (wrap_r(1), c)),
    ]

    def edge_window():
        own["cot"].wait()
        for flow in cot_sides:
            flow.wait()
        for flow in cot_ends:
            flow.start()

    def stats_window():
        sums_fwd.wait()
        band_p = pall[...].reshape(8 * nc, 128)
        hot = (
            lax.broadcasted_iota(jnp.int32, (8 * nc, LABELS), 1)
            == band_p[:, 17:18].astype(jnp.int32)
        ).astype(F32)
        fsend[...] = mm_t0(band_p, hot, precision=HIGH)[0:24, :]
        map_sums.start()
        fbuf[pl.ds(r, 1)] = fsend[...][None]
        nsend[1] = pbuf[...]
        for i, t in ((0, wrap_c(-1)), (2, wrap_c(1))):
            nsend[pl.ds(i, 1)] = pall[pl.ds(lax.rem(t, 2), 1), pl.ds(t // 2, 1)][0]
        nbp[1] = nsend[...]
        for flow in near:
            flow.start()

    def band_conv(buf, w, n, window):
        for k in range(nc):
            block = buf[k % 2, k // 2]
            xcat[0:64, k * 64 : (k + 1) * 64] = block[:, 0:64]
            xcat[64:128, k * 64 : (k + 1) * 64] = block[:, 64:128]
        j = lax.broadcasted_iota(jnp.int32, (128, 64), 0) % 64
        z = mm_t1(xcat[...], w[...].reshape(576, 1024))
        zs[8:136, :] = z
        out = []
        for a in range(3):
            t = a * 192
            before = jnp.where(j > 0, zs[7:135, t : t + 64], 0.0)
            after = jnp.where(j < 63, zs[9:137, t + 128 : t + 192], 0.0)
            out.append(before + z[:, t + 64 : t + 128] + after)
        for half in range(2):
            psend[n, 0, :, half * 64 : half * 64 + 64] = out[2][32 * half : 32 * half + 32]
            psend[n, 1, :, half * 64 : half * 64 + 64] = out[0][64 + 32 * half : 96 + 32 * half]
        up = one(10 + 2 * n, psend.at[n, 0], precv.at[n, 1], (wrap_r(-1), c))
        down = one(11 + 2 * n, psend.at[n, 1], precv.at[n, 0], (wrap_r(1), c))
        up.start()
        down.start()
        top = out[1][0:64] + out[2][64:128]
        low = out[0][0:64] + out[1][64:128]
        window()
        up.wait()
        down.wait()
        came = [
            jnp.concatenate([precv[n, i, :, 0:64], precv[n, i, :, 64:128]], axis=0)
            for i in range(2)
        ]
        top = top + jnp.where(r > 0, came[0], 0.0)
        low = low + jnp.where(r < nr - 1, came[1], 0.0)
        return jnp.concatenate([top, low], axis=0)

    zs[...] = jnp.zeros_like(zs)
    first_in.wait()
    first_fwd.start()
    sums_in.wait()
    sums_fwd.start()
    own["gw1"].wait()
    first_fwd.wait()
    first_raw = band_conv(gbuf, gw1, 0, edge_window)
    ssend[...] = jnp.zeros_like(ssend)
    ssend[0:1, 0:64] = jnp.sum(first_raw, 0, keepdims=True)
    ssend[1:2, 0:64] = jnp.sum(first_raw * first_raw, 0, keepdims=True)
    band_stats = to_rows(1, ssend, sbuf)
    band_stats.start()
    sbuf[pl.ds(r, 1)] = ssend[...][None]
    for flow in ein_sides:
        flow.start()
    stats_window()
    band_stats.wait()
    sums = jnp.sum(sbuf[...], axis=0)[:, 0:64]
    band_total = float(nr * 128)
    band_mean = sums[0:1, :] / band_total
    band_var = sums[1:2, :] / band_total - band_mean * band_mean
    normed = (first_raw - band_mean) * lax.rsqrt(band_var + EPS)
    hidden = jnp.maximum(normed, 0.0).astype(BF16)
    hsend[:, 0:64] = hidden[0:64]
    hsend[:, 64:128] = hidden[64:128]
    hidden_in, hidden_fwd = gather(2, hsend, hbuf)
    hidden_in.start()
    own_block(hsend, hbuf)

    for flow in cot_ends:
        flow.wait()
    own["ein"].wait()
    for flow in ein_sides:
        flow.wait()

    def cot_row(i, carry):
        value = jnp.where(in_map(i, 2, 33), cotp[i].astype(F32), 0.0)
        c3[i] = shifts(value)
        return carry

    lax.fori_loop(0, 36, cot_row, 0)

    def cot_turn(q, carry):
        value = cotp[pl.ds(2 + 8 * q, 8), 0:64, :].astype(F32)
        cott[q] = value.reshape(512, 128).T.astype(BF16)
        return carry

    lax.fori_loop(0, 4, cot_turn, 0)

    hidden_in.wait()
    hidden_fwd.start()
    for flow in ein_ends:
        flow.start()
    own["gw2"].wait()
    hidden_fwd.wait()
    second_raw = band_conv(hbuf, gw2, 1, lambda: None)
    global_out = (gin[...].astype(F32) + second_raw).astype(BF16).astype(F32)
    gop[...] = jnp.zeros_like(gop)
    gop[8:72, 0:64] = global_out[0:64]
    gop[8:72, 64:128] = global_out[64:128]
    for t in range(nc):
        gos[t] = gop[4 * t + 7 : 4 * t + 15, :]

    spread_out = to_cols(0, lambda t: gos.at[t], gob)
    spread_out.start()
    gob[pl.ds(c, 1)] = gos[pl.ds(c, 1)]
    for flow in ein_ends:
        flow.wait()
    map_sums.wait()
    for flow in near:
        flow.wait()
    fsum = jnp.sum(fbuf[...], axis=0)
    averages = fsum[0:16, :] / jnp.maximum(fsum[16:17, :], 1.0)
    ringp[...] = jnp.zeros_like(ringp)
    for br in range(4):
        dr, their_br = {0: (0, 1), 1: (1, 0), 2: (1, 1), 3: (2, 0)}[br]
        for q in range(6):
            dc, their_bc = (0, 3) if q == 0 else (2, 0) if q == 5 else (1, q - 1)
            p = their_br * 4 + their_bc
            ringp[br * 8 + q : br * 8 + q + 1, :] = nbp[dr, dc, p : p + 1, :]
    ring_hot = (
        lax.broadcasted_iota(jnp.int32, (32, LABELS), 1) == ringp[:, 17:18].astype(jnp.int32)
    ).astype(F32)
    own["iw"].wait()
    ring_avg = mm_t1(ring_hot, averages, precision=HIGH)
    pooled = jnp.dot(ring_avg, iw[...], precision=HIGH, preferred_element_type=F32)
    spread_out.wait()
    packets = jnp.concatenate([gob[k].astype(BF16) for k in range(nc)], axis=1)
    both = mm(packets, bd[...].reshape(nc * 128, 256)).astype(BF16).astype(F32)
    csend[0] = both[:, 0:128]
    csend[1] = both[:, 128:256]
    edges = [
        one(14, csend.at[0], crecv.at[1], (wrap_r(-1), c)),
        one(15, csend.at[1], crecv.at[0], (wrap_r(1), c)),
    ]
    for flow in edges:
        flow.start()

    def mix_rows(br, coarse, start, stop):
        terms = coarse + pooled[br * 8 : br * 8 + 8]
        pieces = []
        for q in (1, 2, 3, 4, 5, 0):
            line = terms[q : q + 1, :]
            pieces.append(jnp.broadcast_to(line, (8 if q in (0, 5) else UP, 128)))
        add = jnp.concatenate(pieces, axis=0)

        def mix_row(i, carry):
            value = einp[i].astype(F32) + add
            value = jnp.where(in_map(i, 2, 33), value, 0.0).astype(BF16).astype(F32)
            m3[i] = shifts(value)
            return carry

        lax.fori_loop(start, stop, mix_row, 0)

    mix_rows(1, both[:, 0:128], 2, 18)
    mix_rows(2, both[:, 128:256], 18, 34)
    own["w1"].wait()

    def conv_part(src, w, first, count):
        width = src.shape[1]
        x = jnp.concatenate(
            [src[first + a : first + a + count].reshape(count * width, 384) for a in range(3)],
            axis=1,
        )
        return mm(x, w[...].reshape(1152, 128)).reshape(count, width, 128)

    fa[2:17] = conv_part(m3, w1, 2, 15)
    fa[17:32] = conv_part(m3, w1, 17, 15)
    for flow in edges:
        flow.wait()
    mix_rows(0, crecv[0], 0, 2)
    mix_rows(3, crecv[1], 34, 36)
    fa[0:2] = conv_part(m3, w1, 0, 2)
    fa[32:34] = conv_part(m3, w1, 32, 2)

    tile_cols = [to_cols(1 + n, lambda t, n=n: tsend.at[n], tcol.at[n]) for n in range(2)]
    tile_rows = [to_rows(2 + n, tsum.at[n], trow.at[n]) for n in range(2)]

    def tile_sums(n, x, y):
        tsend[n] = jnp.zeros((8, 128), F32)
        tsend[n, 0:1, :] = jnp.sum(x, axis=(0, 1))[None]
        tsend[n, 1:2, :] = jnp.sum(y, axis=(0, 1))[None]
        tile_cols[n].start()
        tcol[n, pl.ds(c, 1)] = tsend[n][None]

    def tile_sums_2(n):
        tile_cols[n].wait()
        tsum[n] = jnp.sum(tcol[n], axis=0)
        tile_rows[n].start()
        trow[n, pl.ds(r, 1)] = tsum[n][None]

    def tile_sums_3(n):
        tile_rows[n].wait()
        return jnp.sum(trow[n], axis=0)

    act = fa[1:33, 0:64, :]
    tile_sums(0, act, act * act)
    ag[0:17] = conv_part(c3, w2t, 0, 17)
    tile_sums_2(0)
    ag[17:34] = conv_part(c3, w2t, 17, 17)
    sums = tile_sums_3(0)
    pixels = float(nr * nc * 2048)
    act_mean = sums[0:1, :] / pixels
    inverse_dev = lax.rsqrt(sums[1:2, :] / pixels - act_mean * act_mean + EPS)

    def act_row(i, carry):
        na = (fa[i] - act_mean) * inverse_dev
        s = jax.nn.sigmoid(na)
        fa[i] = na
        ng = ag[i] * s * (1.0 + na * (1.0 - s))
        ag[i] = ng
        value = jnp.where(in_map(i, 1, 32), na * s, 0.0).astype(BF16).astype(F32)
        a3[i] = shifts(value)[0:64]
        return carry

    lax.fori_loop(0, 34, act_row, 0)
    ng = ag[1:33, 0:64, :]
    tile_sums(1, ng, ng * fa[1:33, 0:64, :])

    def weight_part(n, turned, src, first):
        for a in range(3):
            got = jnp.zeros((128, 384), F32)
            for q in range(4):
                start = first + a + 8 * q
                rhs = src[start : start + 8, 0:64, :].reshape(512, 384)
                got = got + mm(turned[q], rhs)
            for b in range(3):
                gacc[n, a * 384 + b * 128 : a * 384 + (b + 1) * 128, :] = got[
                    :, b * 128 : (b + 1) * 128
                ].T

    half_rows = 1152 // 2
    chunk = half_rows // chips

    def half_of(h):
        return pl.ds(pl.multiple_of(h * half_rows, 16), half_rows)

    def piece(h, q):
        return pl.ds(pl.multiple_of(h * half_rows + q * chunk, 8), chunk)

    pair_sum = [to_partner(3 + n, gacc.at[n, half_of(1 - core)], gpair.at[n]) for n in range(2)]
    band_sum = [
        to_chips(
            3 + n,
            lambda t, n=n: ghalf.at[n, t],
            gcol.at[n, chip],
            gcol.at[n, pl.ds(0, chips - 1)],
        )
        for n in range(2)
    ]
    map_sum = [to_rows(4 + n, gred.at[n], grow.at[n]) for n in range(2)]
    share = [
        to_chips(
            5 + n,
            lambda t, n=n: gfin.at[n],
            gall.at[n, core, chip],
            gall.at[n, core, pl.ds(0, chips - 1)],
        )
        for n in range(2)
    ]
    share_fwd = [to_partner(5 + n, gall.at[n, core], gall.at[n, core]) for n in range(2)]

    def grad_0(n):
        pair_sum[n].start()

    def grad_1(n):
        pair_sum[n].wait()
        total = gacc[n, half_of(core)] + gpair[n]
        ghalf[n] = total.astype(BF16).reshape(chips, chunk, 128)
        band_sum[n].start()
        gcol[n, pl.ds(chip, 1)] = ghalf[n, pl.ds(chip, 1)]

    def grad_2(n):
        band_sum[n].wait()
        gred[n] = jnp.sum(gcol[n].astype(F32), axis=0)
        map_sum[n].start()
        grow[n, pl.ds(r, 1)] = gred[n][None]

    def grad_3(n):
        map_sum[n].wait()
        total = jnp.sum(grow[n], axis=0)
        gfin[n] = (total * (1.0 / math.sqrt(pixels))).astype(BF16)
        share[n].start()
        gall[n, pl.ds(core, 1), pl.ds(chip, 1)] = gfin[n][None, None]

    def grad_4(n):
        share[n].wait()
        share_fwd[n].start()

    def grad_5(n, out):
        share_fwd[n].wait()
        out[...] = gall[n].reshape(1152, 128).astype(F32)

    weight_part(1, cott, a3, 0)
    grad_0(1)
    tile_sums_2(1)
    for half in range(2):
        got = conv_part(a3, w2, 16 * half, 16)
        enh_out[16 * half : 16 * half + 16] = (
            m3[2 + 16 * half : 18 + 16 * half, 0:64, 128:256].astype(F32) + got
        ).astype(BF16)
    sums = tile_sums_3(1)
    grad_mean = sums[0:1, :] / pixels
    cross_mean = sums[1:2, :] / pixels
    grad_1(1)

    def grad_row(i, carry):
        fg = inverse_dev * (ag[i] - grad_mean - fa[i] * cross_mean)
        fg = jnp.where(in_map(i, 1, 32), fg, 0.0).astype(BF16).astype(F32)
        ag[i] = fg

        return carry

    lax.fori_loop(0, 34, grad_row, 0)

    def grad_turn(q, carry):
        value = ag[pl.ds(1 + 8 * q, 8), 0:64, :]
        fgt[q] = value.reshape(512, 128).T.astype(BF16)
        return carry

    lax.fori_loop(0, 4, grad_turn, 0)
    weight_part(0, fgt, m3, 1)
    grad_0(0)

    grad_1(0)
    grad_2(1)

    rows24 = lax.broadcasted_iota(jnp.int32, (24, W), 0)
    cols24 = lax.broadcasted_iota(jnp.int32, (24, W), 1)
    left = UP * (rows24 % 8) + 1 - rows24 // 8
    inside = (cols24 >= left) & (cols24 < left + UP)
    window = ((inside | ((left < 0) & (cols24 == W - 1))) & (rows24 % 8 < 4)).astype(F32)
    picked = [[], [], []]
    direct = []
    for br in range(2):
        total = jnp.sum(ag[UP * br + 1 : UP * br + 17], axis=0)
        below = total - ag[UP * br + 1] + ag[UP * br + 17]
        above = total - ag[UP * br + 16] + ag[UP * br]
        for a, strip in enumerate((below, total, above)):
            picked[a].append(jnp.dot(window, strip, precision=HIGH, preferred_element_type=F32))
        strip = jnp.sum(c3[UP * br + 2 : UP * br + 18, :, 128:256].astype(F32), axis=0)
        direct.append(jnp.dot(window, strip, precision=HIGH, preferred_element_type=F32)[8:16])
    result = jnp.concatenate(direct, axis=0)
    for a in range(3):
        for b in range(3):
            s_ab = jnp.concatenate([picked[a][br][8 * b : 8 * b + 8] for br in range(2)], axis=0)
            result = result + mm_t1(
                s_ab, w1[a, b * 128 : (b + 1) * 128, :].astype(F32), precision=HIGH
            )
    gg_out[0] = result[0:4] * (1.0 / UP)
    gg_out[1] = result[8:12] * (1.0 / UP)

    grad_2(0)
    grad_3(1)
    grad_3(0)
    grad_4(1)
    grad_4(0)
    grad_5(1, g2_out)
    grad_5(0, g1_out)


def hand_over(*refs):
    half = len(refs) // 2
    for source, target in zip(refs[:half], refs[half:]):
        target[...] = source[...]


def per_device(
    nr,
    nc,
    global_in,
    global_first,
    global_second,
    project_weight,
    enhancer_input,
    instance_map,
    encoder_features,
    instance_weight,
    enhancer_first,
    enhancer_second,
    output_cotangent,
):
    vm = pl.BlockSpec(memory_space=pltpu.VMEM)
    hbm = pl.BlockSpec(memory_space=pltpu.HBM)
    chunk = 1152 // nc
    dma = pltpu.SemaphoreType.DMA
    scratch = [
        pltpu.VMEM((128, 64), BF16),
        pltpu.VMEM((9, 64, 1024), BF16),
        pltpu.VMEM((9, 64, 1024), BF16),
        pltpu.VMEM((1024, 128), BF16),
        pltpu.VMEM((32, 64), jnp.int32),
        pltpu.VMEM((16, 32, 64), F32),
        pltpu.VMEM((16, 128), F32),
        pltpu.VMEM((3, 384, 128), BF16),
        pltpu.VMEM((3, 384, 128), BF16),
        pltpu.VMEM((nc, 128, 256), BF16),
        pltpu.VMEM((64, 128), BF16),
        pltpu.VMEM((2, nc // 2, 64, 128), BF16),
        pltpu.VMEM((2, nc // 2, 64, 128), BF16),
        pltpu.VMEM((64, 128), BF16),
        pltpu.VMEM((128, 1024), BF16),
        pltpu.VMEM((144, 576), F32),
        pltpu.VMEM((2, 2, 32, 128), F32),
        pltpu.VMEM((2, 2, 32, 128), F32),
        pltpu.VMEM((8, 128), F32),
        pltpu.VMEM((nr, 8, 128), F32),
        pltpu.VMEM((80, 128), F32),
        pltpu.VMEM((nc, 8, 128), F32),
        pltpu.VMEM((nc, 8, 128), F32),
        pltpu.VMEM((2, 8, 128), F32),
        pltpu.VMEM((2, 8, 128), F32),
        pltpu.VMEM((36, W, 128), BF16),
        pltpu.VMEM((36, W, 128), BF16),
        pltpu.VMEM((8, 128), F32),
        pltpu.VMEM((2, nc // 2, 8, 128), F32),
        pltpu.VMEM((3, 8, 128), F32),
        pltpu.VMEM((3, 3, 8, 128), F32),
        pltpu.VMEM((32, 128), F32),
        pltpu.VMEM((24, LABELS), F32),
        pltpu.VMEM((nr, 24, LABELS), F32),
        pltpu.VMEM((36, W, 384), BF16),
        pltpu.VMEM((34, 64, 384), BF16),
        pltpu.VMEM((36, W, 384), BF16),
        pltpu.VMEM((4, 128, 512), BF16),
        pltpu.VMEM((4, 128, 512), BF16),
        pltpu.VMEM((3, 384, 128), BF16),
        pltpu.VMEM((34, W, 128), F32),
        pltpu.VMEM((34, W, 128), F32),
        pltpu.VMEM((2, 8, 128), F32),
        pltpu.VMEM((2, nc, 8, 128), F32),
        pltpu.VMEM((2, 8, 128), F32),
        pltpu.VMEM((2, nr, 8, 128), F32),
        pltpu.VMEM((2, 1152, 128), F32),
        pltpu.VMEM((2, 576, 128), F32),
        pltpu.VMEM((2, nc // 2, chunk, 128), BF16),
        pltpu.VMEM((2, nc // 2, chunk, 128), BF16),
        pltpu.VMEM((2, chunk, 128), F32),
        pltpu.VMEM((2, nr, chunk, 128), F32),
        pltpu.VMEM((2, chunk, 128), BF16),
        pltpu.VMEM((2, 2, nc // 2, chunk, 128), BF16),
        dma((11,)),
        dma((7,)),
        dma((7,)),
        dma((7,)),
        dma((7,)),
        dma((3,)),
        dma((3,)),
        dma((6,)),
        dma((6,)),
        dma((16,)),
        dma((16,)),
    ]
    enhanced, g1, g2, gg = pl.pallas_call(
        functools.partial(kernel, nr, nc),
        out_shape=(
            jax.ShapeDtypeStruct((32, 64, 128), BF16),
            jax.ShapeDtypeStruct((1152, 128), F32),
            jax.ShapeDtypeStruct((1152, 128), F32),
            jax.ShapeDtypeStruct((2, 4, 128), F32),
        ),
        in_specs=[hbm] * 11,
        out_specs=(vm, vm, vm, vm),
        scratch_shapes=scratch,
        compiler_params=pltpu.CompilerParams(
            collective_id=0, has_side_effects=True, vmem_limit_bytes=44 * 1024 * 1024
        ),
    )(
        *(
            pltpu.with_memory_space_constraint(x, pltpu.HBM)
            for x in (
                global_in.reshape(128, 64),
                jnp.swapaxes(global_first, 2, 3).reshape(9, 64, 1024),
                jnp.swapaxes(global_second, 2, 3).reshape(9, 64, 1024),
                project_weight,
                enhancer_input,
                instance_map,
                encoder_features,
                instance_weight,
                enhancer_first.reshape(3, 384, 128),
                enhancer_second.reshape(3, 384, 128),
                output_cotangent,
            )
        )
    )
    vms = [vm] * 4
    enhanced, g1, g2, gg = pl.pallas_call(
        hand_over,
        out_shape=tuple(jax.ShapeDtypeStruct(x.shape, x.dtype) for x in (enhanced, g1, g2, gg)),
        in_specs=vms,
        out_specs=tuple(vms),
        compiler_params=pltpu.CompilerParams(vmem_limit_bytes=16 * 1024 * 1024),
    )(enhanced, g1, g2, gg)
    return (enhanced, g1.reshape(3, 3, 128, 128), g2.reshape(3, 3, 128, 128), gg)


def solution(mesh):
    nr, nc = mesh.shape["rows"], mesh.shape["cols"]
    return jax.shard_map(
        functools.partial(per_device, nr, nc),
        mesh=mesh,
        in_specs=(
            P("rows", None, "cols"),
            P(None, None, None, "cols"),
            P(None, None, None, "cols"),
            P(),
            P("rows", "cols", None),
            P("rows", "cols"),
            P(None, "rows", "cols"),
            P(),
            P(),
            P(),
            P("rows", "cols", None),
        ),
        out_specs=(P("rows", "cols", None), P(), P(), P("rows", "cols", None)),
        check_vma=False,
    )
```

```python
import functools
import math

import jax
import jax.numpy as jnp
from jax import lax
from jax.experimental import pallas as pl
from jax.experimental.pallas import tpu as pltpu
from jax.sharding import PartitionSpec as P

MESH = pl.DeviceIdType.MESH
HIGH = lax.Precision.HIGHEST
F32 = jnp.float32
BF16 = jnp.bfloat16
EPS = 1e-05
LABELS = 256
UP = 16
W = 80


class Flow:
    def __init__(self, start, wait):
        self.start = start
        self.wait = wait


def mm(a, b):
    return jnp.dot(a, b, preferred_element_type=F32)


def mm_t0(a, b, **kw):
    return lax.dot_general(a, b, (((0,), (0,)), ((), ())), preferred_element_type=F32, **kw)


def mm_t1(a, b, **kw):
    return lax.dot_general(a, b, (((1,), (1,)), ((), ())), preferred_element_type=F32, **kw)


def kernel(
    nr,
    nc,
    gin_hbm,
    gw1_hbm,
    gw2_hbm,
    pw_hbm,
    ein,
    imap_hbm,
    feats_hbm,
    iw_hbm,
    w1_hbm,
    w2_hbm,
    cot,
    enh_out,
    g1_out,
    g2_out,
    gg_out,
    gin,
    gw1,
    gw2,
    pw,
    imap,
    feats,
    iw,
    w1,
    w2,
    bd,
    gsend,
    gbuf,
    hbuf,
    hsend,
    xcat,
    zs,
    psend,
    precv,
    ssend,
    sbuf,
    gop,
    gos,
    gob,
    csend,
    crecv,
    einp,
    cotp,
    pbuf,
    pall,
    nsend,
    nbp,
    ringp,
    fsend,
    fbuf,
    m3,
    a3,
    c3,
    cott,
    fgt,
    w2t,
    fa,
    ag,
    tsend,
    tall,
    gacc,
    gpair,
    ghalf,
    gcol,
    gred,
    grow,
    gfin,
    gall,
    local_sem,
    ring_s,
    ring_r,
    fwd_s,
    fwd_r,
    col_s,
    col_r,
    row_s,
    row_r,
    all_s,
    all_r,
    nb_s,
    nb_r,
):
    r = lax.axis_index("rows")
    c = lax.axis_index("cols")
    chips = nc // 2
    chip = c // 2
    core = lax.rem(c, 2)

    def remote(src, dst, ss, rs, dev):
        return pltpu.make_async_remote_copy(
            src_ref=src, dst_ref=dst, send_sem=ss, recv_sem=rs, device_id=dev, device_id_type=MESH
        )

    def one(i, src, dst, dev):
        copy = remote(src, dst, nb_s.at[i], nb_r.at[i], dev)
        return Flow(copy.start, copy.wait)

    def many(count, copy_of, got, ss, rs):
        def start():
            def body(k, carry):
                copy_of(k).start()
                return carry

            lax.fori_loop(1, count, body, 0)

        def wait():
            pltpu.make_async_copy(got, got, ss).wait()
            pltpu.make_async_copy(got, got, rs).wait()

        return Flow(start, wait)

    def to_cols(n, src_of, dst):
        def copy_of(k):
            t = lax.rem(c + k, nc)
            return remote(src_of(t), dst.at[c], col_s.at[n], col_r.at[n], (r, t))

        return many(nc, copy_of, dst.at[pl.ds(0, nc - 1)], col_s.at[n], col_r.at[n])

    def to_rows(n, src, dst):
        def copy_of(k):
            return remote(src, dst.at[r], row_s.at[n], row_r.at[n], (lax.rem(r + k, nr), c))

        return many(nr, copy_of, dst.at[pl.ds(0, nr - 1)], row_s.at[n], row_r.at[n])

    def to_all(n, src, dst):
        me = r * nc + c

        def copy_of(k):
            t = lax.rem(me + k, nr * nc)
            return remote(src, dst.at[me], all_s.at[n], all_r.at[n], (t // nc, lax.rem(t, nc)))

        got = dst.at[pl.ds(0, nr * nc - 1)]
        return many(nr * nc, copy_of, got, all_s.at[n], all_r.at[n])

    def to_chips(n, src_of, dst, got):
        def copy_of(k):
            t = lax.rem(chip + k, chips)
            return remote(src_of(t), dst, ring_s.at[n], ring_r.at[n], (r, 2 * t + core))

        return many(chips, copy_of, got, ring_s.at[n], ring_r.at[n])

    def to_partner(n, src, dst):
        copy = remote(src, dst, fwd_s.at[n], fwd_r.at[n], (r, 2 * chip + 1 - core))
        return Flow(copy.start, copy.wait)

    def gather(n, src, dst):
        return (
            to_chips(n, lambda t: src, dst.at[core, chip], dst.at[core, pl.ds(0, chips - 1)]),
            to_partner(n, dst.at[core], dst.at[core]),
        )

    def own_block(src, dst):
        dst[pl.ds(core, 1), pl.ds(chip, 1)] = src[...][None, None]

    def wrap_r(d):
        return lax.rem(r + d + nr, nr)

    def wrap_c(d):
        return lax.rem(c + d + nc, nc)

    pairs = {
        "gin": (gin_hbm, gin),
        "feats": (feats_hbm, feats),
        "imap": (imap_hbm, imap),
        "gw1": (gw1_hbm, gw1),
        "w2": (w2_hbm, w2),
        "cot": (cot, cotp.at[pl.ds(2, 32), pl.ds(0, 64)]),
        "iw": (iw_hbm, iw),
        "gw2": (gw2_hbm, gw2),
        "pw": (pw_hbm, pw),
        "ein": (ein, einp.at[pl.ds(2, 32), pl.ds(0, 64)]),
        "w1": (w1_hbm, w1),
    }
    own = {
        name: pltpu.make_async_copy(src, dst, local_sem.at[i])
        for i, (name, (src, dst)) in enumerate(pairs.items())
    }
    for copy in own.values():
        copy.start()

    barrier = pltpu.get_barrier_semaphore()

    def greet(dr, dc):
        pl.semaphore_signal(barrier, inc=1, device_id=(wrap_r(dr), lax.rem(c + dc, nc)), device_id_type=MESH)

    def greet_cols(k, carry):
        greet(0, k)
        return carry

    def greet_rows(k, carry):
        greet(k, 0)
        return carry

    lax.fori_loop(1, nc, greet_cols, 0)
    lax.fori_loop(1, nr, greet_rows, 0)

    own["gin"].wait()
    gsend[:, 0:64] = gin[0:64, :]
    gsend[:, 64:128] = gin[64:128, :]

    own["feats"].wait()
    own["imap"].wait()
    lane8 = lax.broadcasted_iota(jnp.int32, (8, 64), 1)
    row8 = lax.broadcasted_iota(jnp.int32, (8, 64), 0)
    packed = jnp.zeros((8, 16), F32)
    label = jnp.zeros((8, 1), F32)
    for br in range(2):
        strip = jnp.sum(feats[:, br * UP : (br + 1) * UP, :], axis=1)
        pick = ((lane8 // UP == row8 % 4) & (row8 // 4 == br)).astype(F32)
        packed = packed + mm_t1(pick, strip, precision=HIGH)
        corner = ((lane8 == UP * (row8 % 4)) & (row8 // 4 == br)).astype(F32)
        line = imap[br * UP : br * UP + 1, :].astype(F32)
        label = label + jnp.sum(corner * line, axis=1, keepdims=True)
    pbuf[...] = jnp.zeros_like(pbuf)
    pbuf[:, 0:16] = packed
    pbuf[:, 16:17] = jnp.full((8, 1), float(UP * UP), F32)
    pbuf[:, 17:18] = label

    pl.semaphore_wait(barrier, nc - 1 + nr - 1)

    first_in, first_fwd = gather(0, gsend, gbuf)
    first_in.start()
    own_block(gsend, gbuf)
    sums_in, sums_fwd = gather(1, pbuf, pall)
    sums_in.start()
    own_block(pbuf, pall)

    def halo(i, src, dst):
        rows32 = pl.ds(2, 32)
        sides = [
            one(4 * i, src.at[:, pl.ds(0, 8)], dst.at[rows32, pl.ds(64, 8)], (r, wrap_c(-1))),
            one(4 * i + 1, src.at[:, pl.ds(56, 8)], dst.at[rows32, pl.ds(72, 8)], (r, wrap_c(1))),
        ]
        ends = [
            one(4 * i + 2, dst.at[pl.ds(2, 2)], dst.at[pl.ds(34, 2)], (wrap_r(-1), c)),
            one(4 * i + 3, dst.at[pl.ds(32, 2)], dst.at[pl.ds(0, 2)], (wrap_r(1), c)),
        ]
        return sides, ends

    cot_sides, cot_ends = halo(0, cot, cotp)
    ein_sides, ein_ends = halo(1, ein, einp)
    for flow in cot_sides:
        flow.start()

    own["w2"].wait()
    for a in range(3):
        for b in range(3):
            w2t[a, b * 128 : (b + 1) * 128, :] = (
                w2[2 - a, (2 - b) * 128 : (3 - b) * 128, :].astype(F32).T.astype(BF16)
            )
    own["pw"].wait()
    bd[...] = jnp.zeros_like(bd)
    for k in range(nc):
        bd[k, 0:64, 0:128] = pw[k * 64 : (k + 1) * 64, :]
        bd[k, 64:128, 128:256] = pw[k * 64 : (k + 1) * 64, :]

    col80 = lax.broadcasted_iota(jnp.int32, (W, 128), 0)
    colown = col80 < 64
    colmap = colown | ((col80 < 72) & (c < nc - 1)) | ((col80 >= 72) & (c > 0))

    def shifts(value):
        return jnp.concatenate(
            [
                pltpu.roll(value, 1, 0).astype(BF16),
                value.astype(BF16),
                pltpu.roll(value, W - 1, 0).astype(BF16),
            ],
            axis=1,
        )

    def in_map(i, first, last):
        return colmap & ((i >= first) | (r > 0)) & ((i <= last) | (r < nr - 1))

    map_sums = to_rows(0, fsend, fbuf)
    near = [
        one(8, nsend, nbp.at[2], (wrap_r(-1), c)),
        one(9, nsend, nbp.at[0], (wrap_r(1), c)),
    ]

    def edge_window():
        own["cot"].wait()
        for flow in cot_sides:
            flow.wait()
        for flow in cot_ends:
            flow.start()

    def stats_window():
        sums_fwd.wait()
        band_p = pall[...].reshape(8 * nc, 128)
        hot = (
            lax.broadcasted_iota(jnp.int32, (8 * nc, LABELS), 1)
            == band_p[:, 17:18].astype(jnp.int32)
        ).astype(F32)
        fsend[...] = mm_t0(band_p, hot, precision=HIGH)[0:24, :]
        map_sums.start()
        fbuf[pl.ds(r, 1)] = fsend[...][None]
        nsend[1] = pbuf[...]
        for i, t in ((0, wrap_c(-1)), (2, wrap_c(1))):
            nsend[pl.ds(i, 1)] = pall[pl.ds(lax.rem(t, 2), 1), pl.ds(t // 2, 1)][0]
        nbp[1] = nsend[...]
        for flow in near:
            flow.start()

    def band_conv(buf, w, n, window):
        for k in range(nc):
            block = buf[k % 2, k // 2]
            xcat[0:64, k * 64 : (k + 1) * 64] = block[:, 0:64]
            xcat[64:128, k * 64 : (k + 1) * 64] = block[:, 64:128]
        j = lax.broadcasted_iota(jnp.int32, (128, 64), 0) % 64
        z = mm_t1(xcat[...], w[...].reshape(576, 1024))
        zs[8:136, :] = z
        out = []
        for a in range(3):
            t = a * 192
            before = jnp.where(j > 0, zs[7:135, t : t + 64], 0.0)
            after = jnp.where(j < 63, zs[9:137, t + 128 : t + 192], 0.0)
            out.append(before + z[:, t + 64 : t + 128] + after)
        for half in range(2):
            psend[n, 0, :, half * 64 : half * 64 + 64] = out[2][32 * half : 32 * half + 32]
            psend[n, 1, :, half * 64 : half * 64 + 64] = out[0][64 + 32 * half : 96 + 32 * half]
        up = one(10 + 2 * n, psend.at[n, 0], precv.at[n, 1], (wrap_r(-1), c))
        down = one(11 + 2 * n, psend.at[n, 1], precv.at[n, 0], (wrap_r(1), c))
        up.start()
        down.start()
        top = out[1][0:64] + out[2][64:128]
        low = out[0][0:64] + out[1][64:128]
        window()
        up.wait()
        down.wait()
        came = [
            jnp.concatenate([precv[n, i, :, 0:64], precv[n, i, :, 64:128]], axis=0)
            for i in range(2)
        ]
        top = top + jnp.where(r > 0, came[0], 0.0)
        low = low + jnp.where(r < nr - 1, came[1], 0.0)
        return jnp.concatenate([top, low], axis=0)

    zs[...] = jnp.zeros_like(zs)
    first_in.wait()
    first_fwd.start()
    sums_in.wait()
    sums_fwd.start()
    own["gw1"].wait()
    first_fwd.wait()
    first_raw = band_conv(gbuf, gw1, 0, edge_window)
    ssend[...] = jnp.zeros_like(ssend)
    ssend[0:1, 0:64] = jnp.sum(first_raw, 0, keepdims=True)
    ssend[1:2, 0:64] = jnp.sum(first_raw * first_raw, 0, keepdims=True)
    band_stats = to_rows(1, ssend, sbuf)
    band_stats.start()
    sbuf[pl.ds(r, 1)] = ssend[...][None]
    for flow in ein_sides:
        flow.start()
    stats_window()
    band_stats.wait()
    sums = jnp.sum(sbuf[...], axis=0)[:, 0:64]
    band_total = float(nr * 128)
    band_mean = sums[0:1, :] / band_total
    band_var = sums[1:2, :] / band_total - band_mean * band_mean
    normed = (first_raw - band_mean) * lax.rsqrt(band_var + EPS)
    hidden = jnp.maximum(normed, 0.0).astype(BF16)
    hsend[:, 0:64] = hidden[0:64]
    hsend[:, 64:128] = hidden[64:128]
    hidden_in, hidden_fwd = gather(2, hsend, hbuf)
    hidden_in.start()
    own_block(hsend, hbuf)

    for flow in cot_ends:
        flow.wait()
    own["ein"].wait()
    for flow in ein_sides:
        flow.wait()

    def cot_row(i, carry):
        value = jnp.where(in_map(i, 2, 33), cotp[i].astype(F32), 0.0)
        c3[i] = shifts(value)
        return carry

    lax.fori_loop(0, 36, cot_row, 0)

    def cot_turn(q, carry):
        value = cotp[pl.ds(2 + 8 * q, 8), 0:64, :].astype(F32)
        cott[q] = value.reshape(512, 128).T.astype(BF16)
        return carry

    lax.fori_loop(0, 4, cot_turn, 0)

    hidden_in.wait()
    hidden_fwd.start()
    for flow in ein_ends:
        flow.start()
    own["gw2"].wait()
    hidden_fwd.wait()
    second_raw = band_conv(hbuf, gw2, 1, lambda: None)
    global_out = (gin[...].astype(F32) + second_raw).astype(BF16).astype(F32)
    gop[...] = jnp.zeros_like(gop)
    gop[8:72, 0:64] = global_out[0:64]
    gop[8:72, 64:128] = global_out[64:128]
    for t in range(nc):
        gos[t] = gop[4 * t + 7 : 4 * t + 15, :]

    spread_out = to_cols(0, lambda t: gos.at[t], gob)
    spread_out.start()
    gob[pl.ds(c, 1)] = gos[pl.ds(c, 1)]
    for flow in ein_ends:
        flow.wait()
    map_sums.wait()
    for flow in near:
        flow.wait()
    fsum = jnp.sum(fbuf[...], axis=0)
    averages = fsum[0:16, :] / jnp.maximum(fsum[16:17, :], 1.0)
    ringp[...] = jnp.zeros_like(ringp)
    for br in range(4):
        dr, their_br = {0: (0, 1), 1: (1, 0), 2: (1, 1), 3: (2, 0)}[br]
        for q in range(6):
            dc, their_bc = (0, 3) if q == 0 else (2, 0) if q == 5 else (1, q - 1)
            p = their_br * 4 + their_bc
            ringp[br * 8 + q : br * 8 + q + 1, :] = nbp[dr, dc, p : p + 1, :]
    ring_hot = (
        lax.broadcasted_iota(jnp.int32, (32, LABELS), 1) == ringp[:, 17:18].astype(jnp.int32)
    ).astype(F32)
    own["iw"].wait()
    ring_avg = mm_t1(ring_hot, averages, precision=HIGH)
    pooled = jnp.dot(ring_avg, iw[...], precision=HIGH, preferred_element_type=F32)
    spread_out.wait()
    packets = jnp.concatenate([gob[k].astype(BF16) for k in range(nc)], axis=1)
    both = mm(packets, bd[...].reshape(nc * 128, 256)).astype(BF16).astype(F32)
    csend[0] = both[:, 0:128]
    csend[1] = both[:, 128:256]
    edges = [
        one(14, csend.at[0], crecv.at[1], (wrap_r(-1), c)),
        one(15, csend.at[1], crecv.at[0], (wrap_r(1), c)),
    ]
    for flow in edges:
        flow.start()

    def mix_rows(br, coarse, start, stop):
        terms = coarse + pooled[br * 8 : br * 8 + 8]
        pieces = []
        for q in (1, 2, 3, 4, 5, 0):
            line = terms[q : q + 1, :]
            pieces.append(jnp.broadcast_to(line, (8 if q in (0, 5) else UP, 128)))
        add = jnp.concatenate(pieces, axis=0)

        def mix_row(i, carry):
            value = einp[i].astype(F32) + add
            value = jnp.where(in_map(i, 2, 33), value, 0.0).astype(BF16).astype(F32)
            m3[i] = shifts(value)
            return carry

        lax.fori_loop(start, stop, mix_row, 0)

    mix_rows(1, both[:, 0:128], 2, 18)
    mix_rows(2, both[:, 128:256], 18, 34)
    own["w1"].wait()

    def conv_part(src, w, first, count):
        width = src.shape[1]
        x = jnp.concatenate(
            [src[first + a : first + a + count].reshape(count * width, 384) for a in range(3)],
            axis=1,
        )
        return mm(x, w[...].reshape(1152, 128)).reshape(count, width, 128)

    fa[2:17] = conv_part(m3, w1, 2, 15)
    fa[17:32] = conv_part(m3, w1, 17, 15)
    for flow in edges:
        flow.wait()
    mix_rows(0, crecv[0], 0, 2)
    mix_rows(3, crecv[1], 34, 36)
    fa[0:2] = conv_part(m3, w1, 0, 2)
    fa[32:34] = conv_part(m3, w1, 32, 2)

    tile_all = [to_all(n, tsend.at[n], tall.at[n]) for n in range(2)]

    def tile_sums(n, x, y):
        tsend[n, 0:1, :] = jnp.sum(x, axis=(0, 1))[None]
        tsend[n, 1:2, :] = jnp.sum(y, axis=(0, 1))[None]
        tile_all[n].start()
        tall[n, pl.ds(r * nc + c, 1)] = tsend[n][None]

    def tile_sums_2(n):
        tile_all[n].wait()
        return jnp.sum(tall[n], axis=0)

    act = fa[1:33, 0:64, :]
    tile_sums(0, act, act * act)
    ag[0:17] = conv_part(c3, w2t, 0, 17)
    ag[17:34] = conv_part(c3, w2t, 17, 17)
    sums = tile_sums_2(0)
    pixels = float(nr * nc * 2048)
    act_mean = sums[0:1, :] / pixels
    inverse_dev = lax.rsqrt(sums[1:2, :] / pixels - act_mean * act_mean + EPS)

    def act_row(i, carry):
        na = (fa[i] - act_mean) * inverse_dev
        s = jax.nn.sigmoid(na)
        fa[i] = na
        ng = ag[i] * s * (1.0 + na * (1.0 - s))
        ag[i] = ng
        value = jnp.where(in_map(i, 1, 32), na * s, 0.0).astype(BF16).astype(F32)
        a3[i] = shifts(value)[0:64]
        return carry

    lax.fori_loop(0, 34, act_row, 0)
    ng = ag[1:33, 0:64, :]
    tile_sums(1, ng, ng * fa[1:33, 0:64, :])

    def weight_part(n, turned, src, first):
        for a in range(3):
            got = jnp.zeros((128, 384), F32)
            for q in range(4):
                start = first + a + 8 * q
                rhs = src[start : start + 8, 0:64, :].reshape(512, 384)
                got = got + mm(turned[q], rhs)
            for b in range(3):
                gacc[n, a * 384 + b * 128 : a * 384 + (b + 1) * 128, :] = got[
                    :, b * 128 : (b + 1) * 128
                ].T

    half_rows = 1152 // 2
    chunk = half_rows // chips

    def half_of(h):
        return pl.ds(pl.multiple_of(h * half_rows, 16), half_rows)

    def piece(h, q):
        return pl.ds(pl.multiple_of(h * half_rows + q * chunk, 8), chunk)

    pair_sum = [to_partner(3 + n, gacc.at[n, half_of(1 - core)], gpair.at[n]) for n in range(2)]
    band_sum = [
        to_chips(
            3 + n,
            lambda t, n=n: ghalf.at[n, t],
            gcol.at[n, chip],
            gcol.at[n, pl.ds(0, chips - 1)],
        )
        for n in range(2)
    ]
    map_sum = [to_rows(2 + n, gred.at[n], grow.at[n]) for n in range(2)]
    share = [
        to_chips(
            5 + n,
            lambda t, n=n: gfin.at[n],
            gall.at[n, core, chip],
            gall.at[n, core, pl.ds(0, chips - 1)],
        )
        for n in range(2)
    ]
    share_fwd = [to_partner(5 + n, gall.at[n, core], gall.at[n, core]) for n in range(2)]

    def grad_0(n):
        pair_sum[n].start()

    def grad_1(n):
        pair_sum[n].wait()
        total = gacc[n, half_of(core)] + gpair[n]
        ghalf[n] = total.astype(BF16).reshape(chips, chunk, 128)
        band_sum[n].start()
        gcol[n, pl.ds(chip, 1)] = ghalf[n, pl.ds(chip, 1)]

    def grad_2(n):
        band_sum[n].wait()
        gred[n] = jnp.sum(gcol[n].astype(F32), axis=0)
        map_sum[n].start()
        grow[n, pl.ds(r, 1)] = gred[n][None]

    def grad_3(n):
        map_sum[n].wait()
        total = jnp.sum(grow[n], axis=0)
        gfin[n] = (total * (1.0 / math.sqrt(pixels))).astype(BF16)
        share[n].start()
        gall[n, pl.ds(core, 1), pl.ds(chip, 1)] = gfin[n][None, None]

    def grad_4(n):
        share[n].wait()
        share_fwd[n].start()

    def grad_5(n, out):
        share_fwd[n].wait()
        out[...] = gall[n].reshape(1152, 128).astype(F32)

    weight_part(1, cott, a3, 0)
    grad_0(1)
    for half in range(2):
        got = conv_part(a3, w2, 16 * half, 16)
        enh_out[16 * half : 16 * half + 16] = (
            m3[2 + 16 * half : 18 + 16 * half, 0:64, 128:256].astype(F32) + got
        ).astype(BF16)
    sums = tile_sums_2(1)
    grad_mean = sums[0:1, :] / pixels
    cross_mean = sums[1:2, :] / pixels
    grad_1(1)

    def grad_row(i, carry):
        fg = inverse_dev * (ag[i] - grad_mean - fa[i] * cross_mean)
        fg = jnp.where(in_map(i, 1, 32), fg, 0.0).astype(BF16).astype(F32)
        ag[i] = fg

        return carry

    lax.fori_loop(0, 34, grad_row, 0)

    def grad_turn(q, carry):
        value = ag[pl.ds(1 + 8 * q, 8), 0:64, :]
        fgt[q] = value.reshape(512, 128).T.astype(BF16)
        return carry

    lax.fori_loop(0, 4, grad_turn, 0)
    weight_part(0, fgt, m3, 1)
    grad_0(0)

    grad_1(0)
    grad_2(1)

    rows24 = lax.broadcasted_iota(jnp.int32, (24, W), 0)
    cols24 = lax.broadcasted_iota(jnp.int32, (24, W), 1)
    left = UP * (rows24 % 8) + 1 - rows24 // 8
    inside = (cols24 >= left) & (cols24 < left + UP)
    window = ((inside | ((left < 0) & (cols24 == W - 1))) & (rows24 % 8 < 4)).astype(F32)
    picked = [[], [], []]
    direct = []
    for br in range(2):
        total = jnp.sum(ag[UP * br + 1 : UP * br + 17], axis=0)
        below = total - ag[UP * br + 1] + ag[UP * br + 17]
        above = total - ag[UP * br + 16] + ag[UP * br]
        for a, strip in enumerate((below, total, above)):
            picked[a].append(jnp.dot(window, strip, precision=HIGH, preferred_element_type=F32))
        strip = jnp.sum(c3[UP * br + 2 : UP * br + 18, :, 128:256].astype(F32), axis=0)
        direct.append(jnp.dot(window, strip, precision=HIGH, preferred_element_type=F32)[8:16])
    result = jnp.concatenate(direct, axis=0)
    for a in range(3):
        for b in range(3):
            s_ab = jnp.concatenate([picked[a][br][8 * b : 8 * b + 8] for br in range(2)], axis=0)
            result = result + mm_t1(
                s_ab, w1[a, b * 128 : (b + 1) * 128, :].astype(F32), precision=HIGH
            )
    gg_out[0] = result[0:4] * (1.0 / UP)
    gg_out[1] = result[8:12] * (1.0 / UP)

    grad_2(0)
    grad_3(1)
    grad_3(0)
    grad_4(1)
    grad_4(0)
    grad_5(1, g2_out)
    grad_5(0, g1_out)


def hand_over(*refs):
    half = len(refs) // 2
    for source, target in zip(refs[:half], refs[half:]):
        target[...] = source[...]


def per_device(
    nr,
    nc,
    global_in,
    global_first,
    global_second,
    project_weight,
    enhancer_input,
    instance_map,
    encoder_features,
    instance_weight,
    enhancer_first,
    enhancer_second,
    output_cotangent,
):
    vm = pl.BlockSpec(memory_space=pltpu.VMEM)
    hbm = pl.BlockSpec(memory_space=pltpu.HBM)
    chunk = 1152 // nc
    dma = pltpu.SemaphoreType.DMA
    scratch = [
        pltpu.VMEM((128, 64), BF16),
        pltpu.VMEM((9, 64, 1024), BF16),
        pltpu.VMEM((9, 64, 1024), BF16),
        pltpu.VMEM((1024, 128), BF16),
        pltpu.VMEM((32, 64), jnp.int32),
        pltpu.VMEM((16, 32, 64), F32),
        pltpu.VMEM((16, 128), F32),
        pltpu.VMEM((3, 384, 128), BF16),
        pltpu.VMEM((3, 384, 128), BF16),
        pltpu.VMEM((nc, 128, 256), BF16),
        pltpu.VMEM((64, 128), BF16),
        pltpu.VMEM((2, nc // 2, 64, 128), BF16),
        pltpu.VMEM((2, nc // 2, 64, 128), BF16),
        pltpu.VMEM((64, 128), BF16),
        pltpu.VMEM((128, 1024), BF16),
        pltpu.VMEM((144, 576), F32),
        pltpu.VMEM((2, 2, 32, 128), F32),
        pltpu.VMEM((2, 2, 32, 128), F32),
        pltpu.VMEM((8, 128), F32),
        pltpu.VMEM((nr, 8, 128), F32),
        pltpu.VMEM((80, 128), F32),
        pltpu.VMEM((nc, 8, 128), F32),
        pltpu.VMEM((nc, 8, 128), F32),
        pltpu.VMEM((2, 8, 128), F32),
        pltpu.VMEM((2, 8, 128), F32),
        pltpu.VMEM((36, W, 128), BF16),
        pltpu.VMEM((36, W, 128), BF16),
        pltpu.VMEM((8, 128), F32),
        pltpu.VMEM((2, nc // 2, 8, 128), F32),
        pltpu.VMEM((3, 8, 128), F32),
        pltpu.VMEM((3, 3, 8, 128), F32),
        pltpu.VMEM((32, 128), F32),
        pltpu.VMEM((24, LABELS), F32),
        pltpu.VMEM((nr, 24, LABELS), F32),
        pltpu.VMEM((36, W, 384), BF16),
        pltpu.VMEM((34, 64, 384), BF16),
        pltpu.VMEM((36, W, 384), BF16),
        pltpu.VMEM((4, 128, 512), BF16),
        pltpu.VMEM((4, 128, 512), BF16),
        pltpu.VMEM((3, 384, 128), BF16),
        pltpu.VMEM((34, W, 128), F32),
        pltpu.VMEM((34, W, 128), F32),
        pltpu.VMEM((2, 2, 128), F32),
        pltpu.VMEM((2, nr * nc, 2, 128), F32),
        pltpu.VMEM((2, 1152, 128), F32),
        pltpu.VMEM((2, 576, 128), F32),
        pltpu.VMEM((2, nc // 2, chunk, 128), BF16),
        pltpu.VMEM((2, nc // 2, chunk, 128), BF16),
        pltpu.VMEM((2, chunk, 128), F32),
        pltpu.VMEM((2, nr, chunk, 128), F32),
        pltpu.VMEM((2, chunk, 128), BF16),
        pltpu.VMEM((2, 2, nc // 2, chunk, 128), BF16),
        dma((11,)),
        dma((7,)),
        dma((7,)),
        dma((7,)),
        dma((7,)),
        dma((1,)),
        dma((1,)),
        dma((4,)),
        dma((4,)),
        dma((2,)),
        dma((2,)),
        dma((16,)),
        dma((16,)),
    ]
    enhanced, g1, g2, gg = pl.pallas_call(
        functools.partial(kernel, nr, nc),
        out_shape=(
            jax.ShapeDtypeStruct((32, 64, 128), BF16),
            jax.ShapeDtypeStruct((1152, 128), F32),
            jax.ShapeDtypeStruct((1152, 128), F32),
            jax.ShapeDtypeStruct((2, 4, 128), F32),
        ),
        in_specs=[hbm] * 11,
        out_specs=(vm, vm, vm, vm),
        scratch_shapes=scratch,
        compiler_params=pltpu.CompilerParams(
            collective_id=0, has_side_effects=True, vmem_limit_bytes=44 * 1024 * 1024
        ),
    )(
        *(
            pltpu.with_memory_space_constraint(x, pltpu.HBM)
            for x in (
                global_in.reshape(128, 64),
                jnp.swapaxes(global_first, 2, 3).reshape(9, 64, 1024),
                jnp.swapaxes(global_second, 2, 3).reshape(9, 64, 1024),
                project_weight,
                enhancer_input,
                instance_map,
                encoder_features,
                instance_weight,
                enhancer_first.reshape(3, 384, 128),
                enhancer_second.reshape(3, 384, 128),
                output_cotangent,
            )
        )
    )
    vms = [vm] * 4
    enhanced, g1, g2, gg = pl.pallas_call(
        hand_over,
        out_shape=tuple(jax.ShapeDtypeStruct(x.shape, x.dtype) for x in (enhanced, g1, g2, gg)),
        in_specs=vms,
        out_specs=tuple(vms),
        compiler_params=pltpu.CompilerParams(vmem_limit_bytes=16 * 1024 * 1024),
    )(enhanced, g1, g2, gg)
    return (enhanced, g1.reshape(3, 3, 128, 128), g2.reshape(3, 3, 128, 128), gg)


def solution(mesh):
    nr, nc = mesh.shape["rows"], mesh.shape["cols"]
    return jax.shard_map(
        functools.partial(per_device, nr, nc),
        mesh=mesh,
        in_specs=(
            P("rows", None, "cols"),
            P(None, None, None, "cols"),
            P(None, None, None, "cols"),
            P(),
            P("rows", "cols", None),
            P("rows", "cols"),
            P(None, "rows", "cols"),
            P(),
            P(),
            P(),
            P("rows", "cols", None),
        ),
        out_specs=(P("rows", "cols", None), P(), P(), P("rows", "cols", None)),
        check_vma=False,
    )
```

```python
import functools
import math

import jax
import jax.numpy as jnp
from jax import lax
from jax.experimental import pallas as pl
from jax.experimental.pallas import tpu as pltpu
from jax.sharding import PartitionSpec as P

MESH = pl.DeviceIdType.MESH
HIGH = lax.Precision.HIGHEST
F32 = jnp.float32
BF16 = jnp.bfloat16
EPS = 1e-05
LABELS = 256
UP = 16
W = 80


class Flow:
    def __init__(self, start, wait):
        self.start = start
        self.wait = wait


def mm(a, b):
    return jnp.dot(a, b, preferred_element_type=F32)


def mm_t0(a, b, **kw):
    return lax.dot_general(a, b, (((0,), (0,)), ((), ())), preferred_element_type=F32, **kw)


def mm_t1(a, b, **kw):
    return lax.dot_general(a, b, (((1,), (1,)), ((), ())), preferred_element_type=F32, **kw)


def kernel(
    nr,
    nc,
    gin_hbm,
    gw1_hbm,
    gw2_hbm,
    pw_hbm,
    ein,
    imap_hbm,
    feats_hbm,
    iw_hbm,
    w1_hbm,
    w2_hbm,
    cot,
    enh_out,
    g1_out,
    g2_out,
    gg_out,
    gin,
    gw1,
    gw2,
    pw,
    imap,
    feats,
    iw,
    w1,
    w2,
    bd,
    gsend,
    gbuf,
    hbuf,
    hsend,
    xcat,
    zs,
    psend,
    precv,
    ssend,
    sbuf,
    gop,
    gos,
    gob,
    csend,
    crecv,
    einp,
    cotp,
    pbuf,
    pall,
    nsend,
    nbp,
    ringp,
    fsend,
    fbuf,
    m3,
    a3,
    c3,
    cott,
    fgt,
    w2t,
    fa,
    ag,
    tsend,
    tall,
    gacc,
    gpair,
    ghalf,
    gcol,
    gred,
    grow,
    gfin,
    gall,
    local_sem,
    ring_s,
    ring_r,
    fwd_s,
    fwd_r,
    col_s,
    col_r,
    row_s,
    row_r,
    all_s,
    all_r,
    nb_s,
    nb_r,
):
    r = lax.axis_index("rows")
    c = lax.axis_index("cols")
    chips = nc // 2
    chip = c // 2
    core = lax.rem(c, 2)

    def remote(src, dst, ss, rs, dev):
        return pltpu.make_async_remote_copy(
            src_ref=src, dst_ref=dst, send_sem=ss, recv_sem=rs, device_id=dev, device_id_type=MESH
        )

    def one(i, src, dst, dev):
        copy = remote(src, dst, nb_s.at[i], nb_r.at[i], dev)
        return Flow(copy.start, copy.wait)

    def many(count, copy_of, got, ss, rs):
        def start():
            def body(k, carry):
                copy_of(k).start()
                return carry

            lax.fori_loop(1, count, body, 0)

        def wait():
            pltpu.make_async_copy(got, got, ss).wait()
            pltpu.make_async_copy(got, got, rs).wait()

        return Flow(start, wait)

    def to_cols(n, src_of, dst):
        def copy_of(k):
            t = lax.rem(c + k, nc)
            return remote(src_of(t), dst.at[c], col_s.at[n], col_r.at[n], (r, t))

        return many(nc, copy_of, dst.at[pl.ds(0, nc - 1)], col_s.at[n], col_r.at[n])

    def to_rows(n, src, dst):
        def copy_of(k):
            return remote(src, dst.at[r], row_s.at[n], row_r.at[n], (lax.rem(r + k, nr), c))

        return many(nr, copy_of, dst.at[pl.ds(0, nr - 1)], row_s.at[n], row_r.at[n])

    def to_all(n, src, dst):
        me = r * nc + c

        def copy_of(k):
            t = lax.rem(me + k, nr * nc)
            return remote(src, dst.at[me], all_s.at[n], all_r.at[n], (t // nc, lax.rem(t, nc)))

        got = dst.at[pl.ds(0, nr * nc - 1)]
        return many(nr * nc, copy_of, got, all_s.at[n], all_r.at[n])

    def to_chips(n, src_of, dst, got):
        def copy_of(k):
            t = lax.rem(chip + k, chips)
            return remote(src_of(t), dst, ring_s.at[n], ring_r.at[n], (r, 2 * t + core))

        return many(chips, copy_of, got, ring_s.at[n], ring_r.at[n])

    def to_partner(n, src, dst):
        copy = remote(src, dst, fwd_s.at[n], fwd_r.at[n], (r, 2 * chip + 1 - core))
        return Flow(copy.start, copy.wait)

    def gather(n, src, dst):
        return (
            to_chips(n, lambda t: src, dst.at[core, chip], dst.at[core, pl.ds(0, chips - 1)]),
            to_partner(n, dst.at[core], dst.at[core]),
        )

    def own_block(src, dst):
        dst[pl.ds(core, 1), pl.ds(chip, 1)] = src[...][None, None]

    def wrap_r(d):
        return lax.rem(r + d + nr, nr)

    def wrap_c(d):
        return lax.rem(c + d + nc, nc)

    pairs = {
        "gin": (gin_hbm, gin),
        "feats": (feats_hbm, feats),
        "imap": (imap_hbm, imap),
        "gw1": (gw1_hbm, gw1),
        "w2": (w2_hbm, w2),
        "cot": (cot, cotp.at[pl.ds(2, 32), pl.ds(0, 64)]),
        "iw": (iw_hbm, iw),
        "gw2": (gw2_hbm, gw2),
        "pw": (pw_hbm, pw),
        "ein": (ein, einp.at[pl.ds(2, 32), pl.ds(0, 64)]),
        "w1": (w1_hbm, w1),
    }
    own = {
        name: pltpu.make_async_copy(src, dst, local_sem.at[i])
        for i, (name, (src, dst)) in enumerate(pairs.items())
    }
    for copy in own.values():
        copy.start()

    barrier = pltpu.get_barrier_semaphore()

    def greet(dr, dc):
        pl.semaphore_signal(barrier, inc=1, device_id=(wrap_r(dr), lax.rem(c + dc, nc)), device_id_type=MESH)

    def greet_cols(k, carry):
        greet(0, k)
        return carry

    def greet_rows(k, carry):
        greet(k, 0)
        return carry

    lax.fori_loop(1, nc, greet_cols, 0)
    lax.fori_loop(1, nr, greet_rows, 0)

    own["gin"].wait()
    gsend[:, 0:64] = gin[0:64, :]
    gsend[:, 64:128] = gin[64:128, :]

    own["feats"].wait()
    own["imap"].wait()
    lane8 = lax.broadcasted_iota(jnp.int32, (8, 64), 1)
    row8 = lax.broadcasted_iota(jnp.int32, (8, 64), 0)
    packed = jnp.zeros((8, 16), F32)
    label = jnp.zeros((8, 1), F32)
    for br in range(2):
        strip = jnp.sum(feats[:, br * UP : (br + 1) * UP, :], axis=1)
        pick = ((lane8 // UP == row8 % 4) & (row8 // 4 == br)).astype(F32)
        packed = packed + mm_t1(pick, strip, precision=HIGH)
        corner = ((lane8 == UP * (row8 % 4)) & (row8 // 4 == br)).astype(F32)
        line = imap[br * UP : br * UP + 1, :].astype(F32)
        label = label + jnp.sum(corner * line, axis=1, keepdims=True)
    pbuf[...] = jnp.zeros_like(pbuf)
    pbuf[:, 0:16] = packed
    pbuf[:, 16:17] = jnp.full((8, 1), float(UP * UP), F32)
    pbuf[:, 17:18] = label

    pl.semaphore_wait(barrier, nc - 1 + nr - 1)

    first_in, first_fwd = gather(0, gsend, gbuf)
    first_in.start()
    own_block(gsend, gbuf)
    sums_in, sums_fwd = gather(1, pbuf, pall)
    sums_in.start()
    own_block(pbuf, pall)

    def halo(i, src, dst):
        rows32 = pl.ds(2, 32)
        sides = [
            one(4 * i, src.at[:, pl.ds(0, 8)], dst.at[rows32, pl.ds(64, 8)], (r, wrap_c(-1))),
            one(4 * i + 1, src.at[:, pl.ds(56, 8)], dst.at[rows32, pl.ds(72, 8)], (r, wrap_c(1))),
        ]
        ends = [
            one(4 * i + 2, dst.at[pl.ds(2, 2)], dst.at[pl.ds(34, 2)], (wrap_r(-1), c)),
            one(4 * i + 3, dst.at[pl.ds(32, 2)], dst.at[pl.ds(0, 2)], (wrap_r(1), c)),
        ]
        return sides, ends

    cot_sides, cot_ends = halo(0, cot, cotp)
    ein_sides, ein_ends = halo(1, ein, einp)
    for flow in cot_sides:
        flow.start()

    own["w2"].wait()
    for a in range(3):
        for b in range(3):
            w2t[a, b * 128 : (b + 1) * 128, :] = (
                w2[2 - a, (2 - b) * 128 : (3 - b) * 128, :].astype(F32).T.astype(BF16)
            )
    own["pw"].wait()
    bd[...] = jnp.zeros_like(bd)
    for k in range(nc):
        bd[k, 0:64, 0:128] = pw[k * 64 : (k + 1) * 64, :]
        bd[k, 64:128, 128:256] = pw[k * 64 : (k + 1) * 64, :]

    col80 = lax.broadcasted_iota(jnp.int32, (W, 128), 0)
    colown = col80 < 64
    colmap = colown | ((col80 < 72) & (c < nc - 1)) | ((col80 >= 72) & (c > 0))

    def shifts(value):
        return jnp.concatenate(
            [
                pltpu.roll(value, 1, 0).astype(BF16),
                value.astype(BF16),
                pltpu.roll(value, W - 1, 0).astype(BF16),
            ],
            axis=1,
        )

    def in_map(i, first, last):
        return colmap & ((i >= first) | (r > 0)) & ((i <= last) | (r < nr - 1))

    map_sums = to_rows(0, fsend, fbuf)
    near = [
        one(8, nsend, nbp.at[2], (wrap_r(-1), c)),
        one(9, nsend, nbp.at[0], (wrap_r(1), c)),
    ]

    def edge_window():
        own["cot"].wait()
        for flow in cot_sides:
            flow.wait()
        for flow in cot_ends:
            flow.start()

    def stats_window():
        sums_fwd.wait()
        band_p = pall[...].reshape(8 * nc, 128)
        hot = (
            lax.broadcasted_iota(jnp.int32, (8 * nc, LABELS), 1)
            == band_p[:, 17:18].astype(jnp.int32)
        ).astype(F32)
        fsend[...] = mm_t0(band_p, hot, precision=HIGH)[0:24, :]
        map_sums.start()
        fbuf[pl.ds(r, 1)] = fsend[...][None]
        nsend[1] = pbuf[...]
        for i, t in ((0, wrap_c(-1)), (2, wrap_c(1))):
            nsend[pl.ds(i, 1)] = pall[pl.ds(lax.rem(t, 2), 1), pl.ds(t // 2, 1)][0]
        nbp[1] = nsend[...]
        for flow in near:
            flow.start()

    def band_conv(buf, w, n, window):
        for k in range(nc):
            block = buf[k % 2, k // 2]
            xcat[0:64, k * 64 : (k + 1) * 64] = block[:, 0:64]
            xcat[64:128, k * 64 : (k + 1) * 64] = block[:, 64:128]
        j = lax.broadcasted_iota(jnp.int32, (128, 64), 0) % 64
        z = mm_t1(xcat[...], w[...].reshape(576, 1024))
        zs[8:136, :] = z
        out = []
        for a in range(3):
            t = a * 192
            before = jnp.where(j > 0, zs[7:135, t : t + 64], 0.0)
            after = jnp.where(j < 63, zs[9:137, t + 128 : t + 192], 0.0)
            out.append(before + z[:, t + 64 : t + 128] + after)
        for half in range(2):
            psend[n, 0, :, half * 64 : half * 64 + 64] = out[2][32 * half : 32 * half + 32]
            psend[n, 1, :, half * 64 : half * 64 + 64] = out[0][64 + 32 * half : 96 + 32 * half]
        up = one(10 + 2 * n, psend.at[n, 0], precv.at[n, 1], (wrap_r(-1), c))
        down = one(11 + 2 * n, psend.at[n, 1], precv.at[n, 0], (wrap_r(1), c))
        up.start()
        down.start()
        top = out[1][0:64] + out[2][64:128]
        low = out[0][0:64] + out[1][64:128]
        window()
        up.wait()
        down.wait()
        came = [
            jnp.concatenate([precv[n, i, :, 0:64], precv[n, i, :, 64:128]], axis=0)
            for i in range(2)
        ]
        top = top + jnp.where(r > 0, came[0], 0.0)
        low = low + jnp.where(r < nr - 1, came[1], 0.0)
        return jnp.concatenate([top, low], axis=0)

    zs[...] = jnp.zeros_like(zs)
    first_in.wait()
    first_fwd.start()
    sums_in.wait()
    sums_fwd.start()
    own["gw1"].wait()
    first_fwd.wait()
    first_raw = band_conv(gbuf, gw1, 0, edge_window)
    ssend[...] = jnp.zeros_like(ssend)
    ssend[0:1, 0:64] = jnp.sum(first_raw, 0, keepdims=True)
    ssend[1:2, 0:64] = jnp.sum(first_raw * first_raw, 0, keepdims=True)
    band_stats = to_rows(1, ssend, sbuf)
    band_stats.start()
    sbuf[pl.ds(r, 1)] = ssend[...][None]
    for flow in ein_sides:
        flow.start()
    stats_window()
    band_stats.wait()
    sums = jnp.sum(sbuf[...], axis=0)[:, 0:64]
    band_total = float(nr * 128)
    band_mean = sums[0:1, :] / band_total
    band_var = sums[1:2, :] / band_total - band_mean * band_mean
    normed = (first_raw - band_mean) * lax.rsqrt(band_var + EPS)
    hidden = jnp.maximum(normed, 0.0).astype(BF16)
    hsend[:, 0:64] = hidden[0:64]
    hsend[:, 64:128] = hidden[64:128]
    hidden_in, hidden_fwd = gather(2, hsend, hbuf)
    hidden_in.start()
    own_block(hsend, hbuf)

    for flow in cot_ends:
        flow.wait()
    own["ein"].wait()
    for flow in ein_sides:
        flow.wait()

    def cot_row(i, carry):
        value = jnp.where(in_map(i, 2, 33), cotp[i].astype(F32), 0.0)
        c3[i] = shifts(value)
        return carry

    lax.fori_loop(0, 36, cot_row, 0)

    def cot_turn(q, carry):
        value = cotp[pl.ds(2 + 8 * q, 8), 0:64, :].astype(F32)
        cott[q] = value.reshape(512, 128).T.astype(BF16)
        return carry

    lax.fori_loop(0, 4, cot_turn, 0)

    hidden_in.wait()
    hidden_fwd.start()
    for flow in ein_ends:
        flow.start()
    own["gw2"].wait()
    hidden_fwd.wait()
    second_raw = band_conv(hbuf, gw2, 1, lambda: None)
    global_out = (gin[...].astype(F32) + second_raw).astype(BF16).astype(F32)
    gop[...] = jnp.zeros_like(gop)
    gop[8:72, 0:64] = global_out[0:64]
    gop[8:72, 64:128] = global_out[64:128]
    for t in range(nc):
        gos[t] = gop[4 * t + 7 : 4 * t + 15, :]

    spread_out = to_cols(0, lambda t: gos.at[t], gob)
    spread_out.start()
    gob[pl.ds(c, 1)] = gos[pl.ds(c, 1)]
    for flow in ein_ends:
        flow.wait()
    map_sums.wait()
    for flow in near:
        flow.wait()
    fsum = jnp.sum(fbuf[...], axis=0)
    averages = fsum[0:16, :] / jnp.maximum(fsum[16:17, :], 1.0)
    ringp[...] = jnp.zeros_like(ringp)
    for br in range(4):
        dr, their_br = {0: (0, 1), 1: (1, 0), 2: (1, 1), 3: (2, 0)}[br]
        for q in range(6):
            dc, their_bc = (0, 3) if q == 0 else (2, 0) if q == 5 else (1, q - 1)
            p = their_br * 4 + their_bc
            ringp[br * 8 + q : br * 8 + q + 1, :] = nbp[dr, dc, p : p + 1, :]
    ring_hot = (
        lax.broadcasted_iota(jnp.int32, (32, LABELS), 1) == ringp[:, 17:18].astype(jnp.int32)
    ).astype(F32)
    own["iw"].wait()
    ring_avg = mm_t1(ring_hot, averages, precision=HIGH)
    pooled = jnp.dot(ring_avg, iw[...], precision=HIGH, preferred_element_type=F32)
    spread_out.wait()
    packets = jnp.concatenate([gob[k].astype(BF16) for k in range(nc)], axis=1)
    both = mm(packets, bd[...].reshape(nc * 128, 256)).astype(BF16).astype(F32)
    csend[0] = both[:, 0:128]
    csend[1] = both[:, 128:256]
    edges = [
        one(14, csend.at[0], crecv.at[1], (wrap_r(-1), c)),
        one(15, csend.at[1], crecv.at[0], (wrap_r(1), c)),
    ]
    for flow in edges:
        flow.start()

    def mix_rows(br, coarse, start, stop):
        terms = coarse + pooled[br * 8 : br * 8 + 8]
        pieces = []
        for q in (1, 2, 3, 4, 5, 0):
            line = terms[q : q + 1, :]
            pieces.append(jnp.broadcast_to(line, (8 if q in (0, 5) else UP, 128)))
        add = jnp.concatenate(pieces, axis=0)

        def mix_row(i, carry):
            value = einp[i].astype(F32) + add
            value = jnp.where(in_map(i, 2, 33), value, 0.0).astype(BF16).astype(F32)
            m3[i] = shifts(value)
            return carry

        lax.fori_loop(start, stop, mix_row, 0)

    mix_rows(1, both[:, 0:128], 2, 18)
    mix_rows(2, both[:, 128:256], 18, 34)
    own["w1"].wait()

    def conv_part(src, w, first, count):
        width = src.shape[1]
        x = jnp.concatenate(
            [src[first + a : first + a + count].reshape(count * width, 384) for a in range(3)],
            axis=1,
        )
        return mm(x, w[...].reshape(1152, 128)).reshape(count, width, 128)

    fa[2:17] = conv_part(m3, w1, 2, 15)
    fa[17:32] = conv_part(m3, w1, 17, 15)
    for flow in edges:
        flow.wait()
    mix_rows(0, crecv[0], 0, 2)
    mix_rows(3, crecv[1], 34, 36)
    fa[0:2] = conv_part(m3, w1, 0, 2)
    fa[32:34] = conv_part(m3, w1, 32, 2)

    tile_all = [to_all(n, tsend.at[n], tall.at[n]) for n in range(2)]

    def tile_sums(n, x, y):
        tsend[n, 0:1, :] = jnp.sum(x, axis=(0, 1))[None]
        tsend[n, 1:2, :] = jnp.sum(y, axis=(0, 1))[None]
        tile_all[n].start()
        tall[n, pl.ds(r * nc + c, 1)] = tsend[n][None]

    def tile_sums_2(n):
        tile_all[n].wait()
        return jnp.sum(tall[n], axis=0)

    act = fa[1:33, 0:64, :]
    tile_sums(0, act, act * act)
    ag[0:17] = conv_part(c3, w2t, 0, 17)
    ag[17:34] = conv_part(c3, w2t, 17, 17)
    sums = tile_sums_2(0)
    pixels = float(nr * nc * 2048)
    act_mean = sums[0:1, :] / pixels
    inverse_dev = lax.rsqrt(sums[1:2, :] / pixels - act_mean * act_mean + EPS)

    def act_row(i, carry):
        na = (fa[i] - act_mean) * inverse_dev
        s = jax.nn.sigmoid(na)
        fa[i] = na
        ng = ag[i] * s * (1.0 + na * (1.0 - s))
        ag[i] = ng
        value = jnp.where(in_map(i, 1, 32), na * s, 0.0).astype(BF16).astype(F32)
        a3[i] = shifts(value)[0:64]
        return carry

    lax.fori_loop(0, 34, act_row, 0)
    ng = ag[1:33, 0:64, :]
    tile_sums(1, ng, ng * fa[1:33, 0:64, :])

    def weight_part(n, turned, src, first):
        for a in range(3):
            got = jnp.zeros((128, 384), F32)
            for q in range(4):
                start = first + a + 8 * q
                rhs = src[start : start + 8, 0:64, :].reshape(512, 384)
                got = got + mm(turned[q], rhs)
            for b in range(3):
                gacc[n, a * 384 + b * 128 : a * 384 + (b + 1) * 128, :] = got[
                    :, b * 128 : (b + 1) * 128
                ].T

    half_rows = 1152 // 2
    chunk = half_rows // chips

    def half_of(h):
        return pl.ds(pl.multiple_of(h * half_rows, 16), half_rows)

    def piece(h, q):
        return pl.ds(pl.multiple_of(h * half_rows + q * chunk, 8), chunk)

    pair_sum = [to_partner(3 + n, gacc.at[n, half_of(1 - core)], gpair.at[n]) for n in range(2)]
    band_sum = [
        to_chips(
            3 + n,
            lambda t, n=n: ghalf.at[n, t],
            gcol.at[n, chip],
            gcol.at[n, pl.ds(0, chips - 1)],
        )
        for n in range(2)
    ]
    map_sum = [to_rows(2 + n, gred.at[n], grow.at[n]) for n in range(2)]
    share = [
        to_chips(
            5 + n,
            lambda t, n=n: gfin.at[n],
            gall.at[n, core, chip],
            gall.at[n, core, pl.ds(0, chips - 1)],
        )
        for n in range(2)
    ]
    share_fwd = [to_partner(5 + n, gall.at[n, core], gall.at[n, core]) for n in range(2)]

    def grad_0(n):
        pair_sum[n].start()

    def grad_1(n):
        pair_sum[n].wait()
        total = gacc[n, half_of(core)] + gpair[n]
        ghalf[n] = total.astype(BF16).reshape(chips, chunk, 128)
        band_sum[n].start()
        gcol[n, pl.ds(chip, 1)] = ghalf[n, pl.ds(chip, 1)]

    def grad_2(n):
        band_sum[n].wait()
        gred[n] = jnp.sum(gcol[n].astype(F32), axis=0).astype(BF16)
        map_sum[n].start()
        grow[n, pl.ds(r, 1)] = gred[n][None]

    def grad_3(n):
        map_sum[n].wait()
        total = jnp.sum(grow[n].astype(F32), axis=0)
        gfin[n] = (total * (1.0 / math.sqrt(pixels))).astype(BF16)
        share[n].start()
        gall[n, pl.ds(core, 1), pl.ds(chip, 1)] = gfin[n][None, None]

    def grad_4(n):
        share[n].wait()
        share_fwd[n].start()

    def grad_5(n, out):
        share_fwd[n].wait()
        out[...] = gall[n].reshape(1152, 128).astype(F32)

    weight_part(1, cott, a3, 0)
    grad_0(1)
    for half in range(2):
        got = conv_part(a3, w2, 16 * half, 16)
        enh_out[16 * half : 16 * half + 16] = (
            m3[2 + 16 * half : 18 + 16 * half, 0:64, 128:256].astype(F32) + got
        ).astype(BF16)
    sums = tile_sums_2(1)
    grad_mean = sums[0:1, :] / pixels
    cross_mean = sums[1:2, :] / pixels
    grad_1(1)

    def grad_row(i, carry):
        fg = inverse_dev * (ag[i] - grad_mean - fa[i] * cross_mean)
        fg = jnp.where(in_map(i, 1, 32), fg, 0.0).astype(BF16).astype(F32)
        ag[i] = fg

        return carry

    lax.fori_loop(0, 34, grad_row, 0)

    def grad_turn(q, carry):
        value = ag[pl.ds(1 + 8 * q, 8), 0:64, :]
        fgt[q] = value.reshape(512, 128).T.astype(BF16)
        return carry

    lax.fori_loop(0, 4, grad_turn, 0)
    weight_part(0, fgt, m3, 1)
    grad_0(0)

    grad_1(0)
    grad_2(1)

    rows24 = lax.broadcasted_iota(jnp.int32, (24, W), 0)
    cols24 = lax.broadcasted_iota(jnp.int32, (24, W), 1)
    left = UP * (rows24 % 8) + 1 - rows24 // 8
    inside = (cols24 >= left) & (cols24 < left + UP)
    window = ((inside | ((left < 0) & (cols24 == W - 1))) & (rows24 % 8 < 4)).astype(F32)
    picked = [[], [], []]
    direct = []
    for br in range(2):
        total = jnp.sum(ag[UP * br + 1 : UP * br + 17], axis=0)
        below = total - ag[UP * br + 1] + ag[UP * br + 17]
        above = total - ag[UP * br + 16] + ag[UP * br]
        for a, strip in enumerate((below, total, above)):
            picked[a].append(jnp.dot(window, strip, precision=HIGH, preferred_element_type=F32))
        strip = jnp.sum(c3[UP * br + 2 : UP * br + 18, :, 128:256].astype(F32), axis=0)
        direct.append(jnp.dot(window, strip, precision=HIGH, preferred_element_type=F32)[8:16])
    result = jnp.concatenate(direct, axis=0)
    for a in range(3):
        for b in range(3):
            s_ab = jnp.concatenate([picked[a][br][8 * b : 8 * b + 8] for br in range(2)], axis=0)
            result = result + mm_t1(
                s_ab, w1[a, b * 128 : (b + 1) * 128, :].astype(F32), precision=HIGH
            )
    gg_out[0] = result[0:4] * (1.0 / UP)
    gg_out[1] = result[8:12] * (1.0 / UP)

    grad_2(0)
    grad_3(1)
    grad_3(0)
    grad_4(1)
    grad_4(0)
    grad_5(1, g2_out)
    grad_5(0, g1_out)


def hand_over(*refs):
    half = len(refs) // 2
    for source, target in zip(refs[:half], refs[half:]):
        target[...] = source[...]


def per_device(
    nr,
    nc,
    global_in,
    global_first,
    global_second,
    project_weight,
    enhancer_input,
    instance_map,
    encoder_features,
    instance_weight,
    enhancer_first,
    enhancer_second,
    output_cotangent,
):
    vm = pl.BlockSpec(memory_space=pltpu.VMEM)
    hbm = pl.BlockSpec(memory_space=pltpu.HBM)
    chunk = 1152 // nc
    dma = pltpu.SemaphoreType.DMA
    scratch = [
        pltpu.VMEM((128, 64), BF16),
        pltpu.VMEM((9, 64, 1024), BF16),
        pltpu.VMEM((9, 64, 1024), BF16),
        pltpu.VMEM((1024, 128), BF16),
        pltpu.VMEM((32, 64), jnp.int32),
        pltpu.VMEM((16, 32, 64), F32),
        pltpu.VMEM((16, 128), F32),
        pltpu.VMEM((3, 384, 128), BF16),
        pltpu.VMEM((3, 384, 128), BF16),
        pltpu.VMEM((nc, 128, 256), BF16),
        pltpu.VMEM((64, 128), BF16),
        pltpu.VMEM((2, nc // 2, 64, 128), BF16),
        pltpu.VMEM((2, nc // 2, 64, 128), BF16),
        pltpu.VMEM((64, 128), BF16),
        pltpu.VMEM((128, 1024), BF16),
        pltpu.VMEM((144, 576), F32),
        pltpu.VMEM((2, 2, 32, 128), F32),
        pltpu.VMEM((2, 2, 32, 128), F32),
        pltpu.VMEM((8, 128), F32),
        pltpu.VMEM((nr, 8, 128), F32),
        pltpu.VMEM((80, 128), F32),
        pltpu.VMEM((nc, 8, 128), F32),
        pltpu.VMEM((nc, 8, 128), F32),
        pltpu.VMEM((2, 8, 128), F32),
        pltpu.VMEM((2, 8, 128), F32),
        pltpu.VMEM((36, W, 128), BF16),
        pltpu.VMEM((36, W, 128), BF16),
        pltpu.VMEM((8, 128), F32),
        pltpu.VMEM((2, nc // 2, 8, 128), F32),
        pltpu.VMEM((3, 8, 128), F32),
        pltpu.VMEM((3, 3, 8, 128), F32),
        pltpu.VMEM((32, 128), F32),
        pltpu.VMEM((24, LABELS), F32),
        pltpu.VMEM((nr, 24, LABELS), F32),
        pltpu.VMEM((36, W, 384), BF16),
        pltpu.VMEM((34, 64, 384), BF16),
        pltpu.VMEM((36, W, 384), BF16),
        pltpu.VMEM((4, 128, 512), BF16),
        pltpu.VMEM((4, 128, 512), BF16),
        pltpu.VMEM((3, 384, 128), BF16),
        pltpu.VMEM((34, W, 128), F32),
        pltpu.VMEM((34, W, 128), F32),
        pltpu.VMEM((2, 2, 128), F32),
        pltpu.VMEM((2, nr * nc, 2, 128), F32),
        pltpu.VMEM((2, 1152, 128), F32),
        pltpu.VMEM((2, 576, 128), F32),
        pltpu.VMEM((2, nc // 2, chunk, 128), BF16),
        pltpu.VMEM((2, nc // 2, chunk, 128), BF16),
        pltpu.VMEM((2, chunk, 128), BF16),
        pltpu.VMEM((2, nr, chunk, 128), BF16),
        pltpu.VMEM((2, chunk, 128), BF16),
        pltpu.VMEM((2, 2, nc // 2, chunk, 128), BF16),
        dma((11,)),
        dma((7,)),
        dma((7,)),
        dma((7,)),
        dma((7,)),
        dma((1,)),
        dma((1,)),
        dma((4,)),
        dma((4,)),
        dma((2,)),
        dma((2,)),
        dma((16,)),
        dma((16,)),
    ]
    enhanced, g1, g2, gg = pl.pallas_call(
        functools.partial(kernel, nr, nc),
        out_shape=(
            jax.ShapeDtypeStruct((32, 64, 128), BF16),
            jax.ShapeDtypeStruct((1152, 128), F32),
            jax.ShapeDtypeStruct((1152, 128), F32),
            jax.ShapeDtypeStruct((2, 4, 128), F32),
        ),
        in_specs=[hbm] * 11,
        out_specs=(vm, vm, vm, vm),
        scratch_shapes=scratch,
        compiler_params=pltpu.CompilerParams(
            collective_id=0, has_side_effects=True, vmem_limit_bytes=44 * 1024 * 1024
        ),
    )(
        *(
            pltpu.with_memory_space_constraint(x, pltpu.HBM)
            for x in (
                global_in.reshape(128, 64),
                jnp.swapaxes(global_first, 2, 3).reshape(9, 64, 1024),
                jnp.swapaxes(global_second, 2, 3).reshape(9, 64, 1024),
                project_weight,
                enhancer_input,
                instance_map,
                encoder_features,
                instance_weight,
                enhancer_first.reshape(3, 384, 128),
                enhancer_second.reshape(3, 384, 128),
                output_cotangent,
            )
        )
    )
    vms = [vm] * 4
    enhanced, g1, g2, gg = pl.pallas_call(
        hand_over,
        out_shape=tuple(jax.ShapeDtypeStruct(x.shape, x.dtype) for x in (enhanced, g1, g2, gg)),
        in_specs=vms,
        out_specs=tuple(vms),
        compiler_params=pltpu.CompilerParams(vmem_limit_bytes=16 * 1024 * 1024),
    )(enhanced, g1, g2, gg)
    return (enhanced, g1.reshape(3, 3, 128, 128), g2.reshape(3, 3, 128, 128), gg)


def solution(mesh):
    nr, nc = mesh.shape["rows"], mesh.shape["cols"]
    return jax.shard_map(
        functools.partial(per_device, nr, nc),
        mesh=mesh,
        in_specs=(
            P("rows", None, "cols"),
            P(None, None, None, "cols"),
            P(None, None, None, "cols"),
            P(),
            P("rows", "cols", None),
            P("rows", "cols"),
            P(None, "rows", "cols"),
            P(),
            P(),
            P(),
            P("rows", "cols", None),
        ),
        out_specs=(P("rows", "cols", None), P(), P(), P("rows", "cols", None)),
        check_vma=False,
    )
```

```python
import functools
import math

import jax
import jax.numpy as jnp
from jax import lax
from jax.experimental import pallas as pl
from jax.experimental.pallas import tpu as pltpu
from jax.sharding import PartitionSpec as P

MESH = pl.DeviceIdType.MESH
HIGH = lax.Precision.HIGHEST
F32 = jnp.float32
BF16 = jnp.bfloat16
EPS = 1e-05
LABELS = 256
UP = 16
W = 80


class Flow:
    def __init__(self, start, wait):
        self.start = start
        self.wait = wait


def mm(a, b):
    return jnp.dot(a, b, preferred_element_type=F32)


def mm_t0(a, b, **kw):
    return lax.dot_general(a, b, (((0,), (0,)), ((), ())), preferred_element_type=F32, **kw)


def mm_t1(a, b, **kw):
    return lax.dot_general(a, b, (((1,), (1,)), ((), ())), preferred_element_type=F32, **kw)


def kernel(
    nr,
    nc,
    gin_hbm,
    gw1_hbm,
    gw2_hbm,
    pw_hbm,
    ein,
    imap_hbm,
    feats_hbm,
    iw_hbm,
    w1_hbm,
    w2_hbm,
    cot,
    enh_out,
    g1_out,
    g2_out,
    gg_out,
    gin,
    gw1,
    gw2,
    pw,
    imap,
    feats,
    iw,
    w1,
    w2,
    bd,
    gsend,
    gbuf,
    hbuf,
    hsend,
    xcat,
    zs,
    psend,
    precv,
    ssend,
    sbuf,
    gop,
    gos,
    gob,
    csend,
    crecv,
    einp,
    cotp,
    pbuf,
    pall,
    nsend,
    nbp,
    ringp,
    fsend,
    fbuf,
    m3,
    a3,
    c3,
    cott,
    fgt,
    w2t,
    fa,
    ag,
    tsend,
    tall,
    gacc,
    gpair,
    ghalf,
    gcol,
    gred,
    grow,
    gfin,
    gall,
    local_sem,
    ring_s,
    ring_r,
    fwd_s,
    fwd_r,
    col_s,
    col_r,
    row_s,
    row_r,
    all_s,
    all_r,
    nb_s,
    nb_r,
):
    r = lax.axis_index("rows")
    c = lax.axis_index("cols")
    chips = nc // 2
    chip = c // 2
    core = lax.rem(c, 2)

    def remote(src, dst, ss, rs, dev):
        return pltpu.make_async_remote_copy(
            src_ref=src, dst_ref=dst, send_sem=ss, recv_sem=rs, device_id=dev, device_id_type=MESH
        )

    def one(i, src, dst, dev):
        copy = remote(src, dst, nb_s.at[i], nb_r.at[i], dev)
        return Flow(copy.start, copy.wait)

    def many(count, copy_of, got, ss, rs):
        def start():
            def body(k, carry):
                copy_of(k).start()
                return carry

            lax.fori_loop(1, count, body, 0)

        def wait():
            pltpu.make_async_copy(got, got, ss).wait()
            pltpu.make_async_copy(got, got, rs).wait()

        return Flow(start, wait)

    def to_cols(n, src_of, dst):
        def copy_of(k):
            t = lax.rem(c + k, nc)
            return remote(src_of(t), dst.at[c], col_s.at[n], col_r.at[n], (r, t))

        return many(nc, copy_of, dst.at[pl.ds(0, nc - 1)], col_s.at[n], col_r.at[n])

    def to_rows(n, src, dst):
        def copy_of(k):
            return remote(src, dst.at[r], row_s.at[n], row_r.at[n], (lax.rem(r + k, nr), c))

        return many(nr, copy_of, dst.at[pl.ds(0, nr - 1)], row_s.at[n], row_r.at[n])

    def to_all(n, src, dst):
        me = r * nc + c

        def copy_of(k):
            t = lax.rem(me + k, nr * nc)
            return remote(src, dst.at[me], all_s.at[n], all_r.at[n], (t // nc, lax.rem(t, nc)))

        got = dst.at[pl.ds(0, nr * nc - 1)]
        return many(nr * nc, copy_of, got, all_s.at[n], all_r.at[n])

    def to_chips(n, src_of, dst, got):
        def copy_of(k):
            t = lax.rem(chip + k, chips)
            return remote(src_of(t), dst, ring_s.at[n], ring_r.at[n], (r, 2 * t + core))

        return many(chips, copy_of, got, ring_s.at[n], ring_r.at[n])

    def to_partner(n, src, dst):
        copy = remote(src, dst, fwd_s.at[n], fwd_r.at[n], (r, 2 * chip + 1 - core))
        return Flow(copy.start, copy.wait)

    def gather(n, src, dst):
        return (
            to_chips(n, lambda t: src, dst.at[core, chip], dst.at[core, pl.ds(0, chips - 1)]),
            to_partner(n, dst.at[core], dst.at[core]),
        )

    def own_block(src, dst):
        dst[pl.ds(core, 1), pl.ds(chip, 1)] = src[...][None, None]

    def wrap_r(d):
        return lax.rem(r + d + nr, nr)

    def wrap_c(d):
        return lax.rem(c + d + nc, nc)

    pairs = {
        "gin": (gin_hbm, gin),
        "feats": (feats_hbm, feats),
        "imap": (imap_hbm, imap),
        "gw1": (gw1_hbm, gw1),
        "w2": (w2_hbm, w2),
        "cot": (cot, cotp.at[pl.ds(2, 32), pl.ds(0, 64)]),
        "iw": (iw_hbm, iw),
        "gw2": (gw2_hbm, gw2),
        "pw": (pw_hbm, pw),
        "ein": (ein, einp.at[pl.ds(2, 32), pl.ds(0, 64)]),
        "w1": (w1_hbm, w1),
    }
    own = {
        name: pltpu.make_async_copy(src, dst, local_sem.at[i])
        for i, (name, (src, dst)) in enumerate(pairs.items())
    }
    for copy in own.values():
        copy.start()

    barrier = pltpu.get_barrier_semaphore()

    def greet(dr, dc):
        pl.semaphore_signal(barrier, inc=1, device_id=(wrap_r(dr), lax.rem(c + dc, nc)), device_id_type=MESH)

    def greet_cols(k, carry):
        greet(0, k)
        return carry

    def greet_rows(k, carry):
        greet(k, 0)
        return carry

    lax.fori_loop(1, nc, greet_cols, 0)
    lax.fori_loop(1, nr, greet_rows, 0)

    own["gin"].wait()
    gsend[:, 0:64] = gin[0:64, :]
    gsend[:, 64:128] = gin[64:128, :]

    own["feats"].wait()
    own["imap"].wait()
    lane8 = lax.broadcasted_iota(jnp.int32, (8, 64), 1)
    row8 = lax.broadcasted_iota(jnp.int32, (8, 64), 0)
    packed = jnp.zeros((8, 16), F32)
    label = jnp.zeros((8, 1), F32)
    for br in range(2):
        strip = jnp.sum(feats[:, br * UP : (br + 1) * UP, :], axis=1)
        pick = ((lane8 // UP == row8 % 4) & (row8 // 4 == br)).astype(F32)
        packed = packed + mm_t1(pick, strip, precision=HIGH)
        corner = ((lane8 == UP * (row8 % 4)) & (row8 // 4 == br)).astype(F32)
        line = imap[br * UP : br * UP + 1, :].astype(F32)
        label = label + jnp.sum(corner * line, axis=1, keepdims=True)
    pbuf[...] = jnp.zeros_like(pbuf)
    pbuf[:, 0:16] = packed
    pbuf[:, 16:17] = jnp.full((8, 1), float(UP * UP), F32)
    pbuf[:, 17:18] = label

    pl.semaphore_wait(barrier, nc - 1 + nr - 1)

    first_in, first_fwd = gather(0, gsend, gbuf)
    first_in.start()
    own_block(gsend, gbuf)
    sums_in, sums_fwd = gather(1, pbuf, pall)
    sums_in.start()
    own_block(pbuf, pall)

    def halo(i, src, dst):
        rows32 = pl.ds(2, 32)
        sides = [
            one(4 * i, src.at[:, pl.ds(0, 8)], dst.at[rows32, pl.ds(64, 8)], (r, wrap_c(-1))),
            one(4 * i + 1, src.at[:, pl.ds(56, 8)], dst.at[rows32, pl.ds(72, 8)], (r, wrap_c(1))),
        ]
        ends = [
            one(4 * i + 2, dst.at[pl.ds(2, 2)], dst.at[pl.ds(34, 2)], (wrap_r(-1), c)),
            one(4 * i + 3, dst.at[pl.ds(32, 2)], dst.at[pl.ds(0, 2)], (wrap_r(1), c)),
        ]
        return sides, ends

    cot_sides, cot_ends = halo(0, cot, cotp)
    ein_sides, ein_ends = halo(1, ein, einp)
    for flow in cot_sides:
        flow.start()

    own["w2"].wait()
    for a in range(3):
        for b in range(3):
            w2t[a, b * 128 : (b + 1) * 128, :] = (
                w2[2 - a, (2 - b) * 128 : (3 - b) * 128, :].astype(F32).T.astype(BF16)
            )
    own["pw"].wait()
    bd[...] = jnp.zeros_like(bd)
    for k in range(nc):
        bd[k, 0:64, 0:128] = pw[k * 64 : (k + 1) * 64, :]
        bd[k, 64:128, 128:256] = pw[k * 64 : (k + 1) * 64, :]

    col80 = lax.broadcasted_iota(jnp.int32, (W, 128), 0)
    colown = col80 < 64
    colmap = colown | ((col80 < 72) & (c < nc - 1)) | ((col80 >= 72) & (c > 0))

    def shifts(value):
        return jnp.concatenate(
            [
                pltpu.roll(value, 1, 0).astype(BF16),
                value.astype(BF16),
                pltpu.roll(value, W - 1, 0).astype(BF16),
            ],
            axis=1,
        )

    def in_map(i, first, last):
        return colmap & ((i >= first) | (r > 0)) & ((i <= last) | (r < nr - 1))

    map_sums = to_rows(0, fsend, fbuf)
    near = [
        one(8, nsend, nbp.at[2], (wrap_r(-1), c)),
        one(9, nsend, nbp.at[0], (wrap_r(1), c)),
    ]

    def edge_window():
        own["cot"].wait()
        for flow in cot_sides:
            flow.wait()
        for flow in cot_ends:
            flow.start()

    def stats_window():
        sums_fwd.wait()
        band_p = pall[...].reshape(8 * nc, 128)
        hot = (
            lax.broadcasted_iota(jnp.int32, (8 * nc, LABELS), 1)
            == band_p[:, 17:18].astype(jnp.int32)
        ).astype(F32)
        fsend[...] = mm_t0(band_p, hot, precision=HIGH)[0:24, :]
        map_sums.start()
        fbuf[pl.ds(r, 1)] = fsend[...][None]
        nsend[1] = pbuf[...]
        for i, t in ((0, wrap_c(-1)), (2, wrap_c(1))):
            nsend[pl.ds(i, 1)] = pall[pl.ds(lax.rem(t, 2), 1), pl.ds(t // 2, 1)][0]
        nbp[1] = nsend[...]
        for flow in near:
            flow.start()

    def band_conv(buf, w, n, window):
        for k in range(nc):
            block = buf[k % 2, k // 2]
            xcat[0:64, k * 64 : (k + 1) * 64] = block[:, 0:64]
            xcat[64:128, k * 64 : (k + 1) * 64] = block[:, 64:128]
        j = lax.broadcasted_iota(jnp.int32, (128, 64), 0) % 64
        z = mm_t1(xcat[...], w[...].reshape(576, 1024))
        zs[8:136, :] = z
        out = []
        for a in range(3):
            t = a * 192
            before = jnp.where(j > 0, zs[7:135, t : t + 64], 0.0)
            after = jnp.where(j < 63, zs[9:137, t + 128 : t + 192], 0.0)
            out.append(before + z[:, t + 64 : t + 128] + after)
        for half in range(2):
            psend[n, 0, :, half * 64 : half * 64 + 64] = out[2][32 * half : 32 * half + 32]
            psend[n, 1, :, half * 64 : half * 64 + 64] = out[0][64 + 32 * half : 96 + 32 * half]
        up = one(10 + 2 * n, psend.at[n, 0], precv.at[n, 1], (wrap_r(-1), c))
        down = one(11 + 2 * n, psend.at[n, 1], precv.at[n, 0], (wrap_r(1), c))
        up.start()
        down.start()
        top = out[1][0:64] + out[2][64:128]
        low = out[0][0:64] + out[1][64:128]
        window()
        up.wait()
        down.wait()
        came = [
            jnp.concatenate([precv[n, i, :, 0:64], precv[n, i, :, 64:128]], axis=0)
            for i in range(2)
        ]
        top = top + jnp.where(r > 0, came[0], 0.0)
        low = low + jnp.where(r < nr - 1, came[1], 0.0)
        return jnp.concatenate([top, low], axis=0)

    zs[...] = jnp.zeros_like(zs)
    first_in.wait()
    first_fwd.start()
    sums_in.wait()
    sums_fwd.start()
    own["gw1"].wait()
    first_fwd.wait()
    first_raw = band_conv(gbuf, gw1, 0, edge_window)
    ssend[...] = jnp.zeros_like(ssend)
    ssend[0:1, 0:64] = jnp.sum(first_raw, 0, keepdims=True)
    ssend[1:2, 0:64] = jnp.sum(first_raw * first_raw, 0, keepdims=True)
    band_stats = to_rows(1, ssend, sbuf)
    band_stats.start()
    sbuf[pl.ds(r, 1)] = ssend[...][None]
    for flow in ein_sides:
        flow.start()
    stats_window()
    band_stats.wait()
    sums = jnp.sum(sbuf[...], axis=0)[:, 0:64]
    band_total = float(nr * 128)
    band_mean = sums[0:1, :] / band_total
    band_var = sums[1:2, :] / band_total - band_mean * band_mean
    normed = (first_raw - band_mean) * lax.rsqrt(band_var + EPS)
    hidden = jnp.maximum(normed, 0.0).astype(BF16)
    hsend[:, 0:64] = hidden[0:64]
    hsend[:, 64:128] = hidden[64:128]
    hidden_in, hidden_fwd = gather(2, hsend, hbuf)
    hidden_in.start()
    own_block(hsend, hbuf)

    for flow in cot_ends:
        flow.wait()
    own["ein"].wait()
    for flow in ein_sides:
        flow.wait()

    def cot_row(i, carry):
        value = jnp.where(in_map(i, 2, 33), cotp[i].astype(F32), 0.0)
        c3[i] = shifts(value)
        return carry

    lax.fori_loop(0, 36, cot_row, 0)

    def cot_turn(q, carry):
        value = cotp[pl.ds(2 + 8 * q, 8), 0:64, :].astype(F32)
        cott[q] = value.reshape(512, 128).T.astype(BF16)
        return carry

    lax.fori_loop(0, 4, cot_turn, 0)

    hidden_in.wait()
    hidden_fwd.start()
    for flow in ein_ends:
        flow.start()
    own["gw2"].wait()
    hidden_fwd.wait()
    second_raw = band_conv(hbuf, gw2, 1, lambda: None)
    global_out = (gin[...].astype(F32) + second_raw).astype(BF16).astype(F32)
    gop[...] = jnp.zeros_like(gop)
    gop[8:72, 0:64] = global_out[0:64]
    gop[8:72, 64:128] = global_out[64:128]
    for t in range(nc):
        gos[t] = gop[4 * t + 7 : 4 * t + 15, :]

    spread_out = to_cols(0, lambda t: gos.at[t], gob)
    spread_out.start()
    gob[pl.ds(c, 1)] = gos[pl.ds(c, 1)]
    for flow in ein_ends:
        flow.wait()
    map_sums.wait()
    for flow in near:
        flow.wait()
    fsum = jnp.sum(fbuf[...], axis=0)
    averages = fsum[0:16, :] / jnp.maximum(fsum[16:17, :], 1.0)
    ringp[...] = jnp.zeros_like(ringp)
    for br in range(4):
        dr, their_br = {0: (0, 1), 1: (1, 0), 2: (1, 1), 3: (2, 0)}[br]
        for q in range(6):
            dc, their_bc = (0, 3) if q == 0 else (2, 0) if q == 5 else (1, q - 1)
            p = their_br * 4 + their_bc
            ringp[br * 8 + q : br * 8 + q + 1, :] = nbp[dr, dc, p : p + 1, :]
    ring_hot = (
        lax.broadcasted_iota(jnp.int32, (32, LABELS), 1) == ringp[:, 17:18].astype(jnp.int32)
    ).astype(F32)
    own["iw"].wait()
    ring_avg = mm_t1(ring_hot, averages, precision=HIGH)
    pooled = jnp.dot(ring_avg, iw[...], precision=HIGH, preferred_element_type=F32)
    spread_out.wait()
    packets = jnp.concatenate([gob[k].astype(BF16) for k in range(nc)], axis=1)
    both = mm(packets, bd[...].reshape(nc * 128, 256)).astype(BF16).astype(F32)
    csend[0] = both[:, 0:128]
    csend[1] = both[:, 128:256]
    edges = [
        one(14, csend.at[0], crecv.at[1], (wrap_r(-1), c)),
        one(15, csend.at[1], crecv.at[0], (wrap_r(1), c)),
    ]
    for flow in edges:
        flow.start()

    def mix_rows(br, coarse, start, stop):
        terms = coarse + pooled[br * 8 : br * 8 + 8]
        pieces = []
        for q in (1, 2, 3, 4, 5, 0):
            line = terms[q : q + 1, :]
            pieces.append(jnp.broadcast_to(line, (8 if q in (0, 5) else UP, 128)))
        add = jnp.concatenate(pieces, axis=0)

        def mix_row(i, carry):
            value = einp[i].astype(F32) + add
            value = jnp.where(in_map(i, 2, 33), value, 0.0).astype(BF16).astype(F32)
            m3[i] = shifts(value)
            return carry

        lax.fori_loop(start, stop, mix_row, 0)

    mix_rows(1, both[:, 0:128], 2, 18)
    mix_rows(2, both[:, 128:256], 18, 34)
    own["w1"].wait()

    def conv_part(src, w, first, count):
        width = src.shape[1]
        x = jnp.concatenate(
            [src[first + a : first + a + count].reshape(count * width, 384) for a in range(3)],
            axis=1,
        )
        return mm(x, w[...].reshape(1152, 128)).reshape(count, width, 128)

    fa[2:17] = conv_part(m3, w1, 2, 15)
    fa[17:32] = conv_part(m3, w1, 17, 15)
    for flow in edges:
        flow.wait()
    mix_rows(0, crecv[0], 0, 2)
    mix_rows(3, crecv[1], 34, 36)
    fa[0:2] = conv_part(m3, w1, 0, 2)
    fa[32:34] = conv_part(m3, w1, 32, 2)

    tile_all = [to_all(n, tsend.at[n], tall.at[n]) for n in range(2)]

    def tile_sums(n, x, y):
        tsend[n, 0:1, :] = jnp.sum(x, axis=(0, 1))[None]
        tsend[n, 1:2, :] = jnp.sum(y, axis=(0, 1))[None]
        tile_all[n].start()
        tall[n, pl.ds(r * nc + c, 1)] = tsend[n][None]

    def tile_sums_2(n):
        tile_all[n].wait()
        return jnp.sum(tall[n], axis=0)

    act = fa[1:33, 0:64, :]
    tile_sums(0, act, act * act)
    ag[0:17] = conv_part(c3, w2t, 0, 17)
    ag[17:34] = conv_part(c3, w2t, 17, 17)
    sums = tile_sums_2(0)
    pixels = float(nr * nc * 2048)
    act_mean = sums[0:1, :] / pixels
    inverse_dev = lax.rsqrt(sums[1:2, :] / pixels - act_mean * act_mean + EPS)

    def act_row(i, carry):
        na = (fa[i] - act_mean) * inverse_dev
        s = jax.nn.sigmoid(na)
        fa[i] = na
        ng = ag[i] * s * (1.0 + na * (1.0 - s))
        ag[i] = ng
        value = jnp.where(in_map(i, 1, 32), na * s, 0.0).astype(BF16).astype(F32)
        a3[i] = shifts(value)[0:64]
        return carry

    lax.fori_loop(0, 34, act_row, 0)
    ng = ag[1:33, 0:64, :]
    tile_sums(1, ng, ng * fa[1:33, 0:64, :])

    def weight_part(n, turned, src, first):
        for a in range(3):
            got = jnp.zeros((128, 384), F32)
            for q in range(4):
                start = first + a + 8 * q
                rhs = src[start : start + 8, 0:64, :].reshape(512, 384)
                got = got + mm(turned[q], rhs)
            for b in range(3):
                gacc[n, a * 384 + b * 128 : a * 384 + (b + 1) * 128, :] = got[
                    :, b * 128 : (b + 1) * 128
                ].T

    half_rows = 1152 // 2
    chunk = half_rows // chips

    def half_of(h):
        return pl.ds(pl.multiple_of(h * half_rows, 16), half_rows)

    def piece(h, q):
        return pl.ds(pl.multiple_of(h * half_rows + q * chunk, 8), chunk)

    pair_sum = [to_partner(3 + n, gacc.at[n, half_of(1 - core)], gpair.at[n]) for n in range(2)]
    band_sum = [
        to_chips(
            3 + n,
            lambda t, n=n: ghalf.at[n, t],
            gcol.at[n, chip],
            gcol.at[n, pl.ds(0, chips - 1)],
        )
        for n in range(2)
    ]
    map_sum = [to_rows(2 + n, gred.at[n], grow.at[n]) for n in range(2)]
    share = [
        to_chips(
            5 + n,
            lambda t, n=n: gfin.at[n],
            gall.at[n, core, chip],
            gall.at[n, core, pl.ds(0, chips - 1)],
        )
        for n in range(2)
    ]
    share_fwd = [to_partner(5 + n, gall.at[n, core], gall.at[n, core]) for n in range(2)]

    def grad_0(n):
        pair_sum[n].start()

    def grad_1(n):
        pair_sum[n].wait()
        total = gacc[n, half_of(core)] + gpair[n]
        ghalf[n] = total.astype(BF16).reshape(chips, chunk, 128)
        band_sum[n].start()
        gcol[n, pl.ds(chip, 1)] = ghalf[n, pl.ds(chip, 1)]

    def grad_2(n):
        band_sum[n].wait()
        gred[n] = jnp.sum(gcol[n].astype(F32), axis=0).astype(BF16)
        map_sum[n].start()
        grow[n, pl.ds(r, 1)] = gred[n][None]

    def grad_3(n):
        map_sum[n].wait()
        total = jnp.sum(grow[n].astype(F32), axis=0)
        gfin[n] = (total * (1.0 / math.sqrt(pixels))).astype(BF16)
        share[n].start()
        gall[n, pl.ds(core, 1), pl.ds(chip, 1)] = gfin[n][None, None]

    def grad_4(n):
        share[n].wait()
        share_fwd[n].start()

    def grad_5(n, out):
        share_fwd[n].wait()
        out[...] = gall[n].reshape(1152, 128).astype(F32)

    weight_part(1, cott, a3, 0)
    grad_0(1)
    for half in range(2):
        got = conv_part(a3, w2, 16 * half, 16)
        enh_out[16 * half : 16 * half + 16] = (
            m3[2 + 16 * half : 18 + 16 * half, 0:64, 128:256].astype(F32) + got
        ).astype(BF16)
    sums = tile_sums_2(1)
    grad_mean = sums[0:1, :] / pixels
    cross_mean = sums[1:2, :] / pixels

    def grad_row(i, carry):
        fg = inverse_dev * (ag[i] - grad_mean - fa[i] * cross_mean)
        fg = jnp.where(in_map(i, 1, 32), fg, 0.0).astype(BF16).astype(F32)
        ag[i] = fg

        return carry

    lax.fori_loop(0, 34, grad_row, 0)

    def grad_turn(q, carry):
        value = ag[pl.ds(1 + 8 * q, 8), 0:64, :]
        fgt[q] = value.reshape(512, 128).T.astype(BF16)
        return carry

    lax.fori_loop(0, 4, grad_turn, 0)
    weight_part(0, fgt, m3, 1)
    grad_0(0)
    grad_1(1)

    grad_1(0)
    grad_2(1)

    rows24 = lax.broadcasted_iota(jnp.int32, (24, W), 0)
    cols24 = lax.broadcasted_iota(jnp.int32, (24, W), 1)
    left = UP * (rows24 % 8) + 1 - rows24 // 8
    inside = (cols24 >= left) & (cols24 < left + UP)
    window = ((inside | ((left < 0) & (cols24 == W - 1))) & (rows24 % 8 < 4)).astype(F32)
    picked = [[], [], []]
    direct = []
    for br in range(2):
        total = jnp.sum(ag[UP * br + 1 : UP * br + 17], axis=0)
        below = total - ag[UP * br + 1] + ag[UP * br + 17]
        above = total - ag[UP * br + 16] + ag[UP * br]
        for a, strip in enumerate((below, total, above)):
            picked[a].append(jnp.dot(window, strip, precision=HIGH, preferred_element_type=F32))
        strip = jnp.sum(c3[UP * br + 2 : UP * br + 18, :, 128:256].astype(F32), axis=0)
        direct.append(jnp.dot(window, strip, precision=HIGH, preferred_element_type=F32)[8:16])
    result = jnp.concatenate(direct, axis=0)
    for a in range(3):
        for b in range(3):
            s_ab = jnp.concatenate([picked[a][br][8 * b : 8 * b + 8] for br in range(2)], axis=0)
            result = result + mm_t1(
                s_ab, w1[a, b * 128 : (b + 1) * 128, :].astype(F32), precision=HIGH
            )
    gg_out[0] = result[0:4] * (1.0 / UP)
    gg_out[1] = result[8:12] * (1.0 / UP)

    grad_2(0)
    grad_3(1)
    grad_3(0)
    grad_4(1)
    grad_4(0)
    grad_5(1, g2_out)
    grad_5(0, g1_out)


def hand_over(*refs):
    half = len(refs) // 2
    for source, target in zip(refs[:half], refs[half:]):
        target[...] = source[...]


def per_device(
    nr,
    nc,
    global_in,
    global_first,
    global_second,
    project_weight,
    enhancer_input,
    instance_map,
    encoder_features,
    instance_weight,
    enhancer_first,
    enhancer_second,
    output_cotangent,
):
    vm = pl.BlockSpec(memory_space=pltpu.VMEM)
    hbm = pl.BlockSpec(memory_space=pltpu.HBM)
    chunk = 1152 // nc
    dma = pltpu.SemaphoreType.DMA
    scratch = [
        pltpu.VMEM((128, 64), BF16),
        pltpu.VMEM((9, 64, 1024), BF16),
        pltpu.VMEM((9, 64, 1024), BF16),
        pltpu.VMEM((1024, 128), BF16),
        pltpu.VMEM((32, 64), jnp.int32),
        pltpu.VMEM((16, 32, 64), F32),
        pltpu.VMEM((16, 128), F32),
        pltpu.VMEM((3, 384, 128), BF16),
        pltpu.VMEM((3, 384, 128), BF16),
        pltpu.VMEM((nc, 128, 256), BF16),
        pltpu.VMEM((64, 128), BF16),
        pltpu.VMEM((2, nc // 2, 64, 128), BF16),
        pltpu.VMEM((2, nc // 2, 64, 128), BF16),
        pltpu.VMEM((64, 128), BF16),
        pltpu.VMEM((128, 1024), BF16),
        pltpu.VMEM((144, 576), F32),
        pltpu.VMEM((2, 2, 32, 128), F32),
        pltpu.VMEM((2, 2, 32, 128), F32),
        pltpu.VMEM((8, 128), F32),
        pltpu.VMEM((nr, 8, 128), F32),
        pltpu.VMEM((80, 128), F32),
        pltpu.VMEM((nc, 8, 128), F32),
        pltpu.VMEM((nc, 8, 128), F32),
        pltpu.VMEM((2, 8, 128), F32),
        pltpu.VMEM((2, 8, 128), F32),
        pltpu.VMEM((36, W, 128), BF16),
        pltpu.VMEM((36, W, 128), BF16),
        pltpu.VMEM((8, 128), F32),
        pltpu.VMEM((2, nc // 2, 8, 128), F32),
        pltpu.VMEM((3, 8, 128), F32),
        pltpu.VMEM((3, 3, 8, 128), F32),
        pltpu.VMEM((32, 128), F32),
        pltpu.VMEM((24, LABELS), F32),
        pltpu.VMEM((nr, 24, LABELS), F32),
        pltpu.VMEM((36, W, 384), BF16),
        pltpu.VMEM((34, 64, 384), BF16),
        pltpu.VMEM((36, W, 384), BF16),
        pltpu.VMEM((4, 128, 512), BF16),
        pltpu.VMEM((4, 128, 512), BF16),
        pltpu.VMEM((3, 384, 128), BF16),
        pltpu.VMEM((34, W, 128), F32),
        pltpu.VMEM((34, W, 128), F32),
        pltpu.VMEM((2, 2, 128), F32),
        pltpu.VMEM((2, nr * nc, 2, 128), F32),
        pltpu.VMEM((2, 1152, 128), F32),
        pltpu.VMEM((2, 576, 128), F32),
        pltpu.VMEM((2, nc // 2, chunk, 128), BF16),
        pltpu.VMEM((2, nc // 2, chunk, 128), BF16),
        pltpu.VMEM((2, chunk, 128), BF16),
        pltpu.VMEM((2, nr, chunk, 128), BF16),
        pltpu.VMEM((2, chunk, 128), BF16),
        pltpu.VMEM((2, 2, nc // 2, chunk, 128), BF16),
        dma((11,)),
        dma((7,)),
        dma((7,)),
        dma((7,)),
        dma((7,)),
        dma((1,)),
        dma((1,)),
        dma((4,)),
        dma((4,)),
        dma((2,)),
        dma((2,)),
        dma((16,)),
        dma((16,)),
    ]
    enhanced, g1, g2, gg = pl.pallas_call(
        functools.partial(kernel, nr, nc),
        out_shape=(
            jax.ShapeDtypeStruct((32, 64, 128), BF16),
            jax.ShapeDtypeStruct((1152, 128), F32),
            jax.ShapeDtypeStruct((1152, 128), F32),
            jax.ShapeDtypeStruct((2, 4, 128), F32),
        ),
        in_specs=[hbm] * 11,
        out_specs=(vm, vm, vm, vm),
        scratch_shapes=scratch,
        compiler_params=pltpu.CompilerParams(
            collective_id=0, has_side_effects=True, vmem_limit_bytes=44 * 1024 * 1024
        ),
    )(
        *(
            pltpu.with_memory_space_constraint(x, pltpu.HBM)
            for x in (
                global_in.reshape(128, 64),
                jnp.swapaxes(global_first, 2, 3).reshape(9, 64, 1024),
                jnp.swapaxes(global_second, 2, 3).reshape(9, 64, 1024),
                project_weight,
                enhancer_input,
                instance_map,
                encoder_features,
                instance_weight,
                enhancer_first.reshape(3, 384, 128),
                enhancer_second.reshape(3, 384, 128),
                output_cotangent,
            )
        )
    )
    vms = [vm] * 4
    enhanced, g1, g2, gg = pl.pallas_call(
        hand_over,
        out_shape=tuple(jax.ShapeDtypeStruct(x.shape, x.dtype) for x in (enhanced, g1, g2, gg)),
        in_specs=vms,
        out_specs=tuple(vms),
        compiler_params=pltpu.CompilerParams(vmem_limit_bytes=16 * 1024 * 1024),
    )(enhanced, g1, g2, gg)
    return (enhanced, g1.reshape(3, 3, 128, 128), g2.reshape(3, 3, 128, 128), gg)


def solution(mesh):
    nr, nc = mesh.shape["rows"], mesh.shape["cols"]
    return jax.shard_map(
        functools.partial(per_device, nr, nc),
        mesh=mesh,
        in_specs=(
            P("rows", None, "cols"),
            P(None, None, None, "cols"),
            P(None, None, None, "cols"),
            P(),
            P("rows", "cols", None),
            P("rows", "cols"),
            P(None, "rows", "cols"),
            P(),
            P(),
            P(),
            P("rows", "cols", None),
        ),
        out_specs=(P("rows", "cols", None), P(), P(), P("rows", "cols", None)),
        check_vma=False,
    )
```

```python
import functools
import math

import jax
import jax.numpy as jnp
from jax import lax
from jax.experimental import pallas as pl
from jax.experimental.pallas import tpu as pltpu
from jax.sharding import PartitionSpec as P

MESH = pl.DeviceIdType.MESH
HIGH = lax.Precision.HIGHEST
F32 = jnp.float32
BF16 = jnp.bfloat16
EPS = 1e-05
LABELS = 256
UP = 16
W = 80


class Flow:
    def __init__(self, start, wait):
        self.start = start
        self.wait = wait


def mm(a, b):
    return jnp.dot(a, b, preferred_element_type=F32)


def mm_t0(a, b, **kw):
    return lax.dot_general(a, b, (((0,), (0,)), ((), ())), preferred_element_type=F32, **kw)


def mm_t1(a, b, **kw):
    return lax.dot_general(a, b, (((1,), (1,)), ((), ())), preferred_element_type=F32, **kw)


def kernel(
    nr,
    nc,
    gin_hbm,
    gw1_hbm,
    gw2_hbm,
    pw_hbm,
    ein,
    imap_hbm,
    feats_hbm,
    iw_hbm,
    w1_hbm,
    w2_hbm,
    cot,
    enh_out,
    g1_out,
    g2_out,
    gg_out,
    gin,
    gw1,
    gw2,
    pw,
    imap,
    feats,
    iw,
    w1,
    w2,
    bd,
    gsend,
    gbuf,
    hbuf,
    hsend,
    xcat,
    zs,
    psend,
    precv,
    ssend,
    sbuf,
    gop,
    gos,
    gob,
    csend,
    crecv,
    einp,
    cotp,
    pbuf,
    pall,
    nsend,
    nbp,
    ringp,
    fsend,
    fbuf,
    m3,
    a3,
    c3,
    cott,
    fgt,
    w2t,
    fa,
    ag,
    tsend,
    tall,
    gacc,
    gpair,
    ghalf,
    gcol,
    gred,
    grow,
    gfin,
    gall,
    local_sem,
    ring_s,
    ring_r,
    fwd_s,
    fwd_r,
    col_s,
    col_r,
    row_s,
    row_r,
    all_s,
    all_r,
    nb_s,
    nb_r,
):
    r = lax.axis_index("rows")
    c = lax.axis_index("cols")
    chips = nc // 2
    chip = c // 2
    core = lax.rem(c, 2)

    def remote(src, dst, ss, rs, dev):
        return pltpu.make_async_remote_copy(
            src_ref=src, dst_ref=dst, send_sem=ss, recv_sem=rs, device_id=dev, device_id_type=MESH
        )

    def one(i, src, dst, dev):
        copy = remote(src, dst, nb_s.at[i], nb_r.at[i], dev)
        return Flow(copy.start, copy.wait)

    def many(count, copy_of, got, ss, rs):
        def start():
            def body(k, carry):
                copy_of(k).start()
                return carry

            lax.fori_loop(1, count, body, 0)

        def wait():
            pltpu.make_async_copy(got, got, ss).wait()
            pltpu.make_async_copy(got, got, rs).wait()

        return Flow(start, wait)

    def to_cols(n, src_of, dst):
        def copy_of(k):
            t = lax.rem(c + k, nc)
            return remote(src_of(t), dst.at[c], col_s.at[n], col_r.at[n], (r, t))

        return many(nc, copy_of, dst.at[pl.ds(0, nc - 1)], col_s.at[n], col_r.at[n])

    def to_rows(n, src, dst):
        def copy_of(k):
            return remote(src, dst.at[r], row_s.at[n], row_r.at[n], (lax.rem(r + k, nr), c))

        return many(nr, copy_of, dst.at[pl.ds(0, nr - 1)], row_s.at[n], row_r.at[n])

    def to_all(n, src, dst):
        me = r * nc + c

        def copy_of(k):
            t = lax.rem(me + k, nr * nc)
            return remote(src, dst.at[me], all_s.at[n], all_r.at[n], (t // nc, lax.rem(t, nc)))

        got = dst.at[pl.ds(0, nr * nc - 1)]
        return many(nr * nc, copy_of, got, all_s.at[n], all_r.at[n])

    def to_chips(n, src_of, dst, got):
        def copy_of(k):
            t = lax.rem(chip + k, chips)
            return remote(src_of(t), dst, ring_s.at[n], ring_r.at[n], (r, 2 * t + core))

        return many(chips, copy_of, got, ring_s.at[n], ring_r.at[n])

    def to_partner(n, src, dst):
        copy = remote(src, dst, fwd_s.at[n], fwd_r.at[n], (r, 2 * chip + 1 - core))
        return Flow(copy.start, copy.wait)

    def gather(n, src, dst):
        return (
            to_chips(n, lambda t: src, dst.at[core, chip], dst.at[core, pl.ds(0, chips - 1)]),
            to_partner(n, dst.at[core], dst.at[core]),
        )

    def own_block(src, dst):
        dst[pl.ds(core, 1), pl.ds(chip, 1)] = src[...][None, None]

    def wrap_r(d):
        return lax.rem(r + d + nr, nr)

    def wrap_c(d):
        return lax.rem(c + d + nc, nc)

    pairs = {
        "gin": (gin_hbm, gin),
        "feats": (feats_hbm, feats),
        "imap": (imap_hbm, imap),
        "gw1": (gw1_hbm, gw1),
        "w2": (w2_hbm, w2),
        "cot": (cot, cotp.at[pl.ds(2, 32), pl.ds(0, 64)]),
        "iw": (iw_hbm, iw),
        "gw2": (gw2_hbm, gw2),
        "pw": (pw_hbm, pw),
        "ein": (ein, einp.at[pl.ds(2, 32), pl.ds(0, 64)]),
        "w1": (w1_hbm, w1),
    }
    own = {
        name: pltpu.make_async_copy(src, dst, local_sem.at[i])
        for i, (name, (src, dst)) in enumerate(pairs.items())
    }
    for copy in own.values():
        copy.start()

    barrier = pltpu.get_barrier_semaphore()

    def greet(dr, dc):
        pl.semaphore_signal(barrier, inc=1, device_id=(wrap_r(dr), lax.rem(c + dc, nc)), device_id_type=MESH)

    def greet_cols(k, carry):
        greet(0, k)
        return carry

    def greet_rows(k, carry):
        greet(k, 0)
        return carry

    lax.fori_loop(1, nc, greet_cols, 0)
    lax.fori_loop(1, nr, greet_rows, 0)

    own["gin"].wait()
    gsend[:, 0:64] = gin[0:64, :]
    gsend[:, 64:128] = gin[64:128, :]

    own["feats"].wait()
    own["imap"].wait()
    lane8 = lax.broadcasted_iota(jnp.int32, (8, 64), 1)
    row8 = lax.broadcasted_iota(jnp.int32, (8, 64), 0)
    packed = jnp.zeros((8, 16), F32)
    label = jnp.zeros((8, 1), F32)
    for br in range(2):
        strip = jnp.sum(feats[:, br * UP : (br + 1) * UP, :], axis=1)
        pick = ((lane8 // UP == row8 % 4) & (row8 // 4 == br)).astype(F32)
        packed = packed + mm_t1(pick, strip, precision=HIGH)
        corner = ((lane8 == UP * (row8 % 4)) & (row8 // 4 == br)).astype(F32)
        line = imap[br * UP : br * UP + 1, :].astype(F32)
        label = label + jnp.sum(corner * line, axis=1, keepdims=True)
    pbuf[...] = jnp.zeros_like(pbuf)
    pbuf[:, 0:16] = packed
    pbuf[:, 16:17] = jnp.full((8, 1), float(UP * UP), F32)
    pbuf[:, 17:18] = label

    pl.semaphore_wait(barrier, nc - 1 + nr - 1)

    first_in, first_fwd = gather(0, gsend, gbuf)
    first_in.start()
    own_block(gsend, gbuf)
    sums_in, sums_fwd = gather(1, pbuf, pall)
    sums_in.start()
    own_block(pbuf, pall)

    def halo(i, src, dst):
        rows32 = pl.ds(2, 32)
        sides = [
            one(4 * i, src.at[:, pl.ds(0, 8)], dst.at[rows32, pl.ds(64, 8)], (r, wrap_c(-1))),
            one(4 * i + 1, src.at[:, pl.ds(56, 8)], dst.at[rows32, pl.ds(72, 8)], (r, wrap_c(1))),
        ]
        ends = [
            one(4 * i + 2, dst.at[pl.ds(2, 2)], dst.at[pl.ds(34, 2)], (wrap_r(-1), c)),
            one(4 * i + 3, dst.at[pl.ds(32, 2)], dst.at[pl.ds(0, 2)], (wrap_r(1), c)),
        ]
        return sides, ends

    cot_sides, cot_ends = halo(0, cot, cotp)
    ein_sides, ein_ends = halo(1, ein, einp)
    for flow in cot_sides:
        flow.start()

    own["w2"].wait()
    for a in range(3):
        for b in range(3):
            w2t[a, b * 128 : (b + 1) * 128, :] = (
                w2[2 - a, (2 - b) * 128 : (3 - b) * 128, :].astype(F32).T.astype(BF16)
            )
    own["pw"].wait()
    bd[...] = jnp.zeros_like(bd)
    for k in range(nc):
        bd[k, 0:64, 0:128] = pw[k * 64 : (k + 1) * 64, :]
        bd[k, 64:128, 128:256] = pw[k * 64 : (k + 1) * 64, :]

    col80 = lax.broadcasted_iota(jnp.int32, (W, 128), 0)
    colown = col80 < 64
    colmap = colown | ((col80 < 72) & (c < nc - 1)) | ((col80 >= 72) & (c > 0))

    def shifts(value):
        return jnp.concatenate(
            [
                pltpu.roll(value, 1, 0).astype(BF16),
                value.astype(BF16),
                pltpu.roll(value, W - 1, 0).astype(BF16),
            ],
            axis=1,
        )

    def in_map(i, first, last):
        return colmap & ((i >= first) | (r > 0)) & ((i <= last) | (r < nr - 1))

    map_sums = to_rows(0, fsend, fbuf)
    near = [
        one(8, nsend, nbp.at[2], (wrap_r(-1), c)),
        one(9, nsend, nbp.at[0], (wrap_r(1), c)),
    ]

    def edge_window():
        own["cot"].wait()
        for flow in cot_sides:
            flow.wait()
        for flow in cot_ends:
            flow.start()

    def stats_window():
        sums_fwd.wait()
        band_p = pall[...].reshape(8 * nc, 128)
        hot = (
            lax.broadcasted_iota(jnp.int32, (8 * nc, LABELS), 1)
            == band_p[:, 17:18].astype(jnp.int32)
        ).astype(F32)
        fsend[...] = mm_t0(band_p, hot, precision=HIGH)[0:24, :]
        map_sums.start()
        fbuf[pl.ds(r, 1)] = fsend[...][None]
        nsend[1] = pbuf[...]
        for i, t in ((0, wrap_c(-1)), (2, wrap_c(1))):
            nsend[pl.ds(i, 1)] = pall[pl.ds(lax.rem(t, 2), 1), pl.ds(t // 2, 1)][0]
        nbp[1] = nsend[...]
        for flow in near:
            flow.start()

    def band_conv(buf, w, n, window):
        for k in range(nc):
            block = buf[k % 2, k // 2]
            xcat[0:64, k * 64 : (k + 1) * 64] = block[:, 0:64]
            xcat[64:128, k * 64 : (k + 1) * 64] = block[:, 64:128]
        j = lax.broadcasted_iota(jnp.int32, (128, 64), 0) % 64
        z = mm_t1(xcat[...], w[...].reshape(576, 1024))
        zs[8:136, :] = z
        out = []
        for a in range(3):
            t = a * 192
            before = jnp.where(j > 0, zs[7:135, t : t + 64], 0.0)
            after = jnp.where(j < 63, zs[9:137, t + 128 : t + 192], 0.0)
            out.append(before + z[:, t + 64 : t + 128] + after)
        for half in range(2):
            psend[n, 0, :, half * 64 : half * 64 + 64] = out[2][32 * half : 32 * half + 32]
            psend[n, 1, :, half * 64 : half * 64 + 64] = out[0][64 + 32 * half : 96 + 32 * half]
        up = one(10 + 2 * n, psend.at[n, 0], precv.at[n, 1], (wrap_r(-1), c))
        down = one(11 + 2 * n, psend.at[n, 1], precv.at[n, 0], (wrap_r(1), c))
        up.start()
        down.start()
        top = out[1][0:64] + out[2][64:128]
        low = out[0][0:64] + out[1][64:128]
        window()
        up.wait()
        down.wait()
        came = [
            jnp.concatenate([precv[n, i, :, 0:64], precv[n, i, :, 64:128]], axis=0)
            for i in range(2)
        ]
        top = top + jnp.where(r > 0, came[0], 0.0)
        low = low + jnp.where(r < nr - 1, came[1], 0.0)
        return jnp.concatenate([top, low], axis=0)

    zs[...] = jnp.zeros_like(zs)
    first_in.wait()
    first_fwd.start()
    sums_in.wait()
    sums_fwd.start()
    own["gw1"].wait()
    first_fwd.wait()
    first_raw = band_conv(gbuf, gw1, 0, edge_window)
    ssend[...] = jnp.zeros_like(ssend)
    ssend[0:1, 0:64] = jnp.sum(first_raw, 0, keepdims=True)
    ssend[1:2, 0:64] = jnp.sum(first_raw * first_raw, 0, keepdims=True)
    band_stats = to_rows(1, ssend, sbuf)
    band_stats.start()
    sbuf[pl.ds(r, 1)] = ssend[...][None]
    for flow in ein_sides:
        flow.start()
    stats_window()
    band_stats.wait()
    sums = jnp.sum(sbuf[...], axis=0)[:, 0:64]
    band_total = float(nr * 128)
    band_mean = sums[0:1, :] / band_total
    band_var = sums[1:2, :] / band_total - band_mean * band_mean
    normed = (first_raw - band_mean) * lax.rsqrt(band_var + EPS)
    hidden = jnp.maximum(normed, 0.0).astype(BF16)
    hsend[:, 0:64] = hidden[0:64]
    hsend[:, 64:128] = hidden[64:128]
    hidden_in, hidden_fwd = gather(2, hsend, hbuf)
    hidden_in.start()
    own_block(hsend, hbuf)

    for flow in cot_ends:
        flow.wait()
    own["ein"].wait()
    for flow in ein_sides:
        flow.wait()

    def cot_row(i, carry):
        value = jnp.where(in_map(i, 2, 33), cotp[i].astype(F32), 0.0)
        c3[i] = shifts(value)
        return carry

    lax.fori_loop(0, 36, cot_row, 0)

    def cot_turn(q, carry):
        value = cotp[pl.ds(2 + 8 * q, 8), 0:64, :].astype(F32)
        cott[q] = value.reshape(512, 128).T.astype(BF16)
        return carry

    lax.fori_loop(0, 4, cot_turn, 0)

    hidden_in.wait()
    hidden_fwd.start()
    for flow in ein_ends:
        flow.start()
    own["gw2"].wait()
    hidden_fwd.wait()
    second_raw = band_conv(hbuf, gw2, 1, lambda: None)
    global_out = (gin[...].astype(F32) + second_raw).astype(BF16).astype(F32)
    gop[...] = jnp.zeros_like(gop)
    gop[8:72, 0:64] = global_out[0:64]
    gop[8:72, 64:128] = global_out[64:128]
    for t in range(nc):
        gos[t] = gop[4 * t + 7 : 4 * t + 15, :]

    spread_out = to_cols(0, lambda t: gos.at[t], gob)
    spread_out.start()
    gob[pl.ds(c, 1)] = gos[pl.ds(c, 1)]
    for flow in ein_ends:
        flow.wait()
    map_sums.wait()
    for flow in near:
        flow.wait()
    fsum = jnp.sum(fbuf[...], axis=0)
    averages = fsum[0:16, :] / jnp.maximum(fsum[16:17, :], 1.0)
    ringp[...] = jnp.zeros_like(ringp)
    for br in range(4):
        dr, their_br = {0: (0, 1), 1: (1, 0), 2: (1, 1), 3: (2, 0)}[br]
        for q in range(6):
            dc, their_bc = (0, 3) if q == 0 else (2, 0) if q == 5 else (1, q - 1)
            p = their_br * 4 + their_bc
            ringp[br * 8 + q : br * 8 + q + 1, :] = nbp[dr, dc, p : p + 1, :]
    ring_hot = (
        lax.broadcasted_iota(jnp.int32, (32, LABELS), 1) == ringp[:, 17:18].astype(jnp.int32)
    ).astype(F32)
    own["iw"].wait()
    ring_avg = mm_t1(ring_hot, averages, precision=HIGH)
    pooled = jnp.dot(ring_avg, iw[...], precision=HIGH, preferred_element_type=F32)
    spread_out.wait()
    packets = jnp.concatenate([gob[k].astype(BF16) for k in range(nc)], axis=1)
    both = mm(packets, bd[...].reshape(nc * 128, 256)).astype(BF16).astype(F32)
    csend[0] = both[:, 0:128]
    csend[1] = both[:, 128:256]
    edges = [
        one(14, csend.at[0], crecv.at[1], (wrap_r(-1), c)),
        one(15, csend.at[1], crecv.at[0], (wrap_r(1), c)),
    ]
    for flow in edges:
        flow.start()

    def mix_rows(br, coarse, start, stop):
        terms = coarse + pooled[br * 8 : br * 8 + 8]
        pieces = []
        for q in (1, 2, 3, 4, 5, 0):
            line = terms[q : q + 1, :]
            pieces.append(jnp.broadcast_to(line, (8 if q in (0, 5) else UP, 128)))
        add = jnp.concatenate(pieces, axis=0)

        def mix_row(i, carry):
            value = einp[i].astype(F32) + add
            value = jnp.where(in_map(i, 2, 33), value, 0.0).astype(BF16).astype(F32)
            m3[i] = shifts(value)
            return carry

        lax.fori_loop(start, stop, mix_row, 0)

    mix_rows(1, both[:, 0:128], 2, 18)
    mix_rows(2, both[:, 128:256], 18, 34)
    own["w1"].wait()

    def conv_part(src, w, first, count):
        width = src.shape[1]
        x = jnp.concatenate(
            [src[first + a : first + a + count].reshape(count * width, 384) for a in range(3)],
            axis=1,
        )
        return mm(x, w[...].reshape(1152, 128)).reshape(count, width, 128)

    fa[2:17] = conv_part(m3, w1, 2, 15)
    fa[17:32] = conv_part(m3, w1, 17, 15)
    for flow in edges:
        flow.wait()
    mix_rows(0, crecv[0], 0, 2)
    mix_rows(3, crecv[1], 34, 36)
    fa[0:2] = conv_part(m3, w1, 0, 2)
    fa[32:34] = conv_part(m3, w1, 32, 2)

    tile_all = [to_all(n, tsend.at[n], tall.at[n]) for n in range(2)]

    def tile_sums(n, x, y):
        tsend[n, 0:1, :] = jnp.sum(x, axis=(0, 1))[None]
        tsend[n, 1:2, :] = jnp.sum(y, axis=(0, 1))[None]
        tile_all[n].start()
        tall[n, pl.ds(r * nc + c, 1)] = tsend[n][None]

    def tile_sums_2(n):
        tile_all[n].wait()
        return jnp.sum(tall[n], axis=0)

    act = fa[1:33, 0:64, :]
    tile_sums(0, act, act * act)
    ag[0:17] = conv_part(c3, w2t, 0, 17)
    ag[17:34] = conv_part(c3, w2t, 17, 17)
    sums = tile_sums_2(0)
    pixels = float(nr * nc * 2048)
    act_mean = sums[0:1, :] / pixels
    inverse_dev = lax.rsqrt(sums[1:2, :] / pixels - act_mean * act_mean + EPS)

    def act_row(i, carry):
        na = (fa[i] - act_mean) * inverse_dev
        s = jax.nn.sigmoid(na)
        fa[i] = na
        ng = ag[i] * s * (1.0 + na * (1.0 - s))
        ag[i] = ng
        value = jnp.where(in_map(i, 1, 32), na * s, 0.0).astype(BF16).astype(F32)
        a3[i] = shifts(value)[0:64]
        return carry

    lax.fori_loop(0, 34, act_row, 0)
    ng = ag[1:33, 0:64, :]
    tile_sums(1, ng, ng * fa[1:33, 0:64, :])

    def weight_part(n, turned, src, first):
        for a in range(3):
            got = jnp.zeros((128, 384), F32)
            for q in range(4):
                start = first + a + 8 * q
                rhs = src[start : start + 8, 0:64, :].reshape(512, 384)
                got = got + mm(turned[q], rhs)
            for b in range(3):
                gacc[n, a * 384 + b * 128 : a * 384 + (b + 1) * 128, :] = got[
                    :, b * 128 : (b + 1) * 128
                ].T

    half_rows = 1152 // 2
    chunk = half_rows // chips

    def half_of(h):
        return pl.ds(pl.multiple_of(h * half_rows, 16), half_rows)

    def piece(h, q):
        return pl.ds(pl.multiple_of(h * half_rows + q * chunk, 8), chunk)

    pair_sum = [to_partner(3 + n, gacc.at[n, half_of(1 - core)], gpair.at[n]) for n in range(2)]
    band_sum = [
        to_chips(
            3 + n,
            lambda t, n=n: ghalf.at[n, t],
            gcol.at[n, chip],
            gcol.at[n, pl.ds(0, chips - 1)],
        )
        for n in range(2)
    ]
    map_sum = [to_rows(2 + n, gred.at[n], grow.at[n]) for n in range(2)]
    share = [
        to_chips(
            5 + n,
            lambda t, n=n: gfin.at[n],
            gall.at[n, core, chip],
            gall.at[n, core, pl.ds(0, chips - 1)],
        )
        for n in range(2)
    ]
    share_fwd = [to_partner(5 + n, gall.at[n, core], gall.at[n, core]) for n in range(2)]

    def grad_0(n):
        pair_sum[n].start()

    def grad_1(n):
        pair_sum[n].wait()
        total = gacc[n, half_of(core)] + gpair[n]
        ghalf[n] = total.astype(BF16).reshape(chips, chunk, 128)
        band_sum[n].start()
        gcol[n, pl.ds(chip, 1)] = ghalf[n, pl.ds(chip, 1)]

    def grad_2(n):
        band_sum[n].wait()
        gred[n] = jnp.sum(gcol[n].astype(F32), axis=0).astype(BF16)
        map_sum[n].start()
        grow[n, pl.ds(r, 1)] = gred[n][None]

    def grad_3(n):
        map_sum[n].wait()
        total = jnp.sum(grow[n].astype(F32), axis=0)
        gfin[n] = (total * (1.0 / math.sqrt(pixels))).astype(BF16)
        share[n].start()
        gall[n, pl.ds(core, 1), pl.ds(chip, 1)] = gfin[n][None, None]

    def grad_4(n):
        share[n].wait()
        share_fwd[n].start()

    def grad_5(n, out):
        share_fwd[n].wait()
        out[...] = gall[n].reshape(1152, 128).astype(F32)

    weight_part(1, cott, a3, 0)
    grad_0(1)
    for half in range(2):
        got = conv_part(a3, w2, 16 * half, 16)
        enh_out[16 * half : 16 * half + 16] = (
            m3[2 + 16 * half : 18 + 16 * half, 0:64, 128:256].astype(F32) + got
        ).astype(BF16)
    sums = tile_sums_2(1)
    grad_mean = sums[0:1, :] / pixels
    cross_mean = sums[1:2, :] / pixels
    grad_1(1)

    def grad_row(i, carry):
        fg = inverse_dev * (ag[i] - grad_mean - fa[i] * cross_mean)
        fg = jnp.where(in_map(i, 1, 32), fg, 0.0).astype(BF16).astype(F32)
        ag[i] = fg

        return carry

    lax.fori_loop(0, 34, grad_row, 0)

    def grad_turn(q, carry):
        value = ag[pl.ds(1 + 8 * q, 8), 0:64, :]
        fgt[q] = value.reshape(512, 128).T.astype(BF16)
        return carry

    lax.fori_loop(0, 4, grad_turn, 0)
    weight_part(0, fgt, m3, 1)
    grad_0(0)

    grad_1(0)
    grad_2(1)

    rows24 = lax.broadcasted_iota(jnp.int32, (24, W), 0)
    cols24 = lax.broadcasted_iota(jnp.int32, (24, W), 1)
    left = UP * (rows24 % 8) + 1 - rows24 // 8
    inside = (cols24 >= left) & (cols24 < left + UP)
    window = ((inside | ((left < 0) & (cols24 == W - 1))) & (rows24 % 8 < 4)).astype(F32)
    picked = [[], [], []]
    direct = []
    for br in range(2):
        total = jnp.sum(ag[UP * br + 1 : UP * br + 17], axis=0)
        below = total - ag[UP * br + 1] + ag[UP * br + 17]
        above = total - ag[UP * br + 16] + ag[UP * br]
        for a, strip in enumerate((below, total, above)):
            picked[a].append(jnp.dot(window, strip, precision=HIGH, preferred_element_type=F32))
        strip = jnp.sum(c3[UP * br + 2 : UP * br + 18, :, 128:256].astype(F32), axis=0)
        direct.append(jnp.dot(window, strip, precision=HIGH, preferred_element_type=F32)[8:16])
    grad_2(0)
    grad_3(1)

    result = jnp.concatenate(direct, axis=0)
    for a in range(3):
        for b in range(3):
            s_ab = jnp.concatenate([picked[a][br][8 * b : 8 * b + 8] for br in range(2)], axis=0)
            result = result + mm_t1(
                s_ab, w1[a, b * 128 : (b + 1) * 128, :].astype(F32), precision=HIGH
            )
    gg_out[0] = result[0:4] * (1.0 / UP)
    gg_out[1] = result[8:12] * (1.0 / UP)

    grad_3(0)
    grad_4(1)
    grad_4(0)
    grad_5(1, g2_out)
    grad_5(0, g1_out)


def hand_over(*refs):
    half = len(refs) // 2
    for source, target in zip(refs[:half], refs[half:]):
        target[...] = source[...]


def per_device(
    nr,
    nc,
    global_in,
    global_first,
    global_second,
    project_weight,
    enhancer_input,
    instance_map,
    encoder_features,
    instance_weight,
    enhancer_first,
    enhancer_second,
    output_cotangent,
):
    vm = pl.BlockSpec(memory_space=pltpu.VMEM)
    hbm = pl.BlockSpec(memory_space=pltpu.HBM)
    chunk = 1152 // nc
    dma = pltpu.SemaphoreType.DMA
    scratch = [
        pltpu.VMEM((128, 64), BF16),
        pltpu.VMEM((9, 64, 1024), BF16),
        pltpu.VMEM((9, 64, 1024), BF16),
        pltpu.VMEM((1024, 128), BF16),
        pltpu.VMEM((32, 64), jnp.int32),
        pltpu.VMEM((16, 32, 64), F32),
        pltpu.VMEM((16, 128), F32),
        pltpu.VMEM((3, 384, 128), BF16),
        pltpu.VMEM((3, 384, 128), BF16),
        pltpu.VMEM((nc, 128, 256), BF16),
        pltpu.VMEM((64, 128), BF16),
        pltpu.VMEM((2, nc // 2, 64, 128), BF16),
        pltpu.VMEM((2, nc // 2, 64, 128), BF16),
        pltpu.VMEM((64, 128), BF16),
        pltpu.VMEM((128, 1024), BF16),
        pltpu.VMEM((144, 576), F32),
        pltpu.VMEM((2, 2, 32, 128), F32),
        pltpu.VMEM((2, 2, 32, 128), F32),
        pltpu.VMEM((8, 128), F32),
        pltpu.VMEM((nr, 8, 128), F32),
        pltpu.VMEM((80, 128), F32),
        pltpu.VMEM((nc, 8, 128), F32),
        pltpu.VMEM((nc, 8, 128), F32),
        pltpu.VMEM((2, 8, 128), F32),
        pltpu.VMEM((2, 8, 128), F32),
        pltpu.VMEM((36, W, 128), BF16),
        pltpu.VMEM((36, W, 128), BF16),
        pltpu.VMEM((8, 128), F32),
        pltpu.VMEM((2, nc // 2, 8, 128), F32),
        pltpu.VMEM((3, 8, 128), F32),
        pltpu.VMEM((3, 3, 8, 128), F32),
        pltpu.VMEM((32, 128), F32),
        pltpu.VMEM((24, LABELS), F32),
        pltpu.VMEM((nr, 24, LABELS), F32),
        pltpu.VMEM((36, W, 384), BF16),
        pltpu.VMEM((34, 64, 384), BF16),
        pltpu.VMEM((36, W, 384), BF16),
        pltpu.VMEM((4, 128, 512), BF16),
        pltpu.VMEM((4, 128, 512), BF16),
        pltpu.VMEM((3, 384, 128), BF16),
        pltpu.VMEM((34, W, 128), F32),
        pltpu.VMEM((34, W, 128), F32),
        pltpu.VMEM((2, 2, 128), F32),
        pltpu.VMEM((2, nr * nc, 2, 128), F32),
        pltpu.VMEM((2, 1152, 128), F32),
        pltpu.VMEM((2, 576, 128), F32),
        pltpu.VMEM((2, nc // 2, chunk, 128), BF16),
        pltpu.VMEM((2, nc // 2, chunk, 128), BF16),
        pltpu.VMEM((2, chunk, 128), BF16),
        pltpu.VMEM((2, nr, chunk, 128), BF16),
        pltpu.VMEM((2, chunk, 128), BF16),
        pltpu.VMEM((2, 2, nc // 2, chunk, 128), BF16),
        dma((11,)),
        dma((7,)),
        dma((7,)),
        dma((7,)),
        dma((7,)),
        dma((1,)),
        dma((1,)),
        dma((4,)),
        dma((4,)),
        dma((2,)),
        dma((2,)),
        dma((16,)),
        dma((16,)),
    ]
    enhanced, g1, g2, gg = pl.pallas_call(
        functools.partial(kernel, nr, nc),
        out_shape=(
            jax.ShapeDtypeStruct((32, 64, 128), BF16),
            jax.ShapeDtypeStruct((1152, 128), F32),
            jax.ShapeDtypeStruct((1152, 128), F32),
            jax.ShapeDtypeStruct((2, 4, 128), F32),
        ),
        in_specs=[hbm] * 11,
        out_specs=(vm, vm, vm, vm),
        scratch_shapes=scratch,
        compiler_params=pltpu.CompilerParams(
            collective_id=0, has_side_effects=True, vmem_limit_bytes=44 * 1024 * 1024
        ),
    )(
        *(
            pltpu.with_memory_space_constraint(x, pltpu.HBM)
            for x in (
                global_in.reshape(128, 64),
                jnp.swapaxes(global_first, 2, 3).reshape(9, 64, 1024),
                jnp.swapaxes(global_second, 2, 3).reshape(9, 64, 1024),
                project_weight,
                enhancer_input,
                instance_map,
                encoder_features,
                instance_weight,
                enhancer_first.reshape(3, 384, 128),
                enhancer_second.reshape(3, 384, 128),
                output_cotangent,
            )
        )
    )
    vms = [vm] * 4
    enhanced, g1, g2, gg = pl.pallas_call(
        hand_over,
        out_shape=tuple(jax.ShapeDtypeStruct(x.shape, x.dtype) for x in (enhanced, g1, g2, gg)),
        in_specs=vms,
        out_specs=tuple(vms),
        compiler_params=pltpu.CompilerParams(vmem_limit_bytes=16 * 1024 * 1024),
    )(enhanced, g1, g2, gg)
    return (enhanced, g1.reshape(3, 3, 128, 128), g2.reshape(3, 3, 128, 128), gg)


def solution(mesh):
    nr, nc = mesh.shape["rows"], mesh.shape["cols"]
    return jax.shard_map(
        functools.partial(per_device, nr, nc),
        mesh=mesh,
        in_specs=(
            P("rows", None, "cols"),
            P(None, None, None, "cols"),
            P(None, None, None, "cols"),
            P(),
            P("rows", "cols", None),
            P("rows", "cols"),
            P(None, "rows", "cols"),
            P(),
            P(),
            P(),
            P("rows", "cols", None),
        ),
        out_specs=(P("rows", "cols", None), P(), P(), P("rows", "cols", None)),
        check_vma=False,
    )
```
